256 devices in a mesh: gx: 32 (over y, z), gy: 8 (over x, core).
Axes of the slice: x: 4, y: 4, z: 8, core: 2. Of those that a mesh axis runs over, the one named last changes fastest.
Arguments:
- offsets: float32 [3, 64, 16, 1024], P(None, 'gx', 'gy'), as said below
- charges: float32 [64, 16, 1024], P('gx', 'gy'), may hold values from -0.08 to 0.08
Outputs:
- potential: float32 [64, 16, 1024], P('gx', 'gy')
The draws below stay inside these ranges and needn't reach their ends.
Inputs may be any that keep to these rules, and one draw needn't show every extreme that they name: `offsets`: particle p of a leaf lies in sub-cell (p // 4^2, (p // 4) % 4, p % 4) of the leaf's grid of 4^3 equal sub-cells, inside the middle half of that sub-cell along each dimension.
All inputs are finite; a program needn't handle non-finite values. Where the reference program divides by a largest or mean magnitude, that divisor is 1e-20 or more.
Results may differ from the reference program's by a relative error of at most 0.0003.
Values sent between devices are 32-bit elements; how exact they have to be, the bound alone decides.
A program may use at most 192 MiB of HBM per device.

```python
import jax
import jax.numpy as jnp
from jax import lax

LZ = 16
SUB = 4
PPL = 64
NX = 64
NY = 16


def draw_offsets(key, part):
    jitter = jax.random.uniform(key, (3, NX, NY, LZ, PPL), jnp.float32)
    counter = jnp.arange(PPL, dtype=jnp.int32)
    cells = jnp.stack([counter // (SUB * SUB), counter // SUB % SUB, counter % SUB]).astype(jnp.float32)
    placed = (cells[:, None, None, None, :] + 0.25 + 0.5 * jitter) / SUB
    return placed.reshape(3, NX, NY, LZ * PPL)


def block_levels(key, dims, pieces, least, largest):
    def one(position, blocks):
        draws = jax.random.uniform(jax.random.fold_in(jax.random.fold_in(key, 6), position), (blocks,), jnp.float32, least / len(pieces), largest / len(pieces))
        return jnp.repeat(jnp.exp(draws), dims[position] // blocks).reshape((-1,) + (1,) * (len(dims) - position - 1))

    gain = one(*pieces[0])
    for cut in pieces[1:]:
        gain = gain * one(*cut)
    return gain


def noise(rng, extent, width, bound, pieces=(), kind=jnp.bfloat16):
    entries = jax.random.normal(rng, extent, jnp.float32) * width
    if len(pieces) > 0:
        entries = block_levels(rng, extent, pieces, -0.22, 0.18) * entries
    return jnp.clip(entries, min=-bound, max=bound).astype(kind)


def setup_inputs(seed: int = 0) -> dict:
    seeds = jax.random.split(jax.random.key(seed), 3)
    return {
        "offsets": draw_offsets(jax.random.fold_in(seeds[2], 71), 0),
        "charges": noise(seeds[1], (NX, NY, LZ * PPL), 0.01, 0.08, ((0, 32), (1, 8)), jnp.float32),
    }


highest = lax.Precision.HIGHEST

def cheb_points():
    return jnp.cos((2.0 * jnp.arange(4, dtype=jnp.float32) + 1.0) * jnp.pi / 8.0)

def interpolate(coords):
    points = cheb_points()
    first = points
    second = 2.0 * points * points - 1.0
    third = 4.0 * points * points * points - 3.0 * points
    value = coords[..., None]
    return 0.25 + 0.5 * (value * first + (2.0 * value * value - 1.0) * second + (4.0 * value * value * value - 3.0 * value) * third)

def node_grid():
    points = cheb_points()
    counter = jnp.arange(64, dtype=jnp.int32)
    return jnp.stack([points[counter // 16], points[counter // 4 % 4], points[counter % 4]], -1)

def child_grid():
    counter = jnp.arange(8, dtype=jnp.int32)
    return jnp.stack([counter // 4, counter // 2 % 2, counter % 2], -1).astype(jnp.float32)

def upward_matrix():
    points = cheb_points()
    halves = jnp.array([0.0, 1.0], dtype=jnp.float32)
    shifted = (points[None, :] + 2.0 * halves[:, None] - 1.0) / 2.0
    factor = interpolate(shifted)
    return jnp.einsum('xia,yjb,zkc->xyzijkabc', factor, factor, factor, precision=highest).reshape(512, 64)

def translation(offset):
    node_points = node_grid()
    child_corner = child_grid()
    box_offsets = 2.0 * offset[None, None, :] + child_corner[:, None, :] - child_corner[None, :, :]
    spread = (node_points[None, :, :] - node_points[:, None, :]) / 2.0
    separation = spread[None, :, None, :, :] - box_offsets[:, None, :, None, :]
    adjacent = (lax.optimization_barrier(jnp.max(jnp.abs(box_offsets), -1)) <= 1.0).astype(jnp.float32)[:, None, :, None]
    distance = jnp.sqrt(lax.optimization_barrier(jnp.sum(separation * separation, -1)))
    return ((1.0 - adjacent) / (distance + adjacent)).reshape(512, 512)

def offset_of(counter):
    return (jnp.stack([counter // 9, counter // 3 % 3, counter % 3]) - 1).astype(jnp.int32)

def translation_tables():

    def one_table(counter):
        return translation(offset_of(counter).astype(jnp.float32))
    return lax.map(one_table, jnp.arange(27, dtype=jnp.int32))

def to_parent(moments):
    size_x, size_y, size_z, _ = moments.shape
    moments = moments.reshape(size_x // 2, 2, size_y // 2, 2, size_z // 2, 2, 64)
    return moments.transpose(0, 2, 4, 1, 3, 5, 6).reshape(size_x // 2, size_y // 2, size_z // 2, 512)

def from_parent(moments):
    size_x, size_y, size_z, _ = moments.shape
    moments = moments.reshape(size_x, size_y, size_z, 2, 2, 2, 64)
    return moments.transpose(0, 3, 1, 4, 2, 5, 6).reshape(2 * size_x, 2 * size_y, 2 * size_z, 64)

def matmul(left, right):
    return jnp.dot(left, right, precision=highest, preferred_element_type=jnp.float32)

def coarsen(moments, upward):
    parents = to_parent(moments)
    return matmul(parents.reshape(-1, 512), upward).reshape(parents.shape[:3] + (64,))

def refine(local, upward):
    spread_out = matmul(local.reshape(-1, 64), upward.T).reshape(local.shape[:3] + (512,))
    return from_parent(spread_out)

def pad_one(moments):
    return jnp.pad(moments, ((1, 1), (1, 1), (1, 1), (0, 0)))

def far_translate(padded, scaling, tables):
    size_x, size_y, size_z = (padded.shape[0] - 2, padded.shape[1] - 2, padded.shape[2] - 2)

    def step_fn(running, inputs):
        counter, table = inputs
        offset = offset_of(counter)
        window_piece = lax.dynamic_slice(padded, (offset[0] + 1, offset[1] + 1, offset[2] + 1, jnp.int32(0)), (size_x, size_y, size_z, 512))
        return (running + matmul(window_piece.reshape(-1, 512), table), None)
    running, _ = lax.scan(step_fn, jnp.zeros((size_x * size_y * size_z, 512), jnp.float32), (jnp.arange(27, dtype=jnp.int32), tables))
    return (scaling * running).reshape(size_x, size_y, size_z, 512)

def dense_translate(targets, sources, weights):
    node_points = node_grid()
    spread = (node_points[:, None, :] - node_points[None, :, :]) / 2.0
    box_offsets = sources[None, :, :] - targets[:, None, :]
    separation = spread[None, :, None, :, :] - box_offsets[:, None, :, None, :]
    adjacent = (lax.optimization_barrier(jnp.max(jnp.abs(box_offsets), -1)) <= 1.0).astype(jnp.float32)[:, None, :, None]
    distance = jnp.sqrt(lax.optimization_barrier(jnp.sum(separation * separation, -1)))
    kernel = ((1.0 - adjacent) / (distance + adjacent)).reshape(targets.shape[0] * 64, sources.shape[0] * 64)
    return (0.125 * matmul(kernel, weights.reshape(-1))).reshape(targets.shape[0], 64)

def particle_basis(offsets):
    coords = 2.0 * offsets - 1.0
    along_x = interpolate(coords[0])
    along_y = interpolate(coords[1])
    along_z = interpolate(coords[2])
    product = along_x[..., :, None, None] * along_y[..., None, :, None] * along_z[..., None, None, :]
    return product.reshape(along_x.shape[:-1] + (64,))

def gather_moments(charges, interp_basis):
    return jnp.einsum('...p,...pm->...m', charges, interp_basis, precision=highest, preferred_element_type=jnp.float32)

def evaluate_local(interp_basis, local):
    return jnp.einsum('...pm,...m->...p', interp_basis, local, precision=highest, preferred_element_type=jnp.float32)

def near_field(targets, sources, weights):
    size_x, size_y, depth, count = (targets.shape[1], targets.shape[2], targets.shape[3], targets.shape[4])
    self_mask = jnp.concatenate([jnp.zeros((count, count), jnp.float32), jnp.eye(count, dtype=jnp.float32), jnp.zeros((count, count), jnp.float32)], 1)
    running = jnp.zeros((size_x, size_y, depth, count), jnp.float32)
    for step_x in range(3):
        for step_y in range(3):
            window = sources[:, step_x:step_x + size_x, step_y:step_y + size_y]
            stacked = jnp.concatenate([window[..., 0:depth, :], window[..., 1:depth + 1, :], window[..., 2:depth + 2, :]], -1)
            charge_win = weights[step_x:step_x + size_x, step_y:step_y + size_y]
            charge_win = jnp.concatenate([charge_win[..., 0:depth, :], charge_win[..., 1:depth + 1, :], charge_win[..., 2:depth + 2, :]], -1)
            squared = jnp.zeros((size_x, size_y, depth, count, 3 * count), jnp.float32)
            for comp in range(3):
                differ = targets[comp][..., :, None] - stacked[comp][..., None, :]
                squared = squared + differ * differ
            if step_x == 1 and step_y == 1:
                inverse = lax.rsqrt(squared + self_mask) * (1.0 - self_mask)
            else:
                inverse = lax.rsqrt(squared)
            running = running + lax.optimization_barrier(jnp.sum(inverse * charge_win[..., None, :], -1))
    return running

def reference(offsets, charges):
    upward = upward_matrix()
    tables = translation_tables()
    offsets_five = offsets.reshape(3, NX, NY, LZ, PPL)
    charge_four = charges.reshape(NX, NY, LZ, PPL)
    by_column = offsets_five.transpose(1, 0, 2, 3, 4)

    def column_moments(inputs):
        column_offsets, column_charges = inputs
        return gather_moments(column_charges, particle_basis(column_offsets))
    leaf_moments = lax.map(column_moments, (by_column, charge_four))
    first_moments = coarsen(leaf_moments, upward)
    second_moments = coarsen(first_moments, upward)
    third_moments = coarsen(second_moments, upward)
    leaf_far = from_parent(far_translate(pad_one(to_parent(leaf_moments)), 1.0, tables))
    first_far = from_parent(far_translate(pad_one(to_parent(first_moments)), 0.5, tables))
    second_far = from_parent(far_translate(pad_one(to_parent(second_moments)), 0.25, tables))
    boxes_x, boxes_y, boxes_z = (NX // 8, NY // 8, LZ // 8)
    counter = jnp.arange(boxes_x * boxes_y * boxes_z, dtype=jnp.int32)
    sources = jnp.stack([counter // (boxes_y * boxes_z), counter // boxes_z % boxes_y, counter % boxes_z], -1).astype(jnp.float32)
    flat_third = third_moments.reshape(-1, 64)

    def top_row(column):
        inner = jnp.arange(boxes_y * boxes_z, dtype=jnp.int32)
        targets = jnp.stack([jnp.full((boxes_y * boxes_z,), column, jnp.int32), inner // boxes_z, inner % boxes_z], -1).astype(jnp.float32)
        return dense_translate(targets, sources, flat_third)
    top_far = lax.map(top_row, jnp.arange(boxes_x, dtype=jnp.int32)).reshape(boxes_x, boxes_y, boxes_z, 64)
    second_local = refine(top_far, upward) + second_far
    first_local = refine(second_local, upward) + first_far
    leaf_local = refine(first_local, upward) + leaf_far

    def column_far(inputs):
        column_offsets, column_local = inputs
        return evaluate_local(particle_basis(column_offsets), column_local)
    far_potential = lax.map(column_far, (by_column, leaf_local))
    padded = jnp.pad(offsets_five, ((0, 0), (1, 1), (1, 1), (1, 1), (0, 0)))
    grid_x = jnp.arange(-1, NX + 1, dtype=jnp.int32).astype(jnp.float32)
    grid_y = jnp.arange(-1, NY + 1, dtype=jnp.int32).astype(jnp.float32)
    grid_z = jnp.arange(-1, LZ + 1, dtype=jnp.int32).astype(jnp.float32)
    positions = jnp.stack([padded[0] + grid_x[:, None, None, None], padded[1] + grid_y[None, :, None, None], padded[2] + grid_z[None, None, :, None]])
    charge_pad = jnp.pad(charge_four, ((1, 1), (1, 1), (1, 1), (0, 0)))
    targets_all = positions[:, 1:-1, 1:-1, 1:-1]

    def near_column(column):
        target_slice = lax.dynamic_slice_in_dim(targets_all, column, 1, 1)
        source_slice = lax.dynamic_slice_in_dim(positions, column, 3, 1)
        charge_slice = lax.dynamic_slice_in_dim(charge_pad, column, 3, 0)
        return near_field(target_slice, source_slice, charge_slice)[0]
    near_potential = lax.map(near_column, jnp.arange(NX, dtype=jnp.int32))
    return (far_potential + near_potential).reshape(NX, NY, LZ * PPL)
```

```python
import functools

import jax
import jax.numpy as jnp
import ml_dtypes
import numpy as np
from jax import lax
from jax.experimental import pallas as pl
from jax.experimental.pallas import tpu as pltpu
from jax.sharding import PartitionSpec as P

MESH = pl.DeviceIdType.MESH
F32 = jnp.float32
BF16 = jnp.bfloat16
DIRS = [(ox, oy) for ox in (-1, 0, 1) for oy in (-1, 0, 1) if (ox, oy) != (0, 0)]
ROWS = (1, 2, 3, -1, -2, -3)
TILES = 25


def nodes():
    return np.cos((2.0 * np.arange(4) + 1.0) * np.pi / 8.0)


def cubic():
    t = nodes()
    t2, t3 = 2 * t * t - 1, 4 * t**3 - 3 * t
    return np.stack([0.25 - 0.5 * t2, 0.5 * t - 1.5 * t3, t2, 2 * t3])


def split(x):
    hi = x.astype(ml_dtypes.bfloat16)
    lo = (x - hi.astype(np.float64)).astype(ml_dtypes.bfloat16)
    return hi, lo


def constants():
    t = nodes()
    c = cubic()
    shifted = (t[None, :] + 2.0 * np.arange(2)[:, None] - 1.0) / 2.0
    f = sum(c[k][None, None, :] * shifted[:, :, None] ** k for k in range(4))
    up = np.einsum("xia,yjb,zkc->xyzijkabc", f, f, f).reshape(2, 2, 2, 64, 64)
    uf = up.transpose(2, 4, 0, 1, 3).reshape(128, 256)
    uf = np.concatenate(split(uf), 0)
    u2 = up.transpose(0, 1, 2, 4, 3).reshape(2, 256, 64)
    u2 = np.concatenate(split(u2), 1)
    dn = up.reshape(4, 128, 64)
    dn = np.concatenate(split(dn), 1)
    n = np.arange(64)
    na, nb, nc = n // 16, n // 4 % 4, n % 4
    lane = np.arange(TILES * 128)
    pair, ln = lane // 64, lane % 64
    dx, dy = pair // 7 - 3, pair % 7 - 3
    lxy = np.zeros((TILES, 8, 128))
    lxy[:, 0] = (dx + t[na[ln]] / 2).reshape(TILES, 128)
    lxy[:, 1] = (dy + t[nb[ln]] / 2).reshape(TILES, 128)
    lxy[:, 2] = ((abs(dx) <= 1) & (abs(dy) <= 1)).reshape(TILES, 128)
    rxy = np.broadcast_to(np.stack([t[na] / 2, t[nb] / 2])[:, :, None], (2, 64, 128))
    sub = np.arange(8)
    l128 = np.arange(128)
    z2 = np.stack(
        [
            (dz + t[l128 % 4][None, :] / 2 - t[sub % 4][:, None] / 2) ** 2
            for dz in range(-3, 4)
        ]
    )
    w = np.zeros((3, 8, 128))
    for level, start, length in ((0, 0, 64), (1, 64, 16), (2, 80, 16)):
        for i, dz in enumerate(range(-3, 4)):
            for l in range(start, start + length):
                z = (l - start) % 16
                if z % 2**level or not 0 <= z + dz * 2**level < 16:
                    continue
                odd = (z >> level) % 2
                if (dz == 3 and odd) or (dz == -3 and not odd):
                    continue
                w[level, i, l] = 0.5**level
    pc = np.zeros((3, 4, 8, 128))
    for k in range(4):
        pc[0, k] = c[k][sub % 4][:, None]
        pc[1, k] = c[k][sub // 4][:, None]
        pc[2, k] = c[k][2 + sub // 4][:, None]
    l3 = np.zeros((8, 128))
    l3[0] = t[na[l128 % 64]] / 2
    l3[1] = t[nb[l128 % 64]] / 2
    f32 = [x.astype(np.float32) for x in (lxy, rxy, z2, w, pc, l3)]
    return [uf, u2, dn] + f32


def pair_split(x):
    hi = x.astype(BF16)
    lo = (x - hi.astype(F32)).astype(BF16)
    return hi, lo


def wide(x):
    return jnp.concatenate(pair_split(x), 1)


def folded(product, rows):
    return product[:rows, :128] + product[:rows, 128:] + product[rows:, :128] + product[rows:, 128:]


def dot(left, right):
    return jnp.dot(left, right, preferred_element_type=F32)


def kernel(
    count_x, count_y,
    own_ref, uf_ref, u2_ref, dn_ref, lxy_ref, rxy_ref, z2_ref, w_ref, pc_ref, l3_ref,
    out_ref,
    halo, moments, near_rows, rows, coarse, sources, targets, sums, table, table3, right, right3,
    product, bq, leaf,
    halo_s, halo_r, mom_s, mom_r, g_s, g_r, row_s, row_r, coarse_s, coarse_r,
):
    ix = lax.axis_index("gx")
    iy = lax.axis_index("gy")
    lane = lax.broadcasted_iota(jnp.int32, (8, 128), 1)
    lane64 = lax.broadcasted_iota(jnp.int32, (64, 128), 1)
    row64 = lax.broadcasted_iota(jnp.int32, (64, 128), 0)
    eye = row64 == lane64 % 64
    c = cubic()

    def remote(src, dst, send, recv, dx, dy):
        device = (lax.rem(ix + dx + count_x, count_x), lax.rem(iy + dy + count_y, count_y))
        return pltpu.make_async_remote_copy(
            src_ref=src, dst_ref=dst, send_sem=send, recv_sem=recv,
            device_id=device, device_id_type=MESH,
        )

    barrier = pltpu.get_barrier_semaphore()

    def greet(dx, dy):
        device = (lax.rem(ix + dx + count_x, count_x), lax.rem(iy + dy + count_y, count_y))
        pl.semaphore_signal(barrier, inc=1, device_id=device, device_id_type=MESH)

    for ox, oy in DIRS:
        greet(ox, oy)

    @pl.loop(1, count_y)
    def _(k):
        greet(0, k)

    @pl.loop(1, count_x)
    def _(k):
        greet(k, 0)

    def basis(column, k):
        x = 2.0 * halo[column, 0, k : k + 1, :] - 1.0
        y = 2.0 * halo[column, 1, k : k + 1, :] - 1.0
        z = 2.0 * halo[column, 2, k : k + 1, :] - 1.0

        def poly(i, u):
            return ((pc_ref[i, 3] * u + pc_ref[i, 2]) * u + pc_ref[i, 1]) * u + pc_ref[i, 0]

        along_z = poly(0, z)
        low, high = poly(1, y) * along_z, poly(2, y) * along_z
        pieces = []
        for a in range(4):
            s = ((float(c[3, a]) * x + float(c[2, a])) * x + float(c[1, a])) * x + float(c[0, a])
            pieces += [s * low, s * high]
        return jnp.concatenate(pieces, 0)

    def column_of(cx, cy):
        return (1 + cx) * 4 + 1 + cy

    for cx in range(2):
        for cy in range(2):
            halo[column_of(cx, cy)] = own_ref[cx, cy]
    half_row = lax.broadcasted_iota(jnp.int32, (128, 128), 0) // 64
    half_lane = lax.broadcasted_iota(jnp.int32, (128, 128), 1)
    parity = (half_row == half_lane % 2).astype(F32).astype(BF16)
    halves = (half_row == half_lane // 64).astype(F32).astype(BF16)
    leaf[...] = jnp.zeros((64, 128), F32)

    @pl.loop(0, 4)
    def _(col):
        column = (1 + col // 2) * 4 + 1 + col % 2
        for k in range(8):
            value = basis(column, k) * halo[column, 3, k : k + 1, :]
            hi, lo = pair_split(value)
            bq[64 * k : 64 * k + 64] = hi
            bq[512 + 64 * k : 576 + 64 * k] = lo
        summed = dot(bq[...], parity)
        total = leaf[...]
        for k in range(8):
            here = (lane64 % 64) // 2 == col * 8 + k
            total = jnp.where(
                here,
                summed[64 * k : 64 * k + 64] + summed[512 + 64 * k : 576 + 64 * k],
                total,
            )
        leaf[...] = total

    own = leaf[...]
    moments[4] = jnp.where(lane64[:32] < 64, own[:32], own[32:])
    stacked = jnp.concatenate(
        [own] + [pltpu.roll(own, 128 - 16 * col, 1) for col in range(1, 4)], 0
    )
    first = folded(dot(uf_ref[...], wide(stacked)), 128)
    first = first[:64] + pltpu.roll(first[64:], 127, 1)
    first = jnp.where((lane64 < 16) & (lane64 % 2 == 0), first, 0.0)
    first = first[:32] + pltpu.roll(first[32:], 1, 1)
    near_rows[iy] = pltpu.roll(first, 16 * iy, 1)

    pl.semaphore_wait(barrier, len(DIRS) + count_y - 1 + count_x - 1)

    gy_copies = []
    for k in range(1, count_y):
        copy = remote(near_rows.at[iy], near_rows.at[iy], g_s.at[k], g_r.at[k], 0, k)
        copy.start()
        gy_copies.append(copy)
    halo_copies, moment_copies = [], []
    for d, (ox, oy) in enumerate(DIRS):
        take_x = {1: [2], -1: [1], 0: [1, 2]}[ox]
        put_x = {1: [0], -1: [3], 0: [1, 2]}[ox]
        take_y = {1: (2, 1), -1: (1, 1), 0: (1, 2)}[oy]
        put_y = {1: 0, -1: 3, 0: 1}[oy]
        for i, (a, b) in enumerate(zip(take_x, put_x)):
            copy = remote(
                halo.at[pl.ds(a * 4 + take_y[0], take_y[1])],
                halo.at[pl.ds(b * 4 + put_y, take_y[1])],
                halo_s.at[2 * d + i], halo_r.at[2 * d + i], ox, oy,
            )
            copy.start()
            halo_copies.append(copy)
    for d, (ox, oy) in enumerate(DIRS):
        slot = (1 - ox) * 3 + 1 - oy
        copy = remote(moments.at[4], moments.at[slot], mom_s.at[d], mom_r.at[d], ox, oy)
        copy.start()
        moment_copies.append(copy)

    @pl.loop(0, TILES)
    def _(j):
        gap_x = lxy_ref[j, 0:1, :] - rxy_ref[0]
        gap_y = lxy_ref[j, 1:2, :] - rxy_ref[1]
        adjacent = jnp.broadcast_to(lxy_ref[j, 2:3, :], (64, 128)) > 0.5
        plane = gap_x * gap_x + gap_y * gap_y
        at = pl.ds(pl.multiple_of(j * 128, 128), 128)
        for i in range(7):
            value = lax.rsqrt(plane + jnp.concatenate([z2_ref[i]] * 8, 0))
            if i in (2, 3, 4):
                value = jnp.where(adjacent, 0.0, value)
            hi, lo = pair_split(value)
            table[64 * i : 64 * i + 64, at] = hi
            table[448 + 64 * i : 512 + 64 * i, at] = lo

    @pl.loop(0, count_x // 4)
    def _(j):
        apart = (j - ix // 4).astype(F32)
        side = (lane64 // 64 - iy // 4).astype(F32)
        gap_x = apart + l3_ref[0:1, :] - rxy_ref[0]
        gap_y = side + l3_ref[1:2, :] - rxy_ref[1]
        adjacent = jnp.maximum(jnp.abs(side), jnp.abs(apart)) <= 1.0
        plane = gap_x * gap_x + gap_y * gap_y
        at = pl.ds(pl.multiple_of(j * 128, 128), 128)
        for i in range(3):
            value = lax.rsqrt(plane + jnp.concatenate([z2_ref[i + 2]] * 8, 0))
            value = jnp.where(adjacent, 0.0, value)
            hi, lo = pair_split(value)
            table3[64 * i : 64 * i + 64, at] = hi
            table3[192 + 64 * i : 256 + 64 * i, at] = lo

    for copy in gy_copies:
        copy.wait_recv()
    row = near_rows[0]
    for k in range(1, count_y):
        row = row + near_rows[k]
    rows[ix] = row
    full = jnp.concatenate([row, pltpu.roll(row, 127, 1)], 0)
    full = jnp.where(lane64 % 2 == 0, full, 0.0)

    def part(source, which, step_z, step_y):
        o = folded(dot(u2_ref[which], wide(source)), 256)
        return (
            o[:64]
            + pltpu.roll(o[64:128], 128 - step_z, 1)
            + pltpu.roll(o[128:192], 128 - step_y, 1)
            + pltpu.roll(o[192:], 128 - step_z - step_y, 1)
        )

    second = part(full, ix % 2, 2, 16)
    second = jnp.where((lane64 // 16 % 2 == 0) & (lane64 % 4 == 0), second, 0.0)
    third = part(second, ix // 2 % 2, 4, 32)
    third = jnp.where((lane64 // 16 % 4 == 0) & (lane64 % 8 == 0), third, 0.0)
    packed = second[:16] + pltpu.roll(third[:16], 16, 1)
    for g in range(1, 4):
        at = slice(16 * g, 16 * g + 16)
        packed = packed + pltpu.roll(second[at], g, 1) + pltpu.roll(third[at], 16 + g, 1)
    coarse[ix] = packed

    row_copies = []
    for i, dx in enumerate(ROWS):
        copy = remote(rows.at[ix], rows.at[ix], row_s.at[i], row_r.at[i], dx, 0)
        copy.start()
        row_copies.append(copy)

    @pl.loop(1, count_x)
    def _(k):
        remote(coarse.at[ix], coarse.at[ix], coarse_s.at[k], coarse_r.at[k], k, 0).start()

    for col in range(4):
        column = column_of(col // 2, col % 2)
        for comp in range(3):
            value = halo[column, comp]
            if comp == 0:
                value = value + float(col // 2)
            if comp == 1:
                value = value + float(col % 2)
            if comp == 2:
                k2 = lax.broadcasted_iota(jnp.int32, (8, 128), 0)
                value = value + (2 * k2 + lane // 64).astype(F32)
            turned = value.T
            for k in range(8):
                spread = jnp.broadcast_to(turned[:, k : k + 1], (128, 128))
                targets[col * 8 + k, comp] = jnp.where(lane64 < 64, spread[:64], spread[64:])

    for copy in halo_copies:
        copy.wait_recv()

    inside_x = [ix > 0, None, None, ix < count_x - 1]
    inside_y = [iy > 0, None, None, iy < count_y - 1]
    sub = lax.broadcasted_iota(jnp.int32, (8, 128), 0)
    for wx in range(4):
        for wy in range(4):
            column = wx * 4 + wy
            for comp in range(4):
                value = halo[column, comp]
                if comp == 0:
                    value = value + float(wx - 1)
                if comp == 1:
                    value = value + float(wy - 1)
                if comp == 2:
                    value = value + (2 * sub + lane // 64).astype(F32)
                if comp == 3:
                    for inside in (inside_x[wx], inside_y[wy]):
                        if inside is not None:
                            value = value * inside.astype(F32)
                turned = pltpu.roll(value, 64, 1)
                below = jnp.where(lane < 64, pltpu.roll(turned, 1, 0), turned)
                above = jnp.where(lane < 64, turned, pltpu.roll(turned, 7, 0))
                if comp == 3:
                    below = jnp.where((lane < 64) & (sub == 0), 0.0, below)
                    above = jnp.where((lane >= 64) & (sub == 7), 0.0, above)
                sources[column, 0, comp] = below
                sources[column, 1, comp] = value
                sources[column, 2, comp] = above

    @pl.loop(0, 32)
    def _(block):
        col, k = block // 8, block % 8
        cx, cy = col // 2, col % 2
        tx, ty, tz = targets[block, 0], targets[block, 1], targets[block, 2]
        total = jnp.zeros((64, 128), F32)
        for dx in range(3):
            for dy in range(3):
                column = (cx + dx) * 4 + cy + dy
                for dz in range(3):
                    sx = sources[column, dz, 0, pl.ds(k, 1), :]
                    sy = sources[column, dz, 1, pl.ds(k, 1), :]
                    sz = sources[column, dz, 2, pl.ds(k, 1), :]
                    q = sources[column, dz, 3, pl.ds(k, 1), :]
                    gx, gy, gz = tx - sx, ty - sy, tz - sz
                    inverse = lax.rsqrt(gx * gx + gy * gy + gz * gz)
                    if (dx, dy, dz) == (1, 1, 1):
                        inverse = jnp.where(eye, 0.0, inverse)
                    total = total + inverse * q
        sums[block] = total

    for copy in moment_copies:
        copy.wait_recv()
    for copy in row_copies:
        copy.wait_recv()

    @pl.loop(1, count_x)
    def _(k):
        remote(coarse.at[ix], coarse.at[ix], coarse_s.at[k], coarse_r.at[k], k, 0).wait_recv()

    def unpacked(value, start):
        return jnp.concatenate(
            [pltpu.roll(value, lax.rem(start - g + 128, 128), 1) for g in range(4)], 0
        )

    for j in range(count_x // 4):
        group = coarse[4 * j] + coarse[4 * j + 1] + coarse[4 * j + 2] + coarse[4 * j + 3]
        third = unpacked(group, jnp.int32(112))
        right3[128 * j : 128 * j + 64] = wide(third)
        right3[128 * j + 64 : 128 * j + 128] = wide(pltpu.roll(third, 64, 1))
    o = folded(dot(table3[...], right3[...]), 192)
    local = o[64:128]
    local = local + jnp.where(lane64 == 0, pltpu.roll(o[128:], 120, 1), 0.0)
    local = local + jnp.where(lane64 == 8, pltpu.roll(o[:64], 8, 1), 0.0)
    local3 = jnp.where((lane64 < 16) & (lane64 % 8 == 0), 0.125 * local, 0.0)

    plain, crossed = {}, {}
    for ox in (-1, 0, 1):
        for oy in (-1, 0, 1):
            value = moments[(ox + 1) * 3 + oy + 1]
            turned = pltpu.roll(value, 64, 1)
            lane32 = lane64[:32]
            value = jnp.concatenate(
                [jnp.where(lane32 < 64, value, turned), jnp.where(lane32 < 64, turned, value)], 0
            )
            scale = F32(1.0)
            if ox:
                scale = scale * (ix > 0 if ox < 0 else ix < count_x - 1).astype(F32)
            if oy:
                scale = scale * (iy > 0 if oy < 0 else iy < count_y - 1).astype(F32)
            plain[ox, oy] = value * scale
    by_x = lane64 // 32 % 2
    by_y = lane64 // 16 % 2

    def swap_y(value):
        return jnp.where(by_y == 0, pltpu.roll(value, 112, 1), pltpu.roll(value, 16, 1))

    def leaf_block(dx, dy):
        result = None
        for cx in range(2):
            for cy in range(2):
                ox, oy = (cx + dx) // 2, (cy + dy) // 2
                if abs(ox) > 1 or abs(oy) > 1:
                    continue
                value = plain[ox, oy]
                if dy % 2:
                    value = swap_y(value)
                if dx % 2:
                    value = pltpu.roll(value, 32, 1)
                mine = (by_x == cx) & (by_y == cy)
                value = jnp.where(mine, value, 0.0)
                result = value if result is None else result + value
        return result

    def within(value, count, step, odd):
        ok = (value >= 0) & (value < count)
        if step == 3:
            ok = ok & (odd == 0)
        if step == -3:
            ok = ok & (odd == 1)
        return ok.astype(F32)

    for dx in range(-3, 4):
        line = rows[lax.rem(ix + dx + count_x, count_x)]
        line = jnp.concatenate([line, pltpu.roll(line, 127, 1)], 0)
        line = pltpu.roll(line, lax.rem(64 - 16 * iy + 128, 128), 1)
        line = line * within(ix + dx, count_x, dx, ix % 2)
        x2 = ix // 2 + dx
        base = lax.rem(2 * x2 + 2 * count_x, count_x)
        pair = unpacked(coarse[base] + coarse[base + 1], lax.rem(80 - 32 * (iy // 2) + 128, 128))
        pair = pair * within(x2, count_x // 2, dx, ix // 2 % 2)
        for dy in range(-3, 4):
            one = pltpu.roll(line, (-16 * dy) % 128, 1) * within(iy + dy, count_y, dy, iy % 2)
            two = pltpu.roll(pair, (-32 * dy) % 128, 1)
            two = two * within(iy // 2 + dy, count_y // 2, dy, iy // 2 % 2)
            value = jnp.where(lane64 < 64, leaf_block(dx, dy), jnp.where(lane64 < 80, one, two))
            value = jnp.where(lane64 < 96, value, 0.0)
            at = ((dx + 3) * 7 + dy + 3) * 64
            right[at : at + 64] = wide(value)
    right[49 * 64 : 50 * 64] = jnp.zeros((64, 256), BF16)

    @pl.loop(0, 7)
    def _(j):
        at = pl.ds(pl.multiple_of(j * 128, 128), 128)
        product[at] = dot(table[at], right[...])

    far = jnp.zeros((64, 128), F32)
    for i in range(7):
        dz = i - 3
        o = product[64 * i : 64 * i + 64]
        o2 = product[448 + 64 * i : 512 + 64 * i]
        o = o[:, :128] + o[:, 128:] + o2[:, :128] + o2[:, 128:]
        for level in range(3):
            value = o if dz == 0 else pltpu.roll(o, (-dz * 2**level) % 128, 1)
            far = far + value * w_ref[level, i : i + 1, :]

    def down(source, which, step):
        o = folded(dot(dn_ref[which], wide(source)), 128)
        return jnp.where(lane64 % (2 * step) == 0, o[:64], pltpu.roll(o[64:], step, 1))

    low = lane64 < 16
    local2 = down(local3, ix // 2 % 2 * 2 + iy // 2 % 2, 4) + pltpu.roll(far, 48, 1)
    local2 = jnp.where(low & (lane64 % 4 == 0), local2, 0.0)
    local1 = down(local2, ix % 2 * 2 + iy % 2, 2) + pltpu.roll(far, 64, 1)
    local1 = jnp.where(low & (lane64 % 2 == 0), local1, 0.0)
    local0 = far
    for col in range(4):
        value = down(local1, col, 1)
        if col:
            value = pltpu.roll(value, 16 * col, 1)
        local0 = local0 + jnp.where(lane64 // 16 == col, value, 0.0)
    leaf[...] = local0

    @pl.loop(0, 4)
    def _(col):
        column = (1 + col // 2) * 4 + 1 + col % 2
        near = sums[pl.ds(pl.multiple_of(col * 8, 8), 8)].reshape(512, 128)
        hi, lo = pair_split(near)
        near = dot(hi, halves) + dot(lo, halves)
        here = pltpu.roll(leaf[...], lax.rem(128 - 16 * col, 128), 1)
        for k in range(8):
            spread = jnp.where(
                lane64 < 64,
                jnp.broadcast_to(here[:, 2 * k : 2 * k + 1], (64, 128)),
                jnp.broadcast_to(here[:, 2 * k + 1 : 2 * k + 2], (64, 128)),
            )
            both = basis(column, k) * spread
            both = both + jnp.where(eye, near[64 * k : 64 * k + 64], 0.0)
            out_ref[col, k : k + 1, :] = jnp.sum(both, 0, keepdims=True)

    for copy in gy_copies + halo_copies + moment_copies + row_copies:
        copy.wait_send()

    @pl.loop(1, count_x)
    def _(k):
        remote(coarse.at[ix], coarse.at[ix], coarse_s.at[k], coarse_r.at[k], k, 0).wait_send()


def solution(mesh):
    count_x, count_y = mesh.shape["gx"], mesh.shape["gy"]
    fixed = constants()
    vmem = pl.BlockSpec(memory_space=pltpu.VMEM)
    dma = pltpu.SemaphoreType.DMA
    call = pl.pallas_call(
        functools.partial(kernel, count_x, count_y),
        out_shape=jax.ShapeDtypeStruct((4, 8, 128), F32),
        in_specs=[vmem] * (1 + len(fixed)),
        out_specs=vmem,
        scratch_shapes=[
            pltpu.VMEM((16, 4, 8, 128), F32),
            pltpu.VMEM((9, 32, 128), F32),
            pltpu.VMEM((count_y, 32, 128), F32),
            pltpu.VMEM((count_x, 32, 128), F32),
            pltpu.VMEM((count_x, 16, 128), F32),
            pltpu.VMEM((16, 3, 4, 8, 128), F32),
            pltpu.VMEM((32, 3, 64, 128), F32),
            pltpu.VMEM((32, 64, 128), F32),
            pltpu.VMEM((896, TILES * 128), BF16),
            pltpu.VMEM((384, count_x // 4 * 128), BF16),
            pltpu.VMEM((TILES * 128, 256), BF16),
            pltpu.VMEM((count_x // 4 * 128, 256), BF16),
            pltpu.VMEM((896, 256), F32),
            pltpu.VMEM((1024, 128), BF16),
            pltpu.VMEM((64, 128), F32),
            dma((16,)),
            dma((16,)),
            dma((8,)),
            dma((8,)),
            dma((count_y,)),
            dma((count_y,)),
            dma((6,)),
            dma((6,)),
            dma((count_x,)),
            dma((count_x,)),
        ],
        compiler_params=pltpu.CompilerParams(
            collective_id=0, has_side_effects=True, vmem_limit_bytes=48 << 20
        ),
    )

    def body(offsets, charges):
        own = jnp.concatenate([offsets, charges[None]], 0)
        own = own.transpose(1, 2, 0, 3).reshape(2, 2, 4, 8, 128)
        return call(own, *fixed).reshape(2, 2, 1024)

    in_specs = (P(None, "gx", "gy", None), P("gx", "gy", None))
    out_specs = P("gx", "gy", None)
    return jax.shard_map(body, mesh=mesh, in_specs=in_specs, out_specs=out_specs, check_vma=False)
```

```python
import functools

import jax
import jax.numpy as jnp
import ml_dtypes
import numpy as np
from jax import lax
from jax.experimental import pallas as pl
from jax.experimental.pallas import tpu as pltpu
from jax.sharding import PartitionSpec as P

MESH = pl.DeviceIdType.MESH
F32 = jnp.float32
BF16 = jnp.bfloat16
DIRS = [(ox, oy) for ox in (-1, 0, 1) for oy in (-1, 0, 1) if (ox, oy) != (0, 0)]
ROWS = (1, 2, 3, -1, -2, -3)
TILES = 25


def nodes():
    return np.cos((2.0 * np.arange(4) + 1.0) * np.pi / 8.0)


def cubic():
    t = nodes()
    t2, t3 = 2 * t * t - 1, 4 * t**3 - 3 * t
    return np.stack([0.25 - 0.5 * t2, 0.5 * t - 1.5 * t3, t2, 2 * t3])


def split(x):
    hi = x.astype(ml_dtypes.bfloat16)
    lo = (x - hi.astype(np.float64)).astype(ml_dtypes.bfloat16)
    return hi, lo


def constants():
    t = nodes()
    c = cubic()
    shifted = (t[None, :] + 2.0 * np.arange(2)[:, None] - 1.0) / 2.0
    f = sum(c[k][None, None, :] * shifted[:, :, None] ** k for k in range(4))
    up = np.einsum("xia,yjb,zkc->xyzijkabc", f, f, f).reshape(2, 2, 2, 64, 64)
    uf = up.transpose(2, 4, 0, 1, 3).reshape(128, 256)
    uf = np.concatenate(split(uf), 0)
    u2 = up.transpose(0, 1, 2, 4, 3).reshape(2, 256, 64)
    u2 = np.concatenate(split(u2), 1)
    dn = up.reshape(4, 128, 64)
    dn = np.concatenate(split(dn), 1)
    n = np.arange(64)
    na, nb, nc = n // 16, n // 4 % 4, n % 4
    lane = np.arange(TILES * 128)
    pair, ln = lane // 64, lane % 64
    dx, dy = pair // 7 - 3, pair % 7 - 3
    lxy = np.zeros((TILES, 8, 128))
    lxy[:, 0] = (dx + t[na[ln]] / 2).reshape(TILES, 128)
    lxy[:, 1] = (dy + t[nb[ln]] / 2).reshape(TILES, 128)
    lxy[:, 2] = ((abs(dx) <= 1) & (abs(dy) <= 1)).reshape(TILES, 128)
    rxy = np.broadcast_to(np.stack([t[na] / 2, t[nb] / 2])[:, :, None], (2, 64, 128))
    sub = np.arange(8)
    l128 = np.arange(128)
    z2 = np.stack(
        [
            (dz + t[l128 % 4][None, :] / 2 - t[sub % 4][:, None] / 2) ** 2
            for dz in range(-3, 4)
        ]
    )
    w = np.zeros((3, 8, 128))
    for level, start, length in ((0, 0, 64), (1, 64, 16), (2, 80, 16)):
        for i, dz in enumerate(range(-3, 4)):
            for l in range(start, start + length):
                z = (l - start) % 16
                if z % 2**level or not 0 <= z + dz * 2**level < 16:
                    continue
                odd = (z >> level) % 2
                if (dz == 3 and odd) or (dz == -3 and not odd):
                    continue
                w[level, i, l] = 0.5**level
    pc = np.zeros((3, 4, 8, 128))
    for k in range(4):
        pc[0, k] = c[k][sub % 4][:, None]
        pc[1, k] = c[k][sub // 4][:, None]
        pc[2, k] = c[k][2 + sub // 4][:, None]
    l3 = np.zeros((8, 128))
    l3[0] = t[na[l128 % 64]] / 2
    l3[1] = t[nb[l128 % 64]] / 2
    flat = np.concatenate([x.reshape(-1, 128) for x in (pc, lxy, rxy, z2, w, l3)], 0)
    return [flat.astype(np.float32), uf, u2, dn]


def pair_split(x):
    hi = x.astype(BF16)
    lo = (x - hi.astype(F32)).astype(BF16)
    return hi, lo


def wide(x):
    return jnp.concatenate(pair_split(x), 1)


def folded(product, rows):
    return product[:rows, :128] + product[:rows, 128:] + product[rows:, :128] + product[rows:, 128:]


def dot(left, right):
    return jnp.dot(left, right, preferred_element_type=F32)


def kernel(
    count_x, count_y,
    off_hbm, charge_hbm, flat_hbm, uf_hbm, u2_hbm, dn_hbm,
    out_ref,
    off_ref, charge_ref, flat, uf_ref, u2_ref, dn_ref,
    halo, moments, near_rows, rows, coarse, pieces, source, charge, target, sums, near,
    table, table3, right, right3, product, bq, leaf,
    load_s, halo_s, halo_r, mom_s, mom_r, g_s, g_r, row_s, row_r, coarse_s, coarse_r,
):
    loads = [
        pltpu.make_async_copy(src, dst, load_s.at[i])
        for i, (src, dst) in enumerate(
            [(off_hbm, off_ref), (charge_hbm, charge_ref), (flat_hbm, flat)]
            + [(uf_hbm, uf_ref), (u2_hbm, u2_ref), (dn_hbm, dn_ref)]
        )
    ]
    for load in loads:
        load.start()
    at_lxy = 96
    at_rxy = at_lxy + 8 * TILES
    at_z2 = at_rxy + 128
    at_w = at_z2 + 56
    at_l3 = at_w + 24
    ix = lax.axis_index("gx")
    iy = lax.axis_index("gy")
    lane = lax.broadcasted_iota(jnp.int32, (8, 128), 1)
    lane64 = lax.broadcasted_iota(jnp.int32, (64, 128), 1)
    row64 = lax.broadcasted_iota(jnp.int32, (64, 128), 0)
    eye = row64 == lane64 % 64
    c = cubic()

    def remote(src, dst, send, recv, dx, dy):
        device = (lax.rem(ix + dx + count_x, count_x), lax.rem(iy + dy + count_y, count_y))
        return pltpu.make_async_remote_copy(
            src_ref=src, dst_ref=dst, send_sem=send, recv_sem=recv,
            device_id=device, device_id_type=MESH,
        )

    barrier = pltpu.get_barrier_semaphore()

    def greet(dx, dy):
        device = (lax.rem(ix + dx + count_x, count_x), lax.rem(iy + dy + count_y, count_y))
        pl.semaphore_signal(barrier, inc=1, device_id=device, device_id_type=MESH)

    for ox, oy in DIRS:
        greet(ox, oy)

    @pl.loop(1, count_y)
    def _(k):
        greet(0, k)

    @pl.loop(1, count_x)
    def _(k):
        greet(k, 0)

    def basis(column, k):
        x = 2.0 * halo[column, 0, k : k + 1, :] - 1.0
        y = 2.0 * halo[column, 1, k : k + 1, :] - 1.0
        z = 2.0 * halo[column, 2, k : k + 1, :] - 1.0

        def poly(i, u):
            p = [flat[32 * i + 8 * e : 32 * i + 8 * e + 8] for e in range(4)]
            return ((p[3] * u + p[2]) * u + p[1]) * u + p[0]

        along_z = poly(0, z)
        low, high = poly(1, y) * along_z, poly(2, y) * along_z
        pieces = []
        for a in range(4):
            s = ((float(c[3, a]) * x + float(c[2, a])) * x + float(c[1, a])) * x + float(c[0, a])
            pieces += [s * low, s * high]
        return jnp.concatenate(pieces, 0)

    def column_of(cx, cy):
        return (1 + cx) * 4 + 1 + cy

    for load in loads[:3]:
        load.wait()
    for cx in range(2):
        for cy in range(2):
            for k in range(8):
                at = slice(128 * k, 128 * k + 128)
                for comp in range(3):
                    halo[column_of(cx, cy), comp, k : k + 1] = off_ref[comp, cx, cy : cy + 1, at]
                halo[column_of(cx, cy), 3, k : k + 1] = charge_ref[cx, cy : cy + 1, at]
    half_row = lax.broadcasted_iota(jnp.int32, (128, 128), 0) // 64
    half_lane = lax.broadcasted_iota(jnp.int32, (128, 128), 1)
    parity = (half_row == half_lane % 2).astype(F32).astype(BF16)
    halves = (half_row == half_lane // 64).astype(F32).astype(BF16)
    leaf[...] = jnp.zeros((64, 128), F32)

    @pl.loop(0, 4)
    def _(col):
        column = (1 + col // 2) * 4 + 1 + col % 2
        for k in range(8):
            value = basis(column, k) * halo[column, 3, k : k + 1, :]
            hi, lo = pair_split(value)
            bq[64 * k : 64 * k + 64] = hi
            bq[512 + 64 * k : 576 + 64 * k] = lo
        summed = dot(bq[...], parity)
        total = leaf[...]
        for k in range(8):
            here = (lane64 % 64) // 2 == col * 8 + k
            total = jnp.where(
                here,
                summed[64 * k : 64 * k + 64] + summed[512 + 64 * k : 576 + 64 * k],
                total,
            )
        leaf[...] = total

    for load in loads[3:]:
        load.wait()
    own = leaf[...]
    moments[4] = jnp.where(lane64[:32] < 64, own[:32], own[32:])
    stacked = jnp.concatenate(
        [own] + [pltpu.roll(own, 128 - 16 * col, 1) for col in range(1, 4)], 0
    )
    first = folded(dot(uf_ref[...], wide(stacked)), 128)
    first = first[:64] + pltpu.roll(first[64:], 127, 1)
    first = jnp.where((lane64 < 16) & (lane64 % 2 == 0), first, 0.0)
    first = first[:32] + pltpu.roll(first[32:], 1, 1)
    near_rows[iy] = pltpu.roll(first, 16 * iy, 1)

    pl.semaphore_wait(barrier, len(DIRS) + count_y - 1 + count_x - 1)

    gy_copies = []
    for k in range(1, count_y):
        copy = remote(near_rows.at[iy], near_rows.at[iy], g_s.at[k], g_r.at[k], 0, k)
        copy.start()
        gy_copies.append(copy)
    halo_copies, moment_copies = [], []
    for d, (ox, oy) in enumerate(DIRS):
        take_x = {1: [2], -1: [1], 0: [1, 2]}[ox]
        put_x = {1: [0], -1: [3], 0: [1, 2]}[ox]
        take_y = {1: (2, 1), -1: (1, 1), 0: (1, 2)}[oy]
        put_y = {1: 0, -1: 3, 0: 1}[oy]
        for i, (a, b) in enumerate(zip(take_x, put_x)):
            copy = remote(
                halo.at[pl.ds(a * 4 + take_y[0], take_y[1])],
                halo.at[pl.ds(b * 4 + put_y, take_y[1])],
                halo_s.at[2 * d + i], halo_r.at[2 * d + i], ox, oy,
            )
            copy.start()
            halo_copies.append(copy)
    for d, (ox, oy) in enumerate(DIRS):
        slot = (1 - ox) * 3 + 1 - oy
        copy = remote(moments.at[4], moments.at[slot], mom_s.at[d], mom_r.at[d], ox, oy)
        copy.start()
        moment_copies.append(copy)

    @pl.loop(0, TILES)
    def _(j):
        line = flat[pl.ds(pl.multiple_of(at_lxy + 8 * j, 8), 8)]
        gap_x = line[0:1] - flat[at_rxy : at_rxy + 64]
        gap_y = line[1:2] - flat[at_rxy + 64 : at_rxy + 128]
        adjacent = jnp.broadcast_to(line[2:3], (64, 128)) > 0.5
        plane = gap_x * gap_x + gap_y * gap_y
        at = pl.ds(pl.multiple_of(j * 128, 128), 128)
        for i in range(7):
            value = lax.rsqrt(plane + jnp.concatenate([flat[at_z2 + 8 * i : at_z2 + 8 * i + 8]] * 8, 0))
            if i in (2, 3, 4):
                value = jnp.where(adjacent, 0.0, value)
            hi, lo = pair_split(value)
            table[64 * i : 64 * i + 64, at] = hi
            table[448 + 64 * i : 512 + 64 * i, at] = lo

    @pl.loop(0, count_x // 4)
    def _(j):
        apart = (j - ix // 4).astype(F32)
        side = (lane64 // 64 - iy // 4).astype(F32)
        gap_x = apart + flat[at_l3 : at_l3 + 1] - flat[at_rxy : at_rxy + 64]
        gap_y = side + flat[at_l3 + 1 : at_l3 + 2] - flat[at_rxy + 64 : at_rxy + 128]
        adjacent = jnp.maximum(jnp.abs(side), jnp.abs(apart)) <= 1.0
        plane = gap_x * gap_x + gap_y * gap_y
        at = pl.ds(pl.multiple_of(j * 128, 128), 128)
        for i in range(3):
            value = lax.rsqrt(plane + jnp.concatenate([flat[at_z2 + 8 * i + 16 : at_z2 + 8 * i + 24]] * 8, 0))
            value = jnp.where(adjacent, 0.0, value)
            hi, lo = pair_split(value)
            table3[64 * i : 64 * i + 64, at] = hi
            table3[192 + 64 * i : 256 + 64 * i, at] = lo

    for copy in gy_copies:
        copy.wait_recv()
    row = near_rows[0]
    for k in range(1, count_y):
        row = row + near_rows[k]
    rows[ix] = row
    full = jnp.concatenate([row, pltpu.roll(row, 127, 1)], 0)
    full = jnp.where(lane64 % 2 == 0, full, 0.0)

    def part(source, which, step_z, step_y):
        o = folded(dot(u2_ref[which], wide(source)), 256)
        return (
            o[:64]
            + pltpu.roll(o[64:128], 128 - step_z, 1)
            + pltpu.roll(o[128:192], 128 - step_y, 1)
            + pltpu.roll(o[192:], 128 - step_z - step_y, 1)
        )

    second = part(full, ix % 2, 2, 16)
    second = jnp.where((lane64 // 16 % 2 == 0) & (lane64 % 4 == 0), second, 0.0)
    third = part(second, ix // 2 % 2, 4, 32)
    third = jnp.where((lane64 // 16 % 4 == 0) & (lane64 % 8 == 0), third, 0.0)
    packed = second[:16] + pltpu.roll(third[:16], 16, 1)
    for g in range(1, 4):
        at = slice(16 * g, 16 * g + 16)
        packed = packed + pltpu.roll(second[at], g, 1) + pltpu.roll(third[at], 16 + g, 1)
    coarse[ix] = packed

    row_copies = []
    for i, dx in enumerate(ROWS):
        copy = remote(rows.at[ix], rows.at[ix], row_s.at[i], row_r.at[i], dx, 0)
        copy.start()
        row_copies.append(copy)

    @pl.loop(1, count_x)
    def _(k):
        remote(coarse.at[ix], coarse.at[ix], coarse_s.at[k], coarse_r.at[k], k, 0).start()

    sub = lax.broadcasted_iota(jnp.int32, (8, 128), 0)
    first_term = (sub == 0) | (sub == 1) | (sub == 3)
    second_term = (sub == 2) | (sub == 4)
    half = (lane // 64).astype(F32)

    def three(value):
        a = value.astype(BF16).astype(F32)
        rest = value - a
        b = rest.astype(BF16).astype(F32)
        return [a, b, rest - b]

    def features(column, wx, wy, both):
        x = halo[column, 0] + (wx - 1.0)
        y = halo[column, 1] + (wy - 1.0)
        z = halo[column, 2] + (half - 1.0)
        plane = x * x + y * y
        parts = three(x) + three(y) + three(z) + three(plane + z * z)
        if both:
            beside = z + (2.0 - 4.0 * half)
            parts += three(beside) + three(plane + beside * beside)
        for i, part in enumerate(parts):
            pieces[i] = part

    def spread(i, k):
        return jnp.broadcast_to(pieces[i, k : k + 1], (8, 128))

    def chosen(i, k, six, seven, terms):
        a, b, c = (spread(i + e, k) for e in range(3))
        value = jnp.where(terms[0], a, jnp.where(terms[1], b, c))
        return jnp.where(sub == 6, six, jnp.where(sub == 7, seven, value))

    zero8 = jnp.zeros((8, 128), F32)
    one8 = jnp.ones((8, 128), F32)
    t_terms = ((sub == 0) | (sub == 2) | (sub == 5), (sub == 1) | (sub == 4))
    s_terms = (first_term, second_term)
    scale8 = jnp.where(sub < 6, -2.0, 1.0)

    @pl.loop(0, 4)
    def _(col):
        cx, cy = col // 2, col % 2
        features((1 + cx) * 4 + 1 + cy, cx.astype(F32), cy.astype(F32), False)
        for k in range(0, 8, 2):
            turned = []
            for e in (k, k + 1):
                tiles = [
                    chosen(0, e, one8, one8, t_terms),
                    chosen(3, e, one8, spread(9, e), t_terms),
                    chosen(6, e, spread(10, e), spread(11, e), t_terms),
                ]
                tiles = jnp.concatenate([t * scale8 for t in tiles] + [zero8], 0)
                turned.append((tiles, pltpu.roll(tiles, 64, 1)))
            lane32 = lane64[:32] < 64
            upper = jnp.where(lane32, turned[0][0], turned[1][1])
            lower = jnp.where(lane32, turned[0][1], turned[1][0])
            stack = jnp.concatenate([upper, lower], 0).T.astype(BF16)
            target[col * 8 + k] = stack[:64]
            target[col * 8 + k + 1] = stack[64:]

    for copy in halo_copies:
        copy.wait_recv()

    outside = jnp.where(lax.broadcasted_iota(jnp.int32, (32, 128), 0) == 6, 16384.0, 0.0)
    lane32 = lane64[:32] < 64
    left_half = lane32
    outside_low = jnp.where(left_half, outside, 0.0).astype(BF16)
    outside_high = jnp.where(left_half, 0.0, outside).astype(BF16)

    @pl.loop(0, 16)
    def _(column):
        wx, wy = column // 4, column % 4
        features(column, wx.astype(F32) - 1.0, wy.astype(F32) - 1.0, True)
        at_x, at_y = 2 * ix + wx - 1, 2 * iy + wy - 1
        inside = (at_x >= 0) & (at_x < 2 * count_x) & (at_y >= 0) & (at_y < 2 * count_y)
        q = halo[column, 3] * inside.astype(F32)
        after = jnp.where(sub == 7, 0.0, pltpu.roll(q, 7, 0))
        before = jnp.where(sub == 0, 0.0, pltpu.roll(q, 1, 0))
        charge[column, 0] = jnp.where(lane < 64, q, before)
        charge[column, 1] = q
        charge[column, 2] = jnp.where(lane < 64, after, q)
        source[column, 9, 2] = outside_low
        source[column, 0, 3] = outside_high
        for k in range(8):
            own_tiles = [
                chosen(0, k, spread(9, k), spread(10, k), s_terms),
                chosen(3, k, spread(11, k), one8, s_terms),
                chosen(6, k, one8, one8, s_terms),
                zero8,
            ]
            beside_tiles = [
                jnp.where(sub == 6, spread(15, k), jnp.where(sub == 7, spread(16, k), own_tiles[0])),
                jnp.where(sub == 6, spread(17, k), own_tiles[1]),
                chosen(12, k, one8, one8, s_terms),
                zero8,
            ]
            for e, tiles in enumerate((own_tiles, beside_tiles)):
                tiles = jnp.concatenate(tiles, 0)
                source[column, k + 1, 2 * e] = jnp.where(left_half, tiles, 0.0).astype(BF16)
                source[column, k + 1, 2 * e + 1] = jnp.where(left_half, 0.0, tiles).astype(BF16)

    def near_block(block, carry):
        col, k = block // 8, block % 8
        cx, cy = col // 2, col % 2
        mine = target[block]
        straight = jnp.zeros((64, 128), F32)
        crossed = jnp.zeros((64, 128), F32)
        columns = [(cx + dx) * 4 + cy + dy for dx in range(3) for dy in range(3)]

        def side(column, a, b):
            return jnp.concatenate([source[column, a[0], a[1]], source[column, b[0], b[1]]], 0)

        def row_of(column, dz):
            return charge[column, dz, pl.ds(k, 1), :]

        for column in columns:
            above = side(column, (k + 1, 1), (k + 2, 2))
            below = side(column, (k, 3), (k + 1, 0))
            inverse = lax.rsqrt(dot(mine, jnp.concatenate([above, below], 1)))
            crossed = crossed + inverse[:, :128] * row_of(column, 2)
            crossed = crossed + inverse[:, 128:] * row_of(column, 0)
        for i in range(0, 9, 2):
            group = columns[i : i + 2]
            both = [side(column, (k + 1, 0), (k + 1, 1)) for column in group]
            inverse = lax.rsqrt(dot(mine, jnp.concatenate(both, 1)))
            for e, column in enumerate(group):
                value = inverse[:, 128 * e : 128 * e + 128]
                if i + e == 4:
                    value = jnp.where(eye, 0.0, value)
                straight = straight + value * row_of(column, 1)
        sums[block] = straight + pltpu.roll(crossed, 64, 1)
        return carry

    lax.fori_loop(0, 32, near_block, 0, unroll=2)

    @pl.loop(0, 4)
    def _(col):
        value = sums[pl.ds(pl.multiple_of(col * 8, 8), 8)].reshape(512, 128)
        hi, lo = pair_split(value)
        value = dot(hi, halves) + dot(lo, halves)
        for k in range(8):
            mine = jnp.where(eye, value[64 * k : 64 * k + 64], 0.0)
            near[col, k : k + 1] = jnp.sum(mine, 0, keepdims=True)

    for copy in moment_copies:
        copy.wait_recv()
    for copy in row_copies:
        copy.wait_recv()

    @pl.loop(1, count_x)
    def _(k):
        remote(coarse.at[ix], coarse.at[ix], coarse_s.at[k], coarse_r.at[k], k, 0).wait_recv()

    def unpacked(value, start):
        return jnp.concatenate(
            [pltpu.roll(value, lax.rem(start - g + 128, 128), 1) for g in range(4)], 0
        )

    for j in range(count_x // 4):
        group = coarse[4 * j] + coarse[4 * j + 1] + coarse[4 * j + 2] + coarse[4 * j + 3]
        third = unpacked(group, jnp.int32(112))
        right3[128 * j : 128 * j + 64] = wide(third)
        right3[128 * j + 64 : 128 * j + 128] = wide(pltpu.roll(third, 64, 1))
    o = folded(dot(table3[...], right3[...]), 192)
    local = o[64:128]
    local = local + jnp.where(lane64 == 0, pltpu.roll(o[128:], 120, 1), 0.0)
    local = local + jnp.where(lane64 == 8, pltpu.roll(o[:64], 8, 1), 0.0)
    local3 = jnp.where((lane64 < 16) & (lane64 % 8 == 0), 0.125 * local, 0.0)

    plain, crossed = {}, {}
    for ox in (-1, 0, 1):
        for oy in (-1, 0, 1):
            value = moments[(ox + 1) * 3 + oy + 1]
            turned = pltpu.roll(value, 64, 1)
            lane32 = lane64[:32]
            value = jnp.concatenate(
                [jnp.where(lane32 < 64, value, turned), jnp.where(lane32 < 64, turned, value)], 0
            )
            scale = F32(1.0)
            if ox:
                scale = scale * (ix > 0 if ox < 0 else ix < count_x - 1).astype(F32)
            if oy:
                scale = scale * (iy > 0 if oy < 0 else iy < count_y - 1).astype(F32)
            plain[ox, oy] = value * scale
    by_x = lane64 // 32 % 2
    by_y = lane64 // 16 % 2

    def swap_y(value):
        return jnp.where(by_y == 0, pltpu.roll(value, 112, 1), pltpu.roll(value, 16, 1))

    def leaf_block(dx, dy):
        result = None
        for cx in range(2):
            for cy in range(2):
                ox, oy = (cx + dx) // 2, (cy + dy) // 2
                if abs(ox) > 1 or abs(oy) > 1:
                    continue
                value = plain[ox, oy]
                if dy % 2:
                    value = swap_y(value)
                if dx % 2:
                    value = pltpu.roll(value, 32, 1)
                mine = (by_x == cx) & (by_y == cy)
                value = jnp.where(mine, value, 0.0)
                result = value if result is None else result + value
        return result

    def within(value, count, step, odd):
        ok = (value >= 0) & (value < count)
        if step == 3:
            ok = ok & (odd == 0)
        if step == -3:
            ok = ok & (odd == 1)
        return ok.astype(F32)

    for dx in range(-3, 4):
        line = rows[lax.rem(ix + dx + count_x, count_x)]
        line = jnp.concatenate([line, pltpu.roll(line, 127, 1)], 0)
        line = pltpu.roll(line, lax.rem(64 - 16 * iy + 128, 128), 1)
        line = line * within(ix + dx, count_x, dx, ix % 2)
        x2 = ix // 2 + dx
        base = lax.rem(2 * x2 + 2 * count_x, count_x)
        pair = unpacked(coarse[base] + coarse[base + 1], lax.rem(80 - 32 * (iy // 2) + 128, 128))
        pair = pair * within(x2, count_x // 2, dx, ix // 2 % 2)
        for dy in range(-3, 4):
            one = pltpu.roll(line, (-16 * dy) % 128, 1) * within(iy + dy, count_y, dy, iy % 2)
            two = pltpu.roll(pair, (-32 * dy) % 128, 1)
            two = two * within(iy // 2 + dy, count_y // 2, dy, iy // 2 % 2)
            value = jnp.where(lane64 < 64, leaf_block(dx, dy), jnp.where(lane64 < 80, one, two))
            value = jnp.where(lane64 < 96, value, 0.0)
            at = ((dx + 3) * 7 + dy + 3) * 64
            right[at : at + 64] = wide(value)
    right[49 * 64 : 50 * 64] = jnp.zeros((64, 256), BF16)

    product[...] = dot(table[...], right[...])

    far = jnp.zeros((64, 128), F32)
    for i in range(7):
        dz = i - 3
        o = product[64 * i : 64 * i + 64]
        o2 = product[448 + 64 * i : 512 + 64 * i]
        o = o[:, :128] + o[:, 128:] + o2[:, :128] + o2[:, 128:]
        for level in range(3):
            value = o if dz == 0 else pltpu.roll(o, (-dz * 2**level) % 128, 1)
            far = far + value * flat[at_w + 8 * level + i : at_w + 8 * level + i + 1]

    def down(source, which, step):
        o = folded(dot(dn_ref[which], wide(source)), 128)
        return jnp.where(lane64 % (2 * step) == 0, o[:64], pltpu.roll(o[64:], step, 1))

    low = lane64 < 16
    local2 = down(local3, ix // 2 % 2 * 2 + iy // 2 % 2, 4) + pltpu.roll(far, 48, 1)
    local2 = jnp.where(low & (lane64 % 4 == 0), local2, 0.0)
    local1 = down(local2, ix % 2 * 2 + iy % 2, 2) + pltpu.roll(far, 64, 1)
    local1 = jnp.where(low & (lane64 % 2 == 0), local1, 0.0)
    local0 = far
    for col in range(4):
        value = down(local1, col, 1)
        if col:
            value = pltpu.roll(value, 16 * col, 1)
        local0 = local0 + jnp.where(lane64 // 16 == col, value, 0.0)
    leaf[...] = local0

    @pl.loop(0, 4)
    def _(col):
        column = (1 + col // 2) * 4 + 1 + col % 2
        here = pltpu.roll(leaf[...], lax.rem(128 - 16 * col, 128), 1)
        for k in range(8):
            spread = jnp.where(
                lane64 < 64,
                jnp.broadcast_to(here[:, 2 * k : 2 * k + 1], (64, 128)),
                jnp.broadcast_to(here[:, 2 * k + 1 : 2 * k + 2], (64, 128)),
            )
            both = basis(column, k) * spread
            near[col, k : k + 1] = jnp.sum(both, 0, keepdims=True) + near[col, k : k + 1]

    for col in range(4):
        for k in range(8):
            at = slice(128 * k, 128 * k + 128)
            out_ref[col // 2, col % 2 : col % 2 + 1, at] = near[col, k : k + 1]

    for copy in gy_copies + halo_copies + moment_copies + row_copies:
        copy.wait_send()

    @pl.loop(1, count_x)
    def _(k):
        remote(coarse.at[ix], coarse.at[ix], coarse_s.at[k], coarse_r.at[k], k, 0).wait_send()


def solution(mesh):
    count_x, count_y = mesh.shape["gx"], mesh.shape["gy"]
    fixed = constants()
    vmem = pl.BlockSpec(memory_space=pltpu.VMEM)
    hbm = pl.BlockSpec(memory_space=pltpu.HBM)
    dma = pltpu.SemaphoreType.DMA
    call = pl.pallas_call(
        functools.partial(kernel, count_x, count_y),
        out_shape=jax.ShapeDtypeStruct((2, 2, 1024), F32),
        in_specs=[hbm] * (2 + len(fixed)),
        out_specs=vmem,
        scratch_shapes=[
            pltpu.VMEM((3, 2, 2, 1024), F32),
            pltpu.VMEM((2, 2, 1024), F32),
            pltpu.VMEM(fixed[0].shape, F32),
            pltpu.VMEM(fixed[1].shape, BF16),
            pltpu.VMEM(fixed[2].shape, BF16),
            pltpu.VMEM(fixed[3].shape, BF16),
            pltpu.VMEM((16, 4, 8, 128), F32),
            pltpu.VMEM((9, 32, 128), F32),
            pltpu.VMEM((count_y, 32, 128), F32),
            pltpu.VMEM((count_x, 32, 128), F32),
            pltpu.VMEM((count_x, 16, 128), F32),
            pltpu.VMEM((18, 8, 128), F32),
            pltpu.VMEM((16, 10, 4, 32, 128), BF16),
            pltpu.VMEM((16, 3, 8, 128), F32),
            pltpu.VMEM((32, 64, 64), BF16),
            pltpu.VMEM((32, 64, 128), F32),
            pltpu.VMEM((4, 8, 128), F32),
            pltpu.VMEM((896, TILES * 128), BF16),
            pltpu.VMEM((384, count_x // 4 * 128), BF16),
            pltpu.VMEM((TILES * 128, 256), BF16),
            pltpu.VMEM((count_x // 4 * 128, 256), BF16),
            pltpu.VMEM((896, 256), F32),
            pltpu.VMEM((1024, 128), BF16),
            pltpu.VMEM((64, 128), F32),
            dma((6,)),
            dma((16,)),
            dma((16,)),
            dma((8,)),
            dma((8,)),
            dma((count_y,)),
            dma((count_y,)),
            dma((6,)),
            dma((6,)),
            dma((count_x,)),
            dma((count_x,)),
        ],
        compiler_params=pltpu.CompilerParams(
            collective_id=0, has_side_effects=True, vmem_limit_bytes=64 << 20
        ),
    )

    def body(offsets, charges):
        return call(offsets, charges, *fixed)

    in_specs = (P(None, "gx", "gy", None), P("gx", "gy", None))
    out_specs = P("gx", "gy", None)
    return jax.shard_map(body, mesh=mesh, in_specs=in_specs, out_specs=out_specs, check_vma=False)
```

```python
import functools

import jax
import jax.numpy as jnp
import ml_dtypes
import numpy as np
from jax import lax
from jax.experimental import pallas as pl
from jax.experimental.pallas import tpu as pltpu
from jax.sharding import PartitionSpec as P

MESH = pl.DeviceIdType.MESH
F32 = jnp.float32
BF16 = jnp.bfloat16
DIRS = [(ox, oy) for ox in (-1, 0, 1) for oy in (-1, 0, 1) if (ox, oy) != (0, 0)]
ROWS = (1, 2, 3, -1, -2, -3)
TILES = 25


def nodes():
    return np.cos((2.0 * np.arange(4) + 1.0) * np.pi / 8.0)


def cubic():
    t = nodes()
    t2, t3 = 2 * t * t - 1, 4 * t**3 - 3 * t
    return np.stack([0.25 - 0.5 * t2, 0.5 * t - 1.5 * t3, t2, 2 * t3])


def split(x):
    hi = x.astype(ml_dtypes.bfloat16)
    lo = (x - hi.astype(np.float64)).astype(ml_dtypes.bfloat16)
    return hi, lo


def constants():
    t = nodes()
    c = cubic()
    shifted = (t[None, :] + 2.0 * np.arange(2)[:, None] - 1.0) / 2.0
    f = sum(c[k][None, None, :] * shifted[:, :, None] ** k for k in range(4))
    up = np.einsum("xia,yjb,zkc->xyzijkabc", f, f, f).reshape(2, 2, 2, 64, 64)
    uf = up.transpose(2, 4, 0, 1, 3).reshape(128, 256)
    uf = np.concatenate(split(uf), 0)
    u2 = up.transpose(0, 1, 2, 4, 3).reshape(2, 256, 64)
    u2 = np.concatenate(split(u2), 1)
    dn = up.reshape(4, 128, 64)
    dn = np.concatenate(split(dn), 1)
    return [uf, u2, dn]


def pair_split(x):
    hi = x.astype(BF16)
    lo = (x - hi.astype(F32)).astype(BF16)
    return hi, lo


def wide(x):
    return jnp.concatenate(pair_split(x), 1)


def folded(product, rows):
    return product[:rows, :128] + product[:rows, 128:] + product[rows:, :128] + product[rows:, 128:]


def dot(left, right):
    return jnp.dot(left, right, preferred_element_type=F32)


def kernel(
    count_x, count_y,
    off_hbm, charge_hbm, uf_hbm, u2_hbm, dn_hbm,
    out_ref,
    off_ref, charge_ref, flat, uf_ref, u2_ref, dn_ref,
    halo, moments, near_rows, rows, coarse, pieces, source, charge, target, sums, near,
    table, table3, right, right3, product, bq, leaf, bases,
    load_s, send_s, recv_s,
):
    loads = [
        pltpu.make_async_copy(src, dst, load_s.at[i])
        for i, (src, dst) in enumerate(
            [(off_hbm, off_ref), (charge_hbm, charge_ref)]
            + [(uf_hbm, uf_ref), (u2_hbm, u2_ref), (dn_hbm, dn_ref)]
        )
    ]
    for load in loads:
        load.start()
    at_rxy = 96
    at_z2 = at_rxy + 128
    at_w = at_z2 + 56
    at_l3 = at_w + 24
    ix = lax.axis_index("gx")
    iy = lax.axis_index("gy")
    lane = lax.broadcasted_iota(jnp.int32, (8, 128), 1)
    lane64 = lax.broadcasted_iota(jnp.int32, (64, 128), 1)
    row64 = lax.broadcasted_iota(jnp.int32, (64, 128), 0)
    eye = row64 == lane64 % 64
    sub = lax.broadcasted_iota(jnp.int32, (8, 128), 0)
    c = cubic()
    t = nodes()

    def pick(index, values):
        result = jnp.full(index.shape, float(values[3]), F32)
        for e in (2, 1, 0):
            result = jnp.where(index == e, float(values[e]), result)
        return result

    for i, index in enumerate((sub % 4, sub // 4, 2 + sub // 4)):
        for e in range(4):
            flat[32 * i + 8 * e : 32 * i + 8 * e + 8] = pick(index, c[e])
    flat[at_rxy : at_rxy + 64] = 0.5 * pick(row64 // 16, t)
    flat[at_rxy + 64 : at_rxy + 128] = 0.5 * pick(row64 // 4 % 4, t)
    gap_z = 0.5 * (pick(lane % 4, t) - pick(sub % 4, t))
    for i in range(7):
        gap = gap_z + (i - 3.0)
        flat[at_z2 + 8 * i : at_z2 + 8 * i + 8] = gap * gap
    for level, start, length in ((0, 0, 64), (1, 64, 16), (2, 80, 16)):
        z = lane % 16
        seen = z + (sub - 3) * 2**level
        odd = (z // 2**level) % 2
        ok = (z % 2**level == 0) & (seen >= 0) & (seen < 16) & (sub < 7)
        ok = ok & (lane >= start) & (lane < start + length)
        ok = ok & ((sub < 6) | (odd == 0)) & ((sub > 0) | (odd == 1))
        flat[at_w + 8 * level : at_w + 8 * level + 8] = jnp.where(ok, 0.5**level, 0.0)
    lane_x = 0.5 * pick(lane % 64 // 16, t)
    lane_y = 0.5 * pick(lane // 4 % 4, t)
    flat[at_l3 : at_l3 + 8] = jnp.where(sub == 0, lane_x, lane_y)

    def remote(src, dst, send, recv, dx, dy):
        device = (lax.rem(ix + dx + count_x, count_x), lax.rem(iy + dy + count_y, count_y))
        return pltpu.make_async_remote_copy(
            src_ref=src, dst_ref=dst, send_sem=send, recv_sem=recv,
            device_id=device, device_id_type=MESH,
        )

    barrier = pltpu.get_barrier_semaphore()

    def greet(dx, dy):
        device = (lax.rem(ix + dx + count_x, count_x), lax.rem(iy + dy + count_y, count_y))
        pl.semaphore_signal(barrier, inc=1, device_id=device, device_id_type=MESH)

    for ox, oy in DIRS:
        greet(ox, oy)

    for k in range(1, count_y):
        greet(0, k)
    for k in range(1, count_x):
        greet(k, 0)

    @pl.loop(0, TILES)
    def _(j):
        dx = [(2 * j + e) // 7 - 3 for e in range(2)]
        dy = [(2 * j + e) % 7 - 3 for e in range(2)]
        dx, dy = (jnp.where(lane < 64, v[0], v[1]).astype(F32) for v in (dx, dy))
        gap_x = (dx + lane_x)[:1] - flat[at_rxy : at_rxy + 64]
        gap_y = (dy + lane_y)[:1] - flat[at_rxy + 64 : at_rxy + 128]
        adjacent = jnp.maximum(jnp.abs(dx), jnp.abs(dy))[:1]
        adjacent = jnp.broadcast_to(adjacent, (64, 128)) <= 1.0
        plane = gap_x * gap_x + gap_y * gap_y
        at = pl.ds(pl.multiple_of(j * 128, 128), 128)
        for i in range(7):
            value = lax.rsqrt(plane + jnp.concatenate([flat[at_z2 + 8 * i : at_z2 + 8 * i + 8]] * 8, 0))
            if i in (2, 3, 4):
                value = jnp.where(adjacent, 0.0, value)
            hi, lo = pair_split(value)
            table[64 * i : 64 * i + 64, at] = hi
            table[448 + 64 * i : 512 + 64 * i, at] = lo

    @pl.loop(0, count_x // 4)
    def _(j):
        apart = (j - ix // 4).astype(F32)
        side = (lane64 // 64 - iy // 4).astype(F32)
        gap_x = apart + flat[at_l3 : at_l3 + 1] - flat[at_rxy : at_rxy + 64]
        gap_y = side + flat[at_l3 + 1 : at_l3 + 2] - flat[at_rxy + 64 : at_rxy + 128]
        adjacent = jnp.maximum(jnp.abs(side), jnp.abs(apart)) <= 1.0
        plane = gap_x * gap_x + gap_y * gap_y
        at = pl.ds(pl.multiple_of(j * 128, 128), 128)
        for i in range(3):
            value = lax.rsqrt(plane + jnp.concatenate([flat[at_z2 + 8 * i + 16 : at_z2 + 8 * i + 24]] * 8, 0))
            value = jnp.where(adjacent, 0.0, value)
            hi, lo = pair_split(value)
            table3[64 * i : 64 * i + 64, at] = hi
            table3[192 + 64 * i : 256 + 64 * i, at] = lo

    def basis(column, k):
        x = 2.0 * halo[column, 0, k : k + 1, :] - 1.0
        y = 2.0 * halo[column, 1, k : k + 1, :] - 1.0
        z = 2.0 * halo[column, 2, k : k + 1, :] - 1.0

        def poly(i, u):
            p = [flat[32 * i + 8 * e : 32 * i + 8 * e + 8] for e in range(4)]
            return ((p[3] * u + p[2]) * u + p[1]) * u + p[0]

        along_z = poly(0, z)
        low, high = poly(1, y) * along_z, poly(2, y) * along_z
        pieces = []
        for a in range(4):
            s = ((float(c[3, a]) * x + float(c[2, a])) * x + float(c[1, a])) * x + float(c[0, a])
            pieces += [s * low, s * high]
        return jnp.concatenate(pieces, 0)

    def column_of(cx, cy):
        return (1 + cx) * 4 + 1 + cy

    for load in loads[:2]:
        load.wait()
    for cx in range(2):
        for cy in range(2):
            for k in range(8):
                at = slice(128 * k, 128 * k + 128)
                for comp in range(3):
                    halo[column_of(cx, cy), comp, k : k + 1] = off_ref[comp, cx, cy : cy + 1, at]
                halo[column_of(cx, cy), 3, k : k + 1] = charge_ref[cx, cy : cy + 1, at]
    half_row = lax.broadcasted_iota(jnp.int32, (128, 128), 0) // 64
    half_lane = lax.broadcasted_iota(jnp.int32, (128, 128), 1)
    parity = (half_row == half_lane % 2).astype(F32).astype(BF16)
    halves = (half_row == half_lane // 64).astype(F32).astype(BF16)
    leaf[...] = jnp.zeros((64, 128), F32)

    @pl.loop(0, 4, unroll=True)
    def _(col):
        column = (1 + col // 2) * 4 + 1 + col % 2
        for k in range(8):
            value = basis(column, k)
            bases[8 * col + k] = value
            value = value * halo[column, 3, k : k + 1, :]
            hi, lo = pair_split(value)
            bq[col, 64 * k : 64 * k + 64] = hi
            bq[col, 512 + 64 * k : 576 + 64 * k] = lo
        summed = dot(bq[col], parity)
        total = leaf[...]
        for k in range(8):
            here = (lane64 % 64) // 2 == col * 8 + k
            total = jnp.where(
                here,
                summed[64 * k : 64 * k + 64] + summed[512 + 64 * k : 576 + 64 * k],
                total,
            )
        leaf[...] = total

    for load in loads[2:]:
        load.wait()
    own = leaf[...]
    moments[4] = jnp.where(lane64[:32] < 64, own[:32], own[32:])
    stacked = jnp.concatenate(
        [own] + [pltpu.roll(own, 128 - 16 * col, 1) for col in range(1, 4)], 0
    )
    first = folded(dot(uf_ref[...], wide(stacked)), 128)
    first = first[:64] + pltpu.roll(first[64:], 127, 1)
    first = jnp.where((lane64 < 16) & (lane64 % 2 == 0), first, 0.0)
    first = first[:32] + pltpu.roll(first[32:], 1, 1)
    near_rows[iy] = pltpu.roll(first, 16 * iy, 1)

    pl.semaphore_wait(barrier, len(DIRS) + count_y - 1 + count_x - 1)

    ROW, HALO, LEAF, LINE, COARSE = range(5)
    buffers = (near_rows, halo, moments, rows, coarse)
    counts = (count_y - 1, 12, 8, 6, count_x - 1)

    def send(kind, index, at, dx, dy):
        buffer = buffers[kind]
        sems = (send_s.at[kind], recv_s.at[kind])
        remote(buffer.at[index], buffer.at[at], *sems, dx, dy).start()

    def all_of(kind):
        part = buffers[kind].at[pl.ds(0, counts[kind])]
        return remote(part, part, send_s.at[kind], recv_s.at[kind], 1, 1)

    for k in range(1, count_y):
        send(ROW, iy, iy, 0, k)
    for ox, oy in DIRS:
        take_x = {1: [2], -1: [1], 0: [1, 2]}[ox]
        put_x = {1: [0], -1: [3], 0: [1, 2]}[ox]
        take_y = {1: (2, 1), -1: (1, 1), 0: (1, 2)}[oy]
        put_y = {1: 0, -1: 3, 0: 1}[oy]
        for a, b in zip(take_x, put_x):
            at = (pl.ds(a * 4 + take_y[0], take_y[1]), pl.ds(b * 4 + put_y, take_y[1]))
            send(HALO, *at, ox, oy)
    for ox, oy in DIRS:
        send(LEAF, 4, (1 - ox) * 3 + 1 - oy, ox, oy)

    all_of(ROW).wait_recv()
    row = near_rows[0]
    for k in range(1, count_y):
        row = row + near_rows[k]
    rows[ix] = row
    full = jnp.concatenate([row, pltpu.roll(row, 127, 1)], 0)
    full = jnp.where(lane64 % 2 == 0, full, 0.0)

    def part(source, which, step_z, step_y):
        o = folded(dot(u2_ref[which], wide(source)), 256)
        return (
            o[:64]
            + pltpu.roll(o[64:128], 128 - step_z, 1)
            + pltpu.roll(o[128:192], 128 - step_y, 1)
            + pltpu.roll(o[192:], 128 - step_z - step_y, 1)
        )

    second = part(full, ix % 2, 2, 16)
    second = jnp.where((lane64 // 16 % 2 == 0) & (lane64 % 4 == 0), second, 0.0)
    third = part(second, ix // 2 % 2, 4, 32)
    third = jnp.where((lane64 // 16 % 4 == 0) & (lane64 % 8 == 0), third, 0.0)
    packed = second[:16] + pltpu.roll(third[:16], 16, 1)
    for g in range(1, 4):
        at = slice(16 * g, 16 * g + 16)
        packed = packed + pltpu.roll(second[at], g, 1) + pltpu.roll(third[at], 16 + g, 1)
    coarse[ix] = packed

    for k in range(1, count_x):
        send(COARSE, ix, ix, k, 0)
    for dx in ROWS:
        send(LINE, ix, ix, dx, 0)

    first_term = (sub == 0) | (sub == 1) | (sub == 3)
    second_term = (sub == 2) | (sub == 4)
    half = (lane // 64).astype(F32)

    def three(value):
        a = value.astype(BF16).astype(F32)
        rest = value - a
        b = rest.astype(BF16).astype(F32)
        return [a, b, rest - b]

    def features(column, wx, wy, both):
        x = halo[column, 0] + (wx - 1.0)
        y = halo[column, 1] + (wy - 1.0)
        z = halo[column, 2] + (half - 1.0)
        plane = x * x + y * y
        parts = three(x) + three(y) + three(z) + three(plane + z * z)
        if both:
            beside = z + (2.0 - 4.0 * half)
            parts += three(beside) + three(plane + beside * beside)
        for i, part in enumerate(parts):
            pieces[column, i] = part

    def spread(column, i, k):
        return jnp.broadcast_to(pieces[column, i, k : k + 1], (8, 128))

    def chosen(column, i, k, six, seven, terms):
        a, b, c = (spread(column, i + e, k) for e in range(3))
        value = jnp.where(terms[0], a, jnp.where(terms[1], b, c))
        return jnp.where(sub == 6, six, jnp.where(sub == 7, seven, value))

    zero8 = jnp.zeros((8, 128), F32)
    one8 = jnp.ones((8, 128), F32)
    t_terms = ((sub == 0) | (sub == 2) | (sub == 5), (sub == 1) | (sub == 4))
    s_terms = (first_term, second_term)
    scale8 = jnp.where(sub < 6, -2.0, 1.0)

    @pl.loop(0, 4, unroll=True)
    def _(col):
        cx, cy = col // 2, col % 2
        column = (1 + cx) * 4 + 1 + cy
        features(column, cx.astype(F32), cy.astype(F32), False)
        for k in range(0, 8, 2):
            turned = []
            for e in (k, k + 1):
                tiles = [
                    chosen(column, 0, e, one8, one8, t_terms),
                    chosen(column, 3, e, one8, spread(column, 9, e), t_terms),
                    chosen(column, 6, e, spread(column, 10, e), spread(column, 11, e), t_terms),
                ]
                tiles = jnp.concatenate([t * scale8 for t in tiles] + [zero8], 0)
                turned.append((tiles, pltpu.roll(tiles, 64, 1)))
            lane32 = lane64[:32] < 64
            upper = jnp.where(lane32, turned[0][0], turned[1][1])
            lower = jnp.where(lane32, turned[0][1], turned[1][0])
            stack = jnp.concatenate([upper, lower], 0).T.astype(BF16)
            target[col * 8 + k] = stack[:64]
            target[col * 8 + k + 1] = stack[64:]

    all_of(HALO).wait_recv()

    outside = jnp.where(lax.broadcasted_iota(jnp.int32, (32, 128), 0) == 6, 16384.0, 0.0)
    lane32 = lane64[:32] < 64
    left_half = lane32
    outside_low = jnp.where(left_half, outside, 0.0).astype(BF16)
    outside_high = jnp.where(left_half, 0.0, outside).astype(BF16)

    @pl.loop(0, 16, unroll=4)
    def _(column):
        wx, wy = column // 4, column % 4
        features(column, wx.astype(F32) - 1.0, wy.astype(F32) - 1.0, True)
        at_x, at_y = 2 * ix + wx - 1, 2 * iy + wy - 1
        inside = (at_x >= 0) & (at_x < 2 * count_x) & (at_y >= 0) & (at_y < 2 * count_y)
        q = halo[column, 3] * inside.astype(F32)
        after = jnp.where(sub == 7, 0.0, pltpu.roll(q, 7, 0))
        before = jnp.where(sub == 0, 0.0, pltpu.roll(q, 1, 0))
        charge[column, 0] = jnp.where(lane < 64, q, before)
        charge[column, 1] = q
        charge[column, 2] = jnp.where(lane < 64, after, q)
        source[column, 9, 2] = outside_low
        source[column, 0, 3] = outside_high
        for k in range(8):
            own_tiles = [
                chosen(column, 0, k, spread(column, 9, k), spread(column, 10, k), s_terms),
                chosen(column, 3, k, spread(column, 11, k), one8, s_terms),
                chosen(column, 6, k, one8, one8, s_terms),
                zero8,
            ]
            beside_tiles = [
                jnp.where(sub == 6, spread(column, 15, k), jnp.where(sub == 7, spread(column, 16, k), own_tiles[0])),
                jnp.where(sub == 6, spread(column, 17, k), own_tiles[1]),
                chosen(column, 12, k, one8, one8, s_terms),
                zero8,
            ]
            for e, tiles in enumerate((own_tiles, beside_tiles)):
                tiles = jnp.concatenate(tiles, 0)
                source[column, k + 1, 2 * e] = jnp.where(left_half, tiles, 0.0).astype(BF16)
                source[column, k + 1, 2 * e + 1] = jnp.where(left_half, 0.0, tiles).astype(BF16)

    def near_block(block, carry):
        col, k = block // 8, block % 8
        cx, cy = col // 2, col % 2
        mine = target[block]
        straight = jnp.zeros((64, 128), F32)
        crossed = jnp.zeros((64, 128), F32)
        columns = [(cx + dx) * 4 + cy + dy for dx in range(3) for dy in range(3)]

        def side(column, a, b):
            return jnp.concatenate([source[column, a[0], a[1]], source[column, b[0], b[1]]], 0)

        def row_of(column, dz):
            return charge[column, dz, pl.ds(k, 1), :]

        for column in columns:
            above = side(column, (k + 1, 1), (k + 2, 2))
            below = side(column, (k, 3), (k + 1, 0))
            inverse = lax.rsqrt(dot(mine, jnp.concatenate([above, below], 1)))
            crossed = crossed + inverse[:, :128] * row_of(column, 2)
            crossed = crossed + inverse[:, 128:] * row_of(column, 0)
        for i in range(0, 9, 2):
            group = columns[i : i + 2]
            both = [side(column, (k + 1, 0), (k + 1, 1)) for column in group]
            inverse = lax.rsqrt(dot(mine, jnp.concatenate(both, 1)))
            for e, column in enumerate(group):
                value = inverse[:, 128 * e : 128 * e + 128]
                if i + e == 4:
                    value = jnp.where(eye, 0.0, value)
                straight = straight + value * row_of(column, 1)
        sums[block] = straight + pltpu.roll(crossed, 64, 1)
        return carry

    lax.fori_loop(0, 32, near_block, 0, unroll=8)

    @pl.loop(0, 4, unroll=True)
    def _(col):
        value = sums[pl.ds(pl.multiple_of(col * 8, 8), 8)].reshape(512, 128)
        hi, lo = pair_split(value)
        value = dot(hi, halves) + dot(lo, halves)
        for k in range(8):
            mine = jnp.where(eye, value[64 * k : 64 * k + 64], 0.0)
            near[col, k : k + 1] = jnp.sum(mine, 0, keepdims=True)

    for kind in (LEAF, LINE, COARSE):
        all_of(kind).wait_recv()

    def unpacked(value, start):
        return jnp.concatenate(
            [pltpu.roll(value, lax.rem(start - g + 128, 128), 1) for g in range(4)], 0
        )

    for j in range(count_x // 4):
        group = coarse[4 * j] + coarse[4 * j + 1] + coarse[4 * j + 2] + coarse[4 * j + 3]
        third = unpacked(group, jnp.int32(112))
        right3[128 * j : 128 * j + 64] = wide(third)
        right3[128 * j + 64 : 128 * j + 128] = wide(pltpu.roll(third, 64, 1))
    o = folded(dot(table3[...], right3[...]), 192)
    local = o[64:128]
    local = local + jnp.where(lane64 == 0, pltpu.roll(o[128:], 120, 1), 0.0)
    local = local + jnp.where(lane64 == 8, pltpu.roll(o[:64], 8, 1), 0.0)
    local3 = jnp.where((lane64 < 16) & (lane64 % 8 == 0), 0.125 * local, 0.0)

    plain, crossed = {}, {}
    for ox in (-1, 0, 1):
        for oy in (-1, 0, 1):
            value = moments[(ox + 1) * 3 + oy + 1]
            turned = pltpu.roll(value, 64, 1)
            lane32 = lane64[:32]
            value = jnp.concatenate(
                [jnp.where(lane32 < 64, value, turned), jnp.where(lane32 < 64, turned, value)], 0
            )
            scale = F32(1.0)
            if ox:
                scale = scale * (ix > 0 if ox < 0 else ix < count_x - 1).astype(F32)
            if oy:
                scale = scale * (iy > 0 if oy < 0 else iy < count_y - 1).astype(F32)
            plain[ox, oy] = value * scale
    by_x = lane64 // 32 % 2
    by_y = lane64 // 16 % 2

    def swap_y(value):
        return jnp.where(by_y == 0, pltpu.roll(value, 112, 1), pltpu.roll(value, 16, 1))

    def leaf_block(dx, dy):
        result = None
        for cx in range(2):
            for cy in range(2):
                ox, oy = (cx + dx) // 2, (cy + dy) // 2
                if abs(ox) > 1 or abs(oy) > 1:
                    continue
                value = plain[ox, oy]
                if dy % 2:
                    value = swap_y(value)
                if dx % 2:
                    value = pltpu.roll(value, 32, 1)
                mine = (by_x == cx) & (by_y == cy)
                value = jnp.where(mine, value, 0.0)
                result = value if result is None else result + value
        return result

    def within(value, count, step, odd):
        ok = (value >= 0) & (value < count)
        if step == 3:
            ok = ok & (odd == 0)
        if step == -3:
            ok = ok & (odd == 1)
        return ok.astype(F32)

    for dx in range(-3, 4):
        line = rows[lax.rem(ix + dx + count_x, count_x)]
        line = jnp.concatenate([line, pltpu.roll(line, 127, 1)], 0)
        line = pltpu.roll(line, lax.rem(64 - 16 * iy + 128, 128), 1)
        line = line * within(ix + dx, count_x, dx, ix % 2)
        x2 = ix // 2 + dx
        base = lax.rem(2 * x2 + 2 * count_x, count_x)
        pair = unpacked(coarse[base] + coarse[base + 1], lax.rem(80 - 32 * (iy // 2) + 128, 128))
        pair = pair * within(x2, count_x // 2, dx, ix // 2 % 2)
        for dy in range(-3, 4):
            one = pltpu.roll(line, (-16 * dy) % 128, 1) * within(iy + dy, count_y, dy, iy % 2)
            two = pltpu.roll(pair, (-32 * dy) % 128, 1)
            two = two * within(iy // 2 + dy, count_y // 2, dy, iy // 2 % 2)
            value = jnp.where(lane64 < 64, leaf_block(dx, dy), jnp.where(lane64 < 80, one, two))
            value = jnp.where(lane64 < 96, value, 0.0)
            at = ((dx + 3) * 7 + dy + 3) * 64
            right[at : at + 64] = wide(value)
    right[49 * 64 : 50 * 64] = jnp.zeros((64, 256), BF16)

    product[...] = dot(table[...], right[...])

    far = jnp.zeros((64, 128), F32)
    for i in range(7):
        dz = i - 3
        o = product[64 * i : 64 * i + 64]
        o2 = product[448 + 64 * i : 512 + 64 * i]
        o = o[:, :128] + o[:, 128:] + o2[:, :128] + o2[:, 128:]
        for level in range(3):
            value = o if dz == 0 else pltpu.roll(o, (-dz * 2**level) % 128, 1)
            far = far + value * flat[at_w + 8 * level + i : at_w + 8 * level + i + 1]

    def down(source, which, step):
        o = folded(dot(dn_ref[which], wide(source)), 128)
        return jnp.where(lane64 % (2 * step) == 0, o[:64], pltpu.roll(o[64:], step, 1))

    low = lane64 < 16
    local2 = down(local3, ix // 2 % 2 * 2 + iy // 2 % 2, 4) + pltpu.roll(far, 48, 1)
    local2 = jnp.where(low & (lane64 % 4 == 0), local2, 0.0)
    local1 = down(local2, ix % 2 * 2 + iy % 2, 2) + pltpu.roll(far, 64, 1)
    local1 = jnp.where(low & (lane64 % 2 == 0), local1, 0.0)
    local0 = far
    for col in range(4):
        value = down(local1, col, 1)
        if col:
            value = pltpu.roll(value, 16 * col, 1)
        local0 = local0 + jnp.where(lane64 // 16 == col, value, 0.0)
    leaf[...] = local0

    @pl.loop(0, 4, unroll=True)
    def _(col):
        column = (1 + col // 2) * 4 + 1 + col % 2
        here = pltpu.roll(leaf[...], lax.rem(128 - 16 * col, 128), 1)
        for k in range(8):
            spread = jnp.where(
                lane64 < 64,
                jnp.broadcast_to(here[:, 2 * k : 2 * k + 1], (64, 128)),
                jnp.broadcast_to(here[:, 2 * k + 1 : 2 * k + 2], (64, 128)),
            )
            both = bases[8 * col + k] * spread
            near[col, k : k + 1] = jnp.sum(both, 0, keepdims=True) + near[col, k : k + 1]

    for col in range(4):
        for k in range(8):
            at = slice(128 * k, 128 * k + 128)
            out_ref[col // 2, col % 2 : col % 2 + 1, at] = near[col, k : k + 1]

    for kind in range(5):
        all_of(kind).wait_send()


def solution(mesh):
    count_x, count_y = mesh.shape["gx"], mesh.shape["gy"]
    fixed = constants()
    vmem = pl.BlockSpec(memory_space=pltpu.VMEM)
    hbm = pl.BlockSpec(memory_space=pltpu.HBM)
    dma = pltpu.SemaphoreType.DMA
    call = pl.pallas_call(
        functools.partial(kernel, count_x, count_y),
        out_shape=jax.ShapeDtypeStruct((2, 2, 1024), F32),
        in_specs=[hbm] * (2 + len(fixed)),
        out_specs=vmem,
        scratch_shapes=[
            pltpu.VMEM((3, 2, 2, 1024), F32),
            pltpu.VMEM((2, 2, 1024), F32),
            pltpu.VMEM((96 + 128 + 56 + 24 + 8, 128), F32),
            pltpu.VMEM(fixed[0].shape, BF16),
            pltpu.VMEM(fixed[1].shape, BF16),
            pltpu.VMEM(fixed[2].shape, BF16),
            pltpu.VMEM((16, 4, 8, 128), F32),
            pltpu.VMEM((9, 32, 128), F32),
            pltpu.VMEM((count_y, 32, 128), F32),
            pltpu.VMEM((count_x, 32, 128), F32),
            pltpu.VMEM((count_x, 16, 128), F32),
            pltpu.VMEM((16, 18, 8, 128), F32),
            pltpu.VMEM((16, 10, 4, 32, 128), BF16),
            pltpu.VMEM((16, 3, 8, 128), F32),
            pltpu.VMEM((32, 64, 64), BF16),
            pltpu.VMEM((32, 64, 128), F32),
            pltpu.VMEM((4, 8, 128), F32),
            pltpu.VMEM((896, TILES * 128), BF16),
            pltpu.VMEM((384, count_x // 4 * 128), BF16),
            pltpu.VMEM((TILES * 128, 256), BF16),
            pltpu.VMEM((count_x // 4 * 128, 256), BF16),
            pltpu.VMEM((896, 256), F32),
            pltpu.VMEM((4, 1024, 128), BF16),
            pltpu.VMEM((64, 128), F32),
            pltpu.VMEM((32, 64, 128), F32),
            dma((5,)),
            dma((5,)),
            dma((5,)),
        ],
        compiler_params=pltpu.CompilerParams(
            collective_id=0, has_side_effects=True, vmem_limit_bytes=64 << 20
        ),
    )

    def body(offsets, charges):
        return call(offsets, charges, *fixed)

    in_specs = (P(None, "gx", "gy", None), P("gx", "gy", None))
    out_specs = P("gx", "gy", None)
    return jax.shard_map(body, mesh=mesh, in_specs=in_specs, out_specs=out_specs, check_vma=False)
```

```python
import functools

import jax
import jax.numpy as jnp
import ml_dtypes
import numpy as np
from jax import lax
from jax.experimental import pallas as pl
from jax.experimental.pallas import tpu as pltpu
from jax.sharding import PartitionSpec as P

MESH = pl.DeviceIdType.MESH
F32 = jnp.float32
BF16 = jnp.bfloat16
DIRS = [(ox, oy) for ox in (-1, 0, 1) for oy in (-1, 0, 1) if (ox, oy) != (0, 0)]
ROWS = (1, 2, 3, -1, -2, -3)
WIDER = (1, 2, 3, 4, 5, 6, 7, -1, -2, -3, -4, -5, -6, -7)
TILES = 25


def nodes():
    return np.cos((2.0 * np.arange(4) + 1.0) * np.pi / 8.0)


def cubic():
    t = nodes()
    t2, t3 = 2 * t * t - 1, 4 * t**3 - 3 * t
    return np.stack([0.25 - 0.5 * t2, 0.5 * t - 1.5 * t3, t2, 2 * t3])


def split(x):
    hi = x.astype(ml_dtypes.bfloat16)
    lo = (x - hi.astype(np.float64)).astype(ml_dtypes.bfloat16)
    return hi, lo


def constants():
    t = nodes()
    c = cubic()
    shifted = (t[None, :] + 2.0 * np.arange(2)[:, None] - 1.0) / 2.0
    f = sum(c[k][None, None, :] * shifted[:, :, None] ** k for k in range(4))
    up = np.einsum("xia,yjb,zkc->xyzijkabc", f, f, f).reshape(2, 2, 2, 64, 64)
    uf = up.transpose(2, 4, 0, 1, 3).reshape(128, 256)
    uf = np.concatenate(split(uf), 0)
    u2 = up.transpose(0, 1, 2, 4, 3).reshape(2, 256, 64)
    u2 = np.concatenate(split(u2), 1)
    dn = up.reshape(4, 128, 64)
    dn = np.concatenate(split(dn), 1)
    return [uf, u2, dn]


def pair_split(x):
    hi = x.astype(BF16)
    lo = (x - hi.astype(F32)).astype(BF16)
    return hi, lo


def wide(x):
    return jnp.concatenate(pair_split(x), 1)


def folded(product, rows):
    return product[:rows, :128] + product[:rows, 128:] + product[rows:, :128] + product[rows:, 128:]


def dot(left, right):
    return jnp.dot(left, right, preferred_element_type=F32)


def kernel(
    count_x, count_y,
    off_hbm, charge_hbm, uf_hbm, u2_hbm, dn_hbm,
    out_ref,
    off_ref, charge_ref, flat, uf_ref, u2_ref, dn_ref,
    halo, moments, near_rows, rows, seconds, thirds, pieces, source, charge, target, sums, near,
    table, table3, right, right3, product, bq, leaf, bases,
    load_s, send_s, recv_s,
):
    loads = [
        pltpu.make_async_copy(src, dst, load_s.at[i])
        for i, (src, dst) in enumerate(
            [(off_hbm, off_ref), (charge_hbm, charge_ref)]
            + [(uf_hbm, uf_ref), (u2_hbm, u2_ref), (dn_hbm, dn_ref)]
        )
    ]
    for load in loads:
        load.start()
    at_rxy = 96
    at_z2 = at_rxy + 128
    at_w = at_z2 + 56
    at_l3 = at_w + 24
    ix = lax.axis_index("gx")
    iy = lax.axis_index("gy")
    lane = lax.broadcasted_iota(jnp.int32, (8, 128), 1)
    lane64 = lax.broadcasted_iota(jnp.int32, (64, 128), 1)
    row64 = lax.broadcasted_iota(jnp.int32, (64, 128), 0)
    eye = row64 == lane64 % 64
    sub = lax.broadcasted_iota(jnp.int32, (8, 128), 0)
    c = cubic()
    t = nodes()

    def pick(index, values):
        result = jnp.full(index.shape, float(values[3]), F32)
        for e in (2, 1, 0):
            result = jnp.where(index == e, float(values[e]), result)
        return result

    for i, index in enumerate((sub % 4, sub // 4, 2 + sub // 4)):
        for e in range(4):
            flat[32 * i + 8 * e : 32 * i + 8 * e + 8] = pick(index, c[e])
    flat[at_rxy : at_rxy + 64] = 0.5 * pick(row64 // 16, t)
    flat[at_rxy + 64 : at_rxy + 128] = 0.5 * pick(row64 // 4 % 4, t)
    gap_z = 0.5 * (pick(lane % 4, t) - pick(sub % 4, t))
    for i in range(7):
        gap = gap_z + (i - 3.0)
        flat[at_z2 + 8 * i : at_z2 + 8 * i + 8] = gap * gap
    for level, start, length in ((0, 0, 64), (1, 64, 16), (2, 80, 16)):
        z = lane % 16
        seen = z + (sub - 3) * 2**level
        odd = (z // 2**level) % 2
        ok = (z % 2**level == 0) & (seen >= 0) & (seen < 16) & (sub < 7)
        ok = ok & (lane >= start) & (lane < start + length)
        ok = ok & ((sub < 6) | (odd == 0)) & ((sub > 0) | (odd == 1))
        flat[at_w + 8 * level : at_w + 8 * level + 8] = jnp.where(ok, 0.5**level, 0.0)
    lane_x = 0.5 * pick(lane % 64 // 16, t)
    lane_y = 0.5 * pick(lane // 4 % 4, t)
    flat[at_l3 : at_l3 + 8] = jnp.where(sub == 0, lane_x, lane_y)

    def remote(src, dst, send, recv, dx, dy):
        device = (lax.rem(ix + dx + count_x, count_x), lax.rem(iy + dy + count_y, count_y))
        return pltpu.make_async_remote_copy(
            src_ref=src, dst_ref=dst, send_sem=send, recv_sem=recv,
            device_id=device, device_id_type=MESH,
        )

    barrier = pltpu.get_barrier_semaphore()

    def greet(dx, dy):
        device = (lax.rem(ix + dx + count_x, count_x), lax.rem(iy + dy + count_y, count_y))
        pl.semaphore_signal(barrier, inc=1, device_id=device, device_id_type=MESH)

    for ox, oy in DIRS:
        greet(ox, oy)

    for k in range(1, count_y):
        greet(0, k)
    for k in range(1, count_x):
        greet(k, 0)

    def table_tile(j):
        dx = [(2 * j + e) // 7 - 3 for e in range(2)]
        dy = [(2 * j + e) % 7 - 3 for e in range(2)]
        dx, dy = (jnp.where(lane < 64, v[0], v[1]).astype(F32) for v in (dx, dy))
        gap_x = (dx + lane_x)[:1] - flat[at_rxy : at_rxy + 64]
        gap_y = (dy + lane_y)[:1] - flat[at_rxy + 64 : at_rxy + 128]
        adjacent = jnp.maximum(jnp.abs(dx), jnp.abs(dy))[:1]
        adjacent = jnp.broadcast_to(adjacent, (64, 128)) <= 1.0
        plane = gap_x * gap_x + gap_y * gap_y
        at = pl.ds(pl.multiple_of(j * 128, 128), 128)
        for i in range(7):
            value = lax.rsqrt(plane + jnp.concatenate([flat[at_z2 + 8 * i : at_z2 + 8 * i + 8]] * 8, 0))
            if i in (2, 3, 4):
                value = jnp.where(adjacent, 0.0, value)
            hi, lo = pair_split(value)
            table[64 * i : 64 * i + 64, at] = hi
            table[448 + 64 * i : 512 + 64 * i, at] = lo

    @pl.loop(0, count_x // 4)
    def _(j):
        apart = (j - ix // 4).astype(F32)
        side = (lane64 // 64 - iy // 4).astype(F32)
        gap_x = apart + flat[at_l3 : at_l3 + 1] - flat[at_rxy : at_rxy + 64]
        gap_y = side + flat[at_l3 + 1 : at_l3 + 2] - flat[at_rxy + 64 : at_rxy + 128]
        adjacent = jnp.maximum(jnp.abs(side), jnp.abs(apart)) <= 1.0
        plane = gap_x * gap_x + gap_y * gap_y
        at = pl.ds(pl.multiple_of(j * 128, 128), 128)
        for i in range(3):
            value = lax.rsqrt(plane + jnp.concatenate([flat[at_z2 + 8 * i + 16 : at_z2 + 8 * i + 24]] * 8, 0))
            value = jnp.where(adjacent, 0.0, value)
            hi, lo = pair_split(value)
            table3[64 * i : 64 * i + 64, at] = hi
            table3[192 + 64 * i : 256 + 64 * i, at] = lo

    pl.loop(0, 8)(table_tile)

    def basis(column, k):
        x = 2.0 * halo[column, 0, k : k + 1, :] - 1.0
        y = 2.0 * halo[column, 1, k : k + 1, :] - 1.0
        z = 2.0 * halo[column, 2, k : k + 1, :] - 1.0

        def poly(i, u):
            p = [flat[32 * i + 8 * e : 32 * i + 8 * e + 8] for e in range(4)]
            return ((p[3] * u + p[2]) * u + p[1]) * u + p[0]

        along_z = poly(0, z)
        low, high = poly(1, y) * along_z, poly(2, y) * along_z
        pieces = []
        for a in range(4):
            s = ((float(c[3, a]) * x + float(c[2, a])) * x + float(c[1, a])) * x + float(c[0, a])
            pieces += [s * low, s * high]
        return jnp.concatenate(pieces, 0)

    def column_of(cx, cy):
        return (1 + cx) * 4 + 1 + cy

    for load in loads[:2]:
        load.wait()
    for cx in range(2):
        for cy in range(2):
            for k in range(8):
                at = slice(128 * k, 128 * k + 128)
                for comp in range(3):
                    halo[column_of(cx, cy), comp, k : k + 1] = off_ref[comp, cx, cy : cy + 1, at]
                halo[column_of(cx, cy), 3, k : k + 1] = charge_ref[cx, cy : cy + 1, at]
    ROW, HALO, LEAF, LINE, SECOND, THIRD = range(6)
    buffers = (near_rows, halo, moments, rows, seconds, thirds)
    counts = (count_y - 1, 12, 8, 6, len(WIDER), count_x - 1)

    def send(kind, index, at, dx, dy):
        buffer = buffers[kind]
        sems = (send_s.at[kind], recv_s.at[kind])
        remote(buffer.at[index], buffer.at[at], *sems, dx, dy).start()

    def all_of(kind):
        part = buffers[kind].at[pl.ds(0, counts[kind])]
        return remote(part, part, send_s.at[kind], recv_s.at[kind], 1, 1)

    pl.semaphore_wait(barrier, len(DIRS) + count_y - 1 + count_x - 1)
    for ox, oy in DIRS:
        take_x = {1: [2], -1: [1], 0: [1, 2]}[ox]
        put_x = {1: [0], -1: [3], 0: [1, 2]}[ox]
        take_y = {1: (2, 1), -1: (1, 1), 0: (1, 2)}[oy]
        put_y = {1: 0, -1: 3, 0: 1}[oy]
        for a, b in zip(take_x, put_x):
            at = (pl.ds(a * 4 + take_y[0], take_y[1]), pl.ds(b * 4 + put_y, take_y[1]))
            send(HALO, *at, ox, oy)
    half_row = lax.broadcasted_iota(jnp.int32, (128, 128), 0) // 64
    half_lane = lax.broadcasted_iota(jnp.int32, (128, 128), 1)
    parity = (half_row == half_lane % 2).astype(F32).astype(BF16)
    halves = (half_row == half_lane // 64).astype(F32).astype(BF16)
    leaf[...] = jnp.zeros((64, 128), F32)

    @pl.loop(0, 4, unroll=True)
    def _(col):
        column = (1 + col // 2) * 4 + 1 + col % 2
        for k in range(8):
            value = basis(column, k)
            bases[8 * col + k] = value
            value = value * halo[column, 3, k : k + 1, :]
            hi, lo = pair_split(value)
            bq[col, 64 * k : 64 * k + 64] = hi
            bq[col, 512 + 64 * k : 576 + 64 * k] = lo
        summed = dot(bq[col], parity)
        total = leaf[...]
        for k in range(8):
            here = (lane64 % 64) // 2 == col * 8 + k
            total = jnp.where(
                here,
                summed[64 * k : 64 * k + 64] + summed[512 + 64 * k : 576 + 64 * k],
                total,
            )
        leaf[...] = total

    for load in loads[2:]:
        load.wait()
    own = leaf[...]
    moments[4] = jnp.where(lane64[:32] < 64, own[:32], own[32:])
    stacked = jnp.concatenate(
        [own] + [pltpu.roll(own, 128 - 16 * col, 1) for col in range(1, 4)], 0
    )
    first = folded(dot(uf_ref[...], wide(stacked)), 128)
    first = first[:64] + pltpu.roll(first[64:], 127, 1)
    first = jnp.where((lane64 < 16) & (lane64 % 2 == 0), first, 0.0)
    packet = first[:8]
    for g in range(1, 8):
        packet = packet + pltpu.roll(first[8 * g : 8 * g + 8], 16 * g, 1)
    near_rows[iy] = packet

    for k in range(1, count_y):
        send(ROW, iy, iy, 0, k)
    for ox, oy in DIRS:
        send(LEAF, 4, (1 - ox) * 3 + 1 - oy, ox, oy)

    pl.loop(8, TILES)(table_tile)

    all_of(ROW).wait_recv()
    packets = [near_rows[k] for k in range(count_y)]
    full = []
    for g in range(8):
        tile = jnp.zeros((8, 128), F32)
        for k in range(count_y):
            moved = pltpu.roll(packets[k], 16 * (k - g) % 128, 1) if k != g else packets[k]
            tile = jnp.where(lane // 16 == k, moved, tile)
        full.append(tile)
    full = jnp.concatenate(full, 0)
    rows[ix] = full[:32] + pltpu.roll(full[32:], 1, 1)

    def part(source, which, step_z, step_y):
        o = folded(dot(u2_ref[which], wide(source)), 256)
        return (
            o[:64]
            + pltpu.roll(o[64:128], 128 - step_z, 1)
            + pltpu.roll(o[128:192], 128 - step_y, 1)
            + pltpu.roll(o[192:], 128 - step_z - step_y, 1)
        )

    second = part(full, ix % 2, 2, 16)
    second = jnp.where((lane64 // 16 % 2 == 0) & (lane64 % 4 == 0), second, 0.0)
    third = part(second, ix // 2 % 2, 4, 32)
    third = jnp.where((lane64 // 16 % 4 == 0) & (lane64 % 8 == 0), third, 0.0)
    packed = second[:8]
    for g in range(1, 8):
        packed = packed + pltpu.roll(second[8 * g : 8 * g + 8], g % 4 + 16 * (g // 4), 1)
    seconds[ix] = packed
    packed = third[:8]
    for g in range(1, 8):
        packed = packed + pltpu.roll(third[8 * g : 8 * g + 8], g, 1)
    pair = packed[:2]
    for e in range(1, 4):
        pair = pair + pltpu.roll(packed[2 * e : 2 * e + 2], 16 * e, 1)
    thirds[ix] = pair

    for dx in ROWS:
        send(LINE, ix, ix, dx, 0)
    for dx in WIDER:
        send(SECOND, ix, ix, dx, 0)
    for k in range(1, count_x):
        send(THIRD, ix, ix, k, 0)

    first_term = (sub == 0) | (sub == 1) | (sub == 3)
    second_term = (sub == 2) | (sub == 4)
    half = (lane // 64).astype(F32)

    def three(value):
        a = value.astype(BF16).astype(F32)
        rest = value - a
        b = rest.astype(BF16).astype(F32)
        return [a, b, rest - b]

    def features(column, wx, wy, both):
        x = halo[column, 0] + (wx - 1.0)
        y = halo[column, 1] + (wy - 1.0)
        z = halo[column, 2] + (half - 1.0)
        plane = x * x + y * y
        parts = three(x) + three(y) + three(z) + three(plane + z * z)
        if both:
            beside = z + (2.0 - 4.0 * half)
            parts += three(beside) + three(plane + beside * beside)
        for i, part in enumerate(parts):
            pieces[column, i] = part

    def spread(column, i, k):
        return jnp.broadcast_to(pieces[column, i, k : k + 1], (8, 128))

    def chosen(column, i, k, six, seven, terms):
        a, b, c = (spread(column, i + e, k) for e in range(3))
        value = jnp.where(terms[0], a, jnp.where(terms[1], b, c))
        return jnp.where(sub == 6, six, jnp.where(sub == 7, seven, value))

    zero8 = jnp.zeros((8, 128), F32)
    one8 = jnp.ones((8, 128), F32)
    t_terms = ((sub == 0) | (sub == 2) | (sub == 5), (sub == 1) | (sub == 4))
    s_terms = (first_term, second_term)
    scale8 = jnp.where(sub < 6, -2.0, 1.0)

    @pl.loop(0, 4, unroll=True)
    def _(col):
        cx, cy = col // 2, col % 2
        column = (1 + cx) * 4 + 1 + cy
        features(column, cx.astype(F32), cy.astype(F32), False)
        for k in range(0, 8, 2):
            turned = []
            for e in (k, k + 1):
                tiles = [
                    chosen(column, 0, e, one8, one8, t_terms),
                    chosen(column, 3, e, one8, spread(column, 9, e), t_terms),
                    chosen(column, 6, e, spread(column, 10, e), spread(column, 11, e), t_terms),
                ]
                tiles = jnp.concatenate([t * scale8 for t in tiles] + [zero8], 0)
                turned.append((tiles, pltpu.roll(tiles, 64, 1)))
            lane32 = lane64[:32] < 64
            upper = jnp.where(lane32, turned[0][0], turned[1][1])
            lower = jnp.where(lane32, turned[0][1], turned[1][0])
            stack = jnp.concatenate([upper, lower], 0).T.astype(BF16)
            target[col * 8 + k] = stack[:64]
            target[col * 8 + k + 1] = stack[64:]

    all_of(HALO).wait_recv()

    outside = jnp.where(lax.broadcasted_iota(jnp.int32, (32, 128), 0) == 6, 16384.0, 0.0)
    lane32 = lane64[:32] < 64
    left_half = lane32
    outside_low = jnp.where(left_half, outside, 0.0).astype(BF16)
    outside_high = jnp.where(left_half, 0.0, outside).astype(BF16)

    @pl.loop(0, 16, unroll=4)
    def _(column):
        wx, wy = column // 4, column % 4
        features(column, wx.astype(F32) - 1.0, wy.astype(F32) - 1.0, True)
        at_x, at_y = 2 * ix + wx - 1, 2 * iy + wy - 1
        inside = (at_x >= 0) & (at_x < 2 * count_x) & (at_y >= 0) & (at_y < 2 * count_y)
        q = halo[column, 3] * inside.astype(F32)
        after = jnp.where(sub == 7, 0.0, pltpu.roll(q, 7, 0))
        before = jnp.where(sub == 0, 0.0, pltpu.roll(q, 1, 0))
        charge[column, 0] = jnp.where(lane < 64, q, before)
        charge[column, 1] = q
        charge[column, 2] = jnp.where(lane < 64, after, q)
        source[column, 9, 2] = outside_low
        source[column, 0, 3] = outside_high
        for k in range(8):
            own_tiles = [
                chosen(column, 0, k, spread(column, 9, k), spread(column, 10, k), s_terms),
                chosen(column, 3, k, spread(column, 11, k), one8, s_terms),
                chosen(column, 6, k, one8, one8, s_terms),
                zero8,
            ]
            beside_tiles = [
                jnp.where(sub == 6, spread(column, 15, k), jnp.where(sub == 7, spread(column, 16, k), own_tiles[0])),
                jnp.where(sub == 6, spread(column, 17, k), own_tiles[1]),
                chosen(column, 12, k, one8, one8, s_terms),
                zero8,
            ]
            for e, tiles in enumerate((own_tiles, beside_tiles)):
                tiles = jnp.concatenate(tiles, 0)
                source[column, k + 1, 2 * e] = jnp.where(left_half, tiles, 0.0).astype(BF16)
                source[column, k + 1, 2 * e + 1] = jnp.where(left_half, 0.0, tiles).astype(BF16)

    def near_block(block, carry):
        col, k = block // 8, block % 8
        cx, cy = col // 2, col % 2
        mine = target[block]
        straight = jnp.zeros((64, 128), F32)
        crossed = jnp.zeros((64, 128), F32)
        columns = [(cx + dx) * 4 + cy + dy for dx in range(3) for dy in range(3)]

        def side(column, a, b):
            return jnp.concatenate([source[column, a[0], a[1]], source[column, b[0], b[1]]], 0)

        def row_of(column, dz):
            return charge[column, dz, pl.ds(k, 1), :]

        for column in columns:
            above = side(column, (k + 1, 1), (k + 2, 2))
            below = side(column, (k, 3), (k + 1, 0))
            inverse = lax.rsqrt(dot(mine, jnp.concatenate([above, below], 1)))
            crossed = crossed + inverse[:, :128] * row_of(column, 2)
            crossed = crossed + inverse[:, 128:] * row_of(column, 0)
        for i in range(0, 9, 2):
            group = columns[i : i + 2]
            both = [side(column, (k + 1, 0), (k + 1, 1)) for column in group]
            inverse = lax.rsqrt(dot(mine, jnp.concatenate(both, 1)))
            for e, column in enumerate(group):
                value = inverse[:, 128 * e : 128 * e + 128]
                if i + e == 4:
                    value = jnp.where(eye, 0.0, value)
                straight = straight + value * row_of(column, 1)
        sums[block] = straight + pltpu.roll(crossed, 64, 1)
        return carry

    lax.fori_loop(0, 32, near_block, 0, unroll=8)

    @pl.loop(0, 4, unroll=True)
    def _(col):
        value = sums[pl.ds(pl.multiple_of(col * 8, 8), 8)].reshape(512, 128)
        hi, lo = pair_split(value)
        value = dot(hi, halves) + dot(lo, halves)
        for k in range(8):
            mine = jnp.where(eye, value[64 * k : 64 * k + 64], 0.0)
            near[col, k : k + 1] = jnp.sum(mine, 0, keepdims=True)

    for kind in (LEAF, LINE, SECOND, THIRD):
        all_of(kind).wait_recv()

    for j in range(count_x // 4):
        group = thirds[4 * j] + thirds[4 * j + 1] + thirds[4 * j + 2] + thirds[4 * j + 3]
        group = jnp.concatenate([group] + [pltpu.roll(group, 128 - 16 * e, 1) for e in range(1, 4)], 0)
        third = [group] + [pltpu.roll(group, 128 - g, 1) for g in range(1, 8)]
        third = jnp.concatenate(third, 0)
        right3[128 * j : 128 * j + 64] = wide(third)
        right3[128 * j + 64 : 128 * j + 128] = wide(pltpu.roll(third, 64, 1))
    o = folded(dot(table3[...], right3[...]), 192)
    local = o[64:128]
    local = local + jnp.where(lane64 == 0, pltpu.roll(o[128:], 120, 1), 0.0)
    local = local + jnp.where(lane64 == 8, pltpu.roll(o[:64], 8, 1), 0.0)
    local3 = jnp.where((lane64 < 16) & (lane64 % 8 == 0), 0.125 * local, 0.0)

    plain, crossed = {}, {}
    for ox in (-1, 0, 1):
        for oy in (-1, 0, 1):
            value = moments[(ox + 1) * 3 + oy + 1]
            turned = pltpu.roll(value, 64, 1)
            lane32 = lane64[:32]
            value = jnp.concatenate(
                [jnp.where(lane32 < 64, value, turned), jnp.where(lane32 < 64, turned, value)], 0
            )
            scale = F32(1.0)
            if ox:
                scale = scale * (ix > 0 if ox < 0 else ix < count_x - 1).astype(F32)
            if oy:
                scale = scale * (iy > 0 if oy < 0 else iy < count_y - 1).astype(F32)
            plain[ox, oy] = value * scale
    by_x = lane64 // 32 % 2
    by_y = lane64 // 16 % 2

    def swap_y(value):
        return jnp.where(by_y == 0, pltpu.roll(value, 112, 1), pltpu.roll(value, 16, 1))

    def leaf_block(dx, dy):
        result = None
        for cx in range(2):
            for cy in range(2):
                ox, oy = (cx + dx) // 2, (cy + dy) // 2
                if abs(ox) > 1 or abs(oy) > 1:
                    continue
                value = plain[ox, oy]
                if dy % 2:
                    value = swap_y(value)
                if dx % 2:
                    value = pltpu.roll(value, 32, 1)
                mine = (by_x == cx) & (by_y == cy)
                value = jnp.where(mine, value, 0.0)
                result = value if result is None else result + value
        return result

    def within(value, count, step, odd):
        ok = (value >= 0) & (value < count)
        if step == 3:
            ok = ok & (odd == 0)
        if step == -3:
            ok = ok & (odd == 1)
        return ok.astype(F32)

    for dx in range(-3, 4):
        line = rows[lax.rem(ix + dx + count_x, count_x)]
        line = jnp.concatenate([line, pltpu.roll(line, 127, 1)], 0)
        line = pltpu.roll(line, lax.rem(64 - 16 * iy + 128, 128), 1)
        line = line * within(ix + dx, count_x, dx, ix % 2)
        x2 = ix // 2 + dx
        base = lax.rem(2 * x2 + 2 * count_x, count_x)
        pair = seconds[base] + seconds[base + 1]
        pair = pltpu.roll(pair, lax.rem(80 - 32 * (iy // 2) + 128, 128), 1)
        pair = [pltpu.roll(pair, (-(g % 4) - 16 * (g // 4)) % 128, 1) if g else pair for g in range(8)]
        pair = jnp.concatenate(pair, 0)
        pair = pair * within(x2, count_x // 2, dx, ix // 2 % 2)
        for dy in range(-3, 4):
            one = pltpu.roll(line, (-16 * dy) % 128, 1) * within(iy + dy, count_y, dy, iy % 2)
            two = pltpu.roll(pair, (-32 * dy) % 128, 1)
            two = two * within(iy // 2 + dy, count_y // 2, dy, iy // 2 % 2)
            value = jnp.where(lane64 < 64, leaf_block(dx, dy), jnp.where(lane64 < 80, one, two))
            value = jnp.where(lane64 < 96, value, 0.0)
            at = ((dx + 3) * 7 + dy + 3) * 64
            right[at : at + 64] = wide(value)
    right[49 * 64 : 50 * 64] = jnp.zeros((64, 256), BF16)

    product[...] = dot(table[...], right[...])

    far = jnp.zeros((64, 128), F32)
    for i in range(7):
        dz = i - 3
        o = product[64 * i : 64 * i + 64]
        o2 = product[448 + 64 * i : 512 + 64 * i]
        o = o[:, :128] + o[:, 128:] + o2[:, :128] + o2[:, 128:]
        for level in range(3):
            value = o if dz == 0 else pltpu.roll(o, (-dz * 2**level) % 128, 1)
            far = far + value * flat[at_w + 8 * level + i : at_w + 8 * level + i + 1]

    def down(source, which, step):
        o = folded(dot(dn_ref[which], wide(source)), 128)
        return jnp.where(lane64 % (2 * step) == 0, o[:64], pltpu.roll(o[64:], step, 1))

    low = lane64 < 16
    local2 = down(local3, ix // 2 % 2 * 2 + iy // 2 % 2, 4) + pltpu.roll(far, 48, 1)
    local2 = jnp.where(low & (lane64 % 4 == 0), local2, 0.0)
    local1 = down(local2, ix % 2 * 2 + iy % 2, 2) + pltpu.roll(far, 64, 1)
    local1 = jnp.where(low & (lane64 % 2 == 0), local1, 0.0)
    local0 = far
    for col in range(4):
        value = down(local1, col, 1)
        if col:
            value = pltpu.roll(value, 16 * col, 1)
        local0 = local0 + jnp.where(lane64 // 16 == col, value, 0.0)
    leaf[...] = local0

    @pl.loop(0, 4, unroll=True)
    def _(col):
        column = (1 + col // 2) * 4 + 1 + col % 2
        here = pltpu.roll(leaf[...], lax.rem(128 - 16 * col, 128), 1)
        for k in range(8):
            spread = jnp.where(
                lane64 < 64,
                jnp.broadcast_to(here[:, 2 * k : 2 * k + 1], (64, 128)),
                jnp.broadcast_to(here[:, 2 * k + 1 : 2 * k + 2], (64, 128)),
            )
            both = bases[8 * col + k] * spread
            near[col, k : k + 1] = jnp.sum(both, 0, keepdims=True) + near[col, k : k + 1]

    for col in range(4):
        for k in range(8):
            at = slice(128 * k, 128 * k + 128)
            out_ref[col // 2, col % 2 : col % 2 + 1, at] = near[col, k : k + 1]

    for kind in range(6):
        all_of(kind).wait_send()


def solution(mesh):
    count_x, count_y = mesh.shape["gx"], mesh.shape["gy"]
    fixed = constants()
    vmem = pl.BlockSpec(memory_space=pltpu.VMEM)
    hbm = pl.BlockSpec(memory_space=pltpu.HBM)
    dma = pltpu.SemaphoreType.DMA
    call = pl.pallas_call(
        functools.partial(kernel, count_x, count_y),
        out_shape=jax.ShapeDtypeStruct((2, 2, 1024), F32),
        in_specs=[hbm] * (2 + len(fixed)),
        out_specs=vmem,
        scratch_shapes=[
            pltpu.VMEM((3, 2, 2, 1024), F32),
            pltpu.VMEM((2, 2, 1024), F32),
            pltpu.VMEM((96 + 128 + 56 + 24 + 8, 128), F32),
            pltpu.VMEM(fixed[0].shape, BF16),
            pltpu.VMEM(fixed[1].shape, BF16),
            pltpu.VMEM(fixed[2].shape, BF16),
            pltpu.VMEM((16, 4, 8, 128), F32),
            pltpu.VMEM((9, 32, 128), F32),
            pltpu.VMEM((count_y, 8, 128), F32),
            pltpu.VMEM((count_x, 32, 128), F32),
            pltpu.VMEM((count_x, 8, 128), F32),
            pltpu.VMEM((count_x, 2, 128), F32),
            pltpu.VMEM((16, 18, 8, 128), F32),
            pltpu.VMEM((16, 10, 4, 32, 128), BF16),
            pltpu.VMEM((16, 3, 8, 128), F32),
            pltpu.VMEM((32, 64, 64), BF16),
            pltpu.VMEM((32, 64, 128), F32),
            pltpu.VMEM((4, 8, 128), F32),
            pltpu.VMEM((896, TILES * 128), BF16),
            pltpu.VMEM((384, count_x // 4 * 128), BF16),
            pltpu.VMEM((TILES * 128, 256), BF16),
            pltpu.VMEM((count_x // 4 * 128, 256), BF16),
            pltpu.VMEM((896, 256), F32),
            pltpu.VMEM((4, 1024, 128), BF16),
            pltpu.VMEM((64, 128), F32),
            pltpu.VMEM((32, 64, 128), F32),
            dma((5,)),
            dma((6,)),
            dma((6,)),
        ],
        compiler_params=pltpu.CompilerParams(
            collective_id=0, has_side_effects=True, vmem_limit_bytes=64 << 20
        ),
    )

    def body(offsets, charges):
        return call(offsets, charges, *fixed)

    in_specs = (P(None, "gx", "gy", None), P("gx", "gy", None))
    out_specs = P("gx", "gy", None)
    return jax.shard_map(body, mesh=mesh, in_specs=in_specs, out_specs=out_specs, check_vma=False)
```

```python
import functools

import jax
import jax.numpy as jnp
import ml_dtypes
import numpy as np
from jax import lax
from jax.experimental import pallas as pl
from jax.experimental.pallas import tpu as pltpu
from jax.sharding import PartitionSpec as P

MESH = pl.DeviceIdType.MESH
F32 = jnp.float32
BF16 = jnp.bfloat16
DIRS = [(ox, oy) for ox in (-1, 0, 1) for oy in (-1, 0, 1) if (ox, oy) != (0, 0)]
ROWS = (1, 2, 3, -1, -2, -3)
WIDER = (1, 2, 3, 4, 5, 6, 7, -1, -2, -3, -4, -5, -6, -7)
TILES = 25


def nodes():
    return np.cos((2.0 * np.arange(4) + 1.0) * np.pi / 8.0)


def cubic():
    t = nodes()
    t2, t3 = 2 * t * t - 1, 4 * t**3 - 3 * t
    return np.stack([0.25 - 0.5 * t2, 0.5 * t - 1.5 * t3, t2, 2 * t3])


def split(x):
    hi = x.astype(ml_dtypes.bfloat16)
    lo = (x - hi.astype(np.float64)).astype(ml_dtypes.bfloat16)
    return hi, lo


def constants():
    t = nodes()
    c = cubic()
    shifted = (t[None, :] + 2.0 * np.arange(2)[:, None] - 1.0) / 2.0
    f = sum(c[k][None, None, :] * shifted[:, :, None] ** k for k in range(4))
    up = np.einsum("xia,yjb,zkc->xyzijkabc", f, f, f).reshape(2, 2, 2, 64, 64)
    uf = up.transpose(2, 4, 0, 1, 3).reshape(128, 256)
    uf = np.concatenate(split(uf), 0)
    u2 = up.transpose(0, 1, 2, 4, 3).reshape(2, 256, 64)
    u2 = np.concatenate(split(u2), 1)
    return [uf, u2]


def pair_split(x):
    hi = x.astype(BF16)
    lo = (x - hi.astype(F32)).astype(BF16)
    return hi, lo


def wide(x):
    return jnp.concatenate(pair_split(x), 1)


def folded(product, rows):
    return product[:rows, :128] + product[:rows, 128:] + product[rows:, :128] + product[rows:, 128:]


def dot(left, right):
    return jnp.dot(left, right, preferred_element_type=F32)


def kernel(
    count_x, count_y,
    off_hbm, charge_hbm, uf_hbm, u2_hbm,
    out_ref,
    off_ref, charge_ref, flat, uf_ref, u2_ref,
    halo, moments, near_rows, rows, seconds, thirds, pieces, source, charge, target, sums, near,
    table, table3, right, right3, product, bq, leaf, bases,
    load_s, send_s, recv_s,
):
    loads = [
        pltpu.make_async_copy(src, dst, load_s.at[i])
        for i, (src, dst) in enumerate(
            [(off_hbm, off_ref), (charge_hbm, charge_ref)]
            + [(uf_hbm, uf_ref), (u2_hbm, u2_ref)]
        )
    ]
    for load in loads:
        load.start()
    at_rxy = 96
    at_z2 = at_rxy + 128
    at_w = at_z2 + 56
    at_l3 = at_w + 24
    ix = lax.axis_index("gx")
    iy = lax.axis_index("gy")
    lane = lax.broadcasted_iota(jnp.int32, (8, 128), 1)
    lane64 = lax.broadcasted_iota(jnp.int32, (64, 128), 1)
    row64 = lax.broadcasted_iota(jnp.int32, (64, 128), 0)
    eye = row64 == lane64 % 64
    sub = lax.broadcasted_iota(jnp.int32, (8, 128), 0)
    c = cubic()
    t = nodes()

    def pick(index, values):
        result = jnp.full(index.shape, float(values[3]), F32)
        for e in (2, 1, 0):
            result = jnp.where(index == e, float(values[e]), result)
        return result

    for i, index in enumerate((sub % 4, sub // 4, 2 + sub // 4)):
        for e in range(4):
            flat[32 * i + 8 * e : 32 * i + 8 * e + 8] = pick(index, c[e])
    flat[at_rxy : at_rxy + 64] = 0.5 * pick(row64 // 16, t)
    flat[at_rxy + 64 : at_rxy + 128] = 0.5 * pick(row64 // 4 % 4, t)
    gap_z = 0.5 * (pick(lane % 4, t) - pick(sub % 4, t))
    for i in range(7):
        gap = gap_z + (i - 3.0)
        flat[at_z2 + 8 * i : at_z2 + 8 * i + 8] = gap * gap
    for level, start, length in ((0, 0, 64), (1, 0, 16), (2, 16, 16)):
        z = lane % 16
        seen = z + (sub - 3) * 2**level
        odd = (z // 2**level) % 2
        ok = (z % 2**level == 0) & (seen >= 0) & (seen < 16) & (sub < 7)
        ok = ok & (lane >= start) & (lane < start + length)
        ok = ok & ((sub < 6) | (odd == 0)) & ((sub > 0) | (odd == 1))
        flat[at_w + 8 * level : at_w + 8 * level + 8] = jnp.where(ok, 0.5**level, 0.0)
    lane_x = 0.5 * pick(lane % 64 // 16, t)
    lane_y = 0.5 * pick(lane // 4 % 4, t)
    flat[at_l3 : at_l3 + 8] = jnp.where(sub == 0, lane_x, lane_y)

    def remote(src, dst, send, recv, dx, dy):
        device = (lax.rem(ix + dx + count_x, count_x), lax.rem(iy + dy + count_y, count_y))
        return pltpu.make_async_remote_copy(
            src_ref=src, dst_ref=dst, send_sem=send, recv_sem=recv,
            device_id=device, device_id_type=MESH,
        )

    barrier = pltpu.get_barrier_semaphore()

    def greet(dx, dy):
        device = (lax.rem(ix + dx + count_x, count_x), lax.rem(iy + dy + count_y, count_y))
        pl.semaphore_signal(barrier, inc=1, device_id=device, device_id_type=MESH)

    for ox, oy in DIRS:
        greet(ox, oy)

    for k in range(1, count_y):
        greet(0, k)
    for k in range(1, count_x):
        greet(k, 0)

    def table_tile(j):
        dx = [(2 * j + e) // 7 - 3 for e in range(2)]
        dy = [(2 * j + e) % 7 - 3 for e in range(2)]
        dx, dy = (jnp.where(lane < 64, v[0], v[1]).astype(F32) for v in (dx, dy))
        gap_x = (dx + lane_x)[:1] - flat[at_rxy : at_rxy + 64]
        gap_y = (dy + lane_y)[:1] - flat[at_rxy + 64 : at_rxy + 128]
        adjacent = jnp.maximum(jnp.abs(dx), jnp.abs(dy))[:1]
        adjacent = jnp.broadcast_to(adjacent, (64, 128)) <= 1.0
        plane = gap_x * gap_x + gap_y * gap_y
        at = pl.ds(pl.multiple_of(j * 128, 128), 128)
        for i in range(7):
            value = lax.rsqrt(plane + jnp.concatenate([flat[at_z2 + 8 * i : at_z2 + 8 * i + 8]] * 8, 0))
            if i in (2, 3, 4):
                value = jnp.where(adjacent, 0.0, value)
            hi, lo = pair_split(value)
            table[64 * i : 64 * i + 64, at] = hi
            table[448 + 64 * i : 512 + 64 * i, at] = lo

    @pl.loop(0, count_x // 4)
    def _(j):
        apart = (j - ix // 4).astype(F32)
        side = (lane64 // 64 - iy // 4).astype(F32)
        gap_x = apart + flat[at_l3 : at_l3 + 1] - flat[at_rxy : at_rxy + 64]
        gap_y = side + flat[at_l3 + 1 : at_l3 + 2] - flat[at_rxy + 64 : at_rxy + 128]
        adjacent = jnp.maximum(jnp.abs(side), jnp.abs(apart)) <= 1.0
        plane = gap_x * gap_x + gap_y * gap_y
        at = pl.ds(pl.multiple_of(j * 128, 128), 128)
        for i in range(3):
            value = lax.rsqrt(plane + jnp.concatenate([flat[at_z2 + 8 * i + 16 : at_z2 + 8 * i + 24]] * 8, 0))
            value = jnp.where(adjacent, 0.0, value)
            hi, lo = pair_split(value)
            table3[64 * i : 64 * i + 64, at] = hi
            table3[192 + 64 * i : 256 + 64 * i, at] = lo

    pl.loop(0, 8)(table_tile)

    def basis(column, k, level=0, col=None):
        places = [halo[column, comp, k : k + 1, :] for comp in range(3)]
        if level:
            size = 2**level
            corner = (
                ((2 * ix + col // 2) % size).astype(F32),
                ((2 * iy + col % 2) % size).astype(F32),
                (2 * k) % size + (lane[:1] // 64).astype(F32),
            )
            places = [(place + at) * (1.0 / size) for place, at in zip(places, corner)]
        x, y, z = (2.0 * place - 1.0 for place in places)

        def poly(i, u):
            p = [flat[32 * i + 8 * e : 32 * i + 8 * e + 8] for e in range(4)]
            return ((p[3] * u + p[2]) * u + p[1]) * u + p[0]

        along_z = poly(0, z)
        low, high = poly(1, y) * along_z, poly(2, y) * along_z
        pieces = []
        for a in range(4):
            s = ((float(c[3, a]) * x + float(c[2, a])) * x + float(c[1, a])) * x + float(c[0, a])
            pieces += [s * low, s * high]
        return jnp.concatenate(pieces, 0)

    def column_of(cx, cy):
        return (1 + cx) * 4 + 1 + cy

    for load in loads[:2]:
        load.wait()
    for cx in range(2):
        for cy in range(2):
            for k in range(8):
                at = slice(128 * k, 128 * k + 128)
                for comp in range(3):
                    halo[column_of(cx, cy), comp, k : k + 1] = off_ref[comp, cx, cy : cy + 1, at]
                halo[column_of(cx, cy), 3, k : k + 1] = charge_ref[cx, cy : cy + 1, at]
    ROW, HALO, LEAF, LINE, SECOND, THIRD = range(6)
    buffers = (near_rows, halo, moments, rows, seconds, thirds)
    counts = (count_y - 1, 12, 8, 6, len(WIDER), count_x - 1)

    def send(kind, index, at, dx, dy):
        buffer = buffers[kind]
        sems = (send_s.at[kind], recv_s.at[kind])
        remote(buffer.at[index], buffer.at[at], *sems, dx, dy).start()

    def all_of(kind):
        part = buffers[kind].at[pl.ds(0, counts[kind])]
        return remote(part, part, send_s.at[kind], recv_s.at[kind], 1, 1)

    pl.semaphore_wait(barrier, len(DIRS) + count_y - 1 + count_x - 1)
    for ox, oy in DIRS:
        take_x = {1: [2], -1: [1], 0: [1, 2]}[ox]
        put_x = {1: [0], -1: [3], 0: [1, 2]}[ox]
        take_y = {1: (2, 1), -1: (1, 1), 0: (1, 2)}[oy]
        put_y = {1: 0, -1: 3, 0: 1}[oy]
        for a, b in zip(take_x, put_x):
            at = (pl.ds(a * 4 + take_y[0], take_y[1]), pl.ds(b * 4 + put_y, take_y[1]))
            send(HALO, *at, ox, oy)
    half_row = lax.broadcasted_iota(jnp.int32, (128, 128), 0) // 64
    half_lane = lax.broadcasted_iota(jnp.int32, (128, 128), 1)
    parity = (half_row == half_lane % 2).astype(F32).astype(BF16)
    halves = (half_row == half_lane // 64).astype(F32).astype(BF16)
    leaf[...] = jnp.zeros((64, 128), F32)

    @pl.loop(0, 4, unroll=True)
    def _(col):
        column = (1 + col // 2) * 4 + 1 + col % 2
        for k in range(8):
            value = basis(column, k)
            bases[0, 8 * col + k] = value
            value = value * halo[column, 3, k : k + 1, :]
            hi, lo = pair_split(value)
            bq[col, 64 * k : 64 * k + 64] = hi
            bq[col, 512 + 64 * k : 576 + 64 * k] = lo
        summed = dot(bq[col], parity)
        total = leaf[...]
        for k in range(8):
            here = (lane64 % 64) // 2 == col * 8 + k
            total = jnp.where(
                here,
                summed[64 * k : 64 * k + 64] + summed[512 + 64 * k : 576 + 64 * k],
                total,
            )
        leaf[...] = total

    for load in loads[2:]:
        load.wait()
    own = leaf[...]
    moments[4] = jnp.where(lane64[:32] < 64, own[:32], own[32:])
    stacked = jnp.concatenate(
        [own] + [pltpu.roll(own, 128 - 16 * col, 1) for col in range(1, 4)], 0
    )
    first = folded(dot(uf_ref[...], wide(stacked)), 128)
    first = first[:64] + pltpu.roll(first[64:], 127, 1)
    first = jnp.where((lane64 < 16) & (lane64 % 2 == 0), first, 0.0)
    packet = first[:8]
    for g in range(1, 8):
        packet = packet + pltpu.roll(first[8 * g : 8 * g + 8], 16 * g, 1)
    near_rows[iy] = packet

    for k in range(1, count_y):
        send(ROW, iy, iy, 0, k)
    for ox, oy in DIRS:
        send(LEAF, 4, (1 - ox) * 3 + 1 - oy, ox, oy)

    pl.loop(8, TILES)(table_tile)

    @pl.loop(0, 4, unroll=True)
    def _(col):
        column = (1 + col // 2) * 4 + 1 + col % 2
        for level in range(1, 4):
            for k in range(8):
                bases[level, 8 * col + k] = basis(column, k, level, col)

    first_term = (sub == 0) | (sub == 1) | (sub == 3)
    second_term = (sub == 2) | (sub == 4)
    half = (lane // 64).astype(F32)

    def three(value):
        a = value.astype(BF16).astype(F32)
        rest = value - a
        b = rest.astype(BF16).astype(F32)
        return [a, b, rest - b]

    def features(column, wx, wy, both):
        x = halo[column, 0] + (wx - 1.0)
        y = halo[column, 1] + (wy - 1.0)
        z = halo[column, 2] + (half - 1.0)
        plane = x * x + y * y
        parts = three(x) + three(y) + three(z) + three(plane + z * z)
        if both:
            beside = z + (2.0 - 4.0 * half)
            parts += three(beside) + three(plane + beside * beside)
        for i, part in enumerate(parts):
            pieces[column, i] = part

    def spread(column, i, k):
        return jnp.broadcast_to(pieces[column, i, k : k + 1], (8, 128))

    def chosen(column, i, k, six, seven, terms):
        a, b, c = (spread(column, i + e, k) for e in range(3))
        value = jnp.where(terms[0], a, jnp.where(terms[1], b, c))
        return jnp.where(sub == 6, six, jnp.where(sub == 7, seven, value))

    zero8 = jnp.zeros((8, 128), F32)
    one8 = jnp.ones((8, 128), F32)
    t_terms = ((sub == 0) | (sub == 2) | (sub == 5), (sub == 1) | (sub == 4))
    s_terms = (first_term, second_term)
    scale8 = jnp.where(sub < 6, -2.0, 1.0)

    @pl.loop(0, 4, unroll=True)
    def _(col):
        cx, cy = col // 2, col % 2
        column = (1 + cx) * 4 + 1 + cy
        features(column, cx.astype(F32), cy.astype(F32), False)
        for k in range(0, 8, 2):
            turned = []
            for e in (k, k + 1):
                tiles = [
                    chosen(column, 0, e, one8, one8, t_terms),
                    chosen(column, 3, e, one8, spread(column, 9, e), t_terms),
                    chosen(column, 6, e, spread(column, 10, e), spread(column, 11, e), t_terms),
                ]
                tiles = jnp.concatenate([t * scale8 for t in tiles] + [zero8], 0)
                turned.append((tiles, pltpu.roll(tiles, 64, 1)))
            lane32 = lane64[:32] < 64
            upper = jnp.where(lane32, turned[0][0], turned[1][1])
            lower = jnp.where(lane32, turned[0][1], turned[1][0])
            stack = jnp.concatenate([upper, lower], 0).T.astype(BF16)
            target[col * 8 + k] = stack[:64]
            target[col * 8 + k + 1] = stack[64:]

    outside = jnp.where(lax.broadcasted_iota(jnp.int32, (32, 128), 0) == 6, 16384.0, 0.0)
    lane32 = lane64[:32] < 64
    left_half = lane32
    outside_low = jnp.where(left_half, outside, 0.0).astype(BF16)
    outside_high = jnp.where(left_half, 0.0, outside).astype(BF16)

    def source_column(column):
        wx, wy = column // 4, column % 4
        features(column, wx.astype(F32) - 1.0, wy.astype(F32) - 1.0, True)
        at_x, at_y = 2 * ix + wx - 1, 2 * iy + wy - 1
        inside = (at_x >= 0) & (at_x < 2 * count_x) & (at_y >= 0) & (at_y < 2 * count_y)
        q = halo[column, 3] * inside.astype(F32)
        after = jnp.where(sub == 7, 0.0, pltpu.roll(q, 7, 0))
        before = jnp.where(sub == 0, 0.0, pltpu.roll(q, 1, 0))
        charge[column, 0] = jnp.where(lane < 64, q, before)
        charge[column, 1] = q
        charge[column, 2] = jnp.where(lane < 64, after, q)
        source[column, 9, 2] = outside_low
        source[column, 0, 3] = outside_high
        for k in range(8):
            own_tiles = [
                chosen(column, 0, k, spread(column, 9, k), spread(column, 10, k), s_terms),
                chosen(column, 3, k, spread(column, 11, k), one8, s_terms),
                chosen(column, 6, k, one8, one8, s_terms),
                zero8,
            ]
            beside_tiles = [
                jnp.where(sub == 6, spread(column, 15, k), jnp.where(sub == 7, spread(column, 16, k), own_tiles[0])),
                jnp.where(sub == 6, spread(column, 17, k), own_tiles[1]),
                chosen(column, 12, k, one8, one8, s_terms),
                zero8,
            ]
            for e, tiles in enumerate((own_tiles, beside_tiles)):
                tiles = jnp.concatenate(tiles, 0)
                source[column, k + 1, 2 * e] = jnp.where(left_half, tiles, 0.0).astype(BF16)
                source[column, k + 1, 2 * e + 1] = jnp.where(left_half, 0.0, tiles).astype(BF16)

    def near_sum(mine, k, columns, own):
        straight = jnp.zeros((64, 128), F32)
        crossed = jnp.zeros((64, 128), F32)

        def side(column, a, b):
            return jnp.concatenate([source[column, a[0], a[1]], source[column, b[0], b[1]]], 0)

        def row_of(column, dz):
            return charge[column, dz, pl.ds(k, 1), :]

        for column in columns:
            above = side(column, (k + 1, 1), (k + 2, 2))
            below = side(column, (k, 3), (k + 1, 0))
            inverse = lax.rsqrt(dot(mine, jnp.concatenate([above, below], 1)))
            crossed = crossed + inverse[:, :128] * row_of(column, 2)
            crossed = crossed + inverse[:, 128:] * row_of(column, 0)
        for i in range(0, len(columns), 2):
            group = columns[i : i + 2]
            both = [side(column, (k + 1, 0), (k + 1, 1)) for column in group]
            inverse = lax.rsqrt(dot(mine, jnp.concatenate(both, 1)))
            for e, column in enumerate(group):
                value = inverse[:, 128 * e : 128 * e + 128]
                if own and i + e == 0:
                    value = jnp.where(eye, 0.0, value)
                straight = straight + value * row_of(column, 1)
        return straight + pltpu.roll(crossed, 64, 1)

    @pl.loop(0, 4, unroll=True)
    def _(col):
        source_column((1 + col // 2) * 4 + 1 + col % 2)

    def inner_block(block, carry):
        col, k = block // 8, block % 8
        cx, cy = col // 2, col % 2
        columns = [(1 + a) * 4 + 1 + b for a in (cx, 1 - cx) for b in (cy, 1 - cy)]
        sums[block] = near_sum(target[block], k, columns, True)
        return carry

    lax.fori_loop(0, 32, inner_block, 0, unroll=8)

    all_of(ROW).wait_recv()
    packets = [near_rows[k] for k in range(count_y)]
    full = []
    for g in range(8):
        tile = jnp.zeros((8, 128), F32)
        for k in range(count_y):
            moved = pltpu.roll(packets[k], 16 * (k - g) % 128, 1) if k != g else packets[k]
            tile = jnp.where(lane // 16 == k, moved, tile)
        full.append(tile)
    full = jnp.concatenate(full, 0)
    rows[ix] = full[:32] + pltpu.roll(full[32:], 1, 1)

    def part(source, which, step_z, step_y):
        o = folded(dot(u2_ref[which], wide(source)), 256)
        return (
            o[:64]
            + pltpu.roll(o[64:128], 128 - step_z, 1)
            + pltpu.roll(o[128:192], 128 - step_y, 1)
            + pltpu.roll(o[192:], 128 - step_z - step_y, 1)
        )

    second = part(full, ix % 2, 2, 16)
    second = jnp.where((lane64 // 16 % 2 == 0) & (lane64 % 4 == 0), second, 0.0)
    third = part(second, ix // 2 % 2, 4, 32)
    third = jnp.where((lane64 // 16 % 4 == 0) & (lane64 % 8 == 0), third, 0.0)
    packed = second[:8]
    for g in range(1, 8):
        packed = packed + pltpu.roll(second[8 * g : 8 * g + 8], g % 4 + 16 * (g // 4), 1)
    seconds[ix] = packed
    packed = third[:8]
    for g in range(1, 8):
        packed = packed + pltpu.roll(third[8 * g : 8 * g + 8], g, 1)
    pair = packed[:2]
    for e in range(1, 4):
        pair = pair + pltpu.roll(packed[2 * e : 2 * e + 2], 16 * e, 1)
    thirds[ix] = pair

    for dx in ROWS:
        send(LINE, ix, ix, dx, 0)
    for dx in WIDER:
        send(SECOND, ix, ix, dx, 0)
    for k in range(1, count_x):
        send(THIRD, ix, ix, k, 0)

    all_of(HALO).wait_recv()


    @pl.loop(0, 4, unroll=True)
    def _(e):
        for column in (e, 12 + e):
            source_column(column)

    @pl.loop(0, 2, unroll=True)
    def _(e):
        for column in (4, 7):
            source_column(column + 4 * e)

    def outer_block(block, carry):
        col, k = block // 8, block % 8
        cx, cy = col // 2, col % 2
        columns = [12 * cx + cy + b for b in range(3)] + [4 + 3 * cy, 8 + 3 * cy]
        sums[block] = sums[block] + near_sum(target[block], k, columns, False)
        return carry

    lax.fori_loop(0, 32, outer_block, 0, unroll=8)

    @pl.loop(0, 4, unroll=True)
    def _(col):
        value = sums[pl.ds(pl.multiple_of(col * 8, 8), 8)].reshape(512, 128)
        hi, lo = pair_split(value)
        value = dot(hi, halves) + dot(lo, halves)
        for k in range(8):
            mine = jnp.where(eye, value[64 * k : 64 * k + 64], 0.0)
            near[col, k : k + 1] = jnp.sum(mine, 0, keepdims=True)

    all_of(LEAF).wait_recv()
    plain = {}
    for ox in (-1, 0, 1):
        for oy in (-1, 0, 1):
            value = moments[(ox + 1) * 3 + oy + 1]
            turned = pltpu.roll(value, 64, 1)
            lane32 = lane64[:32]
            value = jnp.concatenate(
                [jnp.where(lane32 < 64, value, turned), jnp.where(lane32 < 64, turned, value)], 0
            )
            scale = F32(1.0)
            if ox:
                scale = scale * (ix > 0 if ox < 0 else ix < count_x - 1).astype(F32)
            if oy:
                scale = scale * (iy > 0 if oy < 0 else iy < count_y - 1).astype(F32)
            plain[ox, oy] = value * scale
    by_x = lane64 // 32 % 2
    by_y = lane64 // 16 % 2

    def swap_y(value):
        return jnp.where(by_y == 0, pltpu.roll(value, 112, 1), pltpu.roll(value, 16, 1))

    def leaf_block(dx, dy):
        result = None
        for cx in range(2):
            for cy in range(2):
                ox, oy = (cx + dx) // 2, (cy + dy) // 2
                if abs(ox) > 1 or abs(oy) > 1:
                    continue
                value = plain[ox, oy]
                if dy % 2:
                    value = swap_y(value)
                if dx % 2:
                    value = pltpu.roll(value, 32, 1)
                mine = (by_x == cx) & (by_y == cy)
                value = jnp.where(mine, value, 0.0)
                result = value if result is None else result + value
        return result

    for dx in range(-3, 4):
        for dy in range(-3, 4):
            value = leaf_block(dx, dy)
            high = value.astype(BF16).astype(F32)
            at = ((dx + 3) * 7 + dy + 3) * 64
            right[at : at + 64] = jnp.where(lane64 < 64, high, value - high).astype(BF16)
    right[49 * 64 : 50 * 64] = jnp.zeros((64, 128), BF16)

    product[...] = dot(table[...], right[...])

    def shifted(i, fold, levels):
        o = product[64 * i : 64 * i + 64] + product[448 + 64 * i : 512 + 64 * i]
        o = o + pltpu.roll(o, fold, 1)
        total = jnp.zeros((64, 128), F32)
        for level in levels:
            value = o if i == 3 else pltpu.roll(o, (-(i - 3) * 2**level) % 128, 1)
            total = total + value * flat[at_w + 8 * level + i : at_w + 8 * level + i + 1]
        return total

    far = shifted(0, 64, (0,))
    for i in range(1, 7):
        far = far + shifted(i, 64, (0,))
    leaf[...] = far

    @pl.loop(0, 4, unroll=True)
    def _(col):
        here = pltpu.roll(leaf[...], (128 - 16 * col) % 128, 1)
        for k in range(8):
            spread = jnp.where(
                lane64 < 64,
                jnp.broadcast_to(here[:, 2 * k : 2 * k + 1], (64, 128)),
                jnp.broadcast_to(here[:, 2 * k + 1 : 2 * k + 2], (64, 128)),
            )
            both = jnp.sum(bases[0, 8 * col + k] * spread, 0, keepdims=True)
            near[col, k : k + 1] = near[col, k : k + 1] + both

    for kind in (LINE, SECOND):
        all_of(kind).wait_recv()
    def within(value, count, step, odd):
        ok = (value >= 0) & (value < count)
        if step == 3:
            ok = ok & (odd == 0)
        if step == -3:
            ok = ok & (odd == 1)
        return ok.astype(F32)

    for dx in range(-3, 4):
        line = rows[lax.rem(ix + dx + count_x, count_x)]
        line = jnp.concatenate([line, pltpu.roll(line, 127, 1)], 0)
        line = pltpu.roll(line, lax.rem(128 - 16 * iy, 128), 1)
        line = line * within(ix + dx, count_x, dx, ix % 2)
        x2 = ix // 2 + dx
        base = lax.rem(2 * x2 + 2 * count_x, count_x)
        pair = seconds[base] + seconds[base + 1]
        pair = pltpu.roll(pair, lax.rem(144 - 32 * (iy // 2), 128), 1)
        pair = [pltpu.roll(pair, (-(g % 4) - 16 * (g // 4)) % 128, 1) if g else pair for g in range(8)]
        pair = jnp.concatenate(pair, 0)
        pair = pair * within(x2, count_x // 2, dx, ix // 2 % 2)
        for dy in range(-3, 4):
            one = pltpu.roll(line, (-16 * dy) % 128, 1) * within(iy + dy, count_y, dy, iy % 2)
            two = pltpu.roll(pair, (-32 * dy) % 128, 1)
            two = two * within(iy // 2 + dy, count_y // 2, dy, iy // 2 % 2)
            value = jnp.where(lane64 < 16, one, two)
            high = value.astype(BF16).astype(F32)
            low = jnp.where(lane64 < 64, pltpu.roll(value - high, 32, 1), 0.0)
            at = ((dx + 3) * 7 + dy + 3) * 64
            right[at : at + 64] = jnp.where(lane64 < 32, high, low).astype(BF16)

    product[...] = dot(table[...], right[...])

    far12 = shifted(0, 96, (1, 2))
    for i in range(1, 7):
        far12 = far12 + shifted(i, 96, (1, 2))

    all_of(THIRD).wait_recv()
    for j in range(count_x // 4):
        group = thirds[4 * j] + thirds[4 * j + 1] + thirds[4 * j + 2] + thirds[4 * j + 3]
        group = jnp.concatenate([group] + [pltpu.roll(group, 128 - 16 * e, 1) for e in range(1, 4)], 0)
        third = [group] + [pltpu.roll(group, 128 - g, 1) for g in range(1, 8)]
        third = jnp.concatenate(third, 0)
        right3[128 * j : 128 * j + 64] = wide(third)
        right3[128 * j + 64 : 128 * j + 128] = wide(pltpu.roll(third, 64, 1))
    o = folded(dot(table3[...], right3[...]), 192)
    local = o[64:128]
    local = local + jnp.where(lane64 == 0, pltpu.roll(o[128:], 120, 1), 0.0)
    local = local + jnp.where(lane64 == 8, pltpu.roll(o[:64], 8, 1), 0.0)
    local3 = jnp.where((lane64 < 16) & (lane64 % 8 == 0), 0.125 * local, 0.0)

    def column(value, at):
        return jnp.broadcast_to(value[:, at : at + 1], (64, 128))

    for k in range(8):
        if k % 4 == 0:
            high3 = column(local3, 2 * k)
        if k % 2 == 0:
            high2 = column(far12, 16 + 2 * k)
        high1 = column(far12, 2 * k)
        for col in range(4):
            block = 8 * col + k
            both = bases[1, block] * high1 + bases[2, block] * high2 + bases[3, block] * high3
            both = jnp.sum(both, 0, keepdims=True) + near[col, k : k + 1]
            out_ref[col // 2, col % 2 : col % 2 + 1, 128 * k : 128 * k + 128] = both

    for kind in range(6):
        all_of(kind).wait_send()


def solution(mesh):
    count_x, count_y = mesh.shape["gx"], mesh.shape["gy"]
    fixed = constants()
    vmem = pl.BlockSpec(memory_space=pltpu.VMEM)
    hbm = pl.BlockSpec(memory_space=pltpu.HBM)
    dma = pltpu.SemaphoreType.DMA
    call = pl.pallas_call(
        functools.partial(kernel, count_x, count_y),
        out_shape=jax.ShapeDtypeStruct((2, 2, 1024), F32),
        in_specs=[hbm] * (2 + len(fixed)),
        out_specs=vmem,
        scratch_shapes=[
            pltpu.VMEM((3, 2, 2, 1024), F32),
            pltpu.VMEM((2, 2, 1024), F32),
            pltpu.VMEM((96 + 128 + 56 + 24 + 8, 128), F32),
            pltpu.VMEM(fixed[0].shape, BF16),
            pltpu.VMEM(fixed[1].shape, BF16),
            pltpu.VMEM((16, 4, 8, 128), F32),
            pltpu.VMEM((9, 32, 128), F32),
            pltpu.VMEM((count_y, 8, 128), F32),
            pltpu.VMEM((count_x, 32, 128), F32),
            pltpu.VMEM((count_x, 8, 128), F32),
            pltpu.VMEM((count_x, 2, 128), F32),
            pltpu.VMEM((16, 18, 8, 128), F32),
            pltpu.VMEM((16, 10, 4, 32, 128), BF16),
            pltpu.VMEM((16, 3, 8, 128), F32),
            pltpu.VMEM((32, 64, 64), BF16),
            pltpu.VMEM((32, 64, 128), F32),
            pltpu.VMEM((4, 8, 128), F32),
            pltpu.VMEM((896, TILES * 128), BF16),
            pltpu.VMEM((384, count_x // 4 * 128), BF16),
            pltpu.VMEM((TILES * 128, 128), BF16),
            pltpu.VMEM((count_x // 4 * 128, 256), BF16),
            pltpu.VMEM((896, 128), F32),
            pltpu.VMEM((4, 1024, 128), BF16),
            pltpu.VMEM((64, 128), F32),
            pltpu.VMEM((4, 32, 64, 128), F32),
            dma((4,)),
            dma((6,)),
            dma((6,)),
        ],
        compiler_params=pltpu.CompilerParams(
            collective_id=0, has_side_effects=True, vmem_limit_bytes=64 << 20
        ),
    )

    def body(offsets, charges):
        return call(offsets, charges, *fixed)

    in_specs = (P(None, "gx", "gy", None), P("gx", "gy", None))
    out_specs = P("gx", "gy", None)
    return jax.shard_map(body, mesh=mesh, in_specs=in_specs, out_specs=out_specs, check_vma=False)
```

```python
import functools

import jax
import jax.numpy as jnp
import ml_dtypes
import numpy as np
from jax import lax
from jax.experimental import pallas as pl
from jax.experimental.pallas import tpu as pltpu
from jax.sharding import PartitionSpec as P

MESH = pl.DeviceIdType.MESH
F32 = jnp.float32
BF16 = jnp.bfloat16
DIRS = [(ox, oy) for ox in (-1, 0, 1) for oy in (-1, 0, 1) if (ox, oy) != (0, 0)]
ROWS = (1, 2, -1, -2)
WIDER = (1, 2, 3, 4, 5, 6, 7, -1, -2, -3, -4, -5, -6, -7)
TILES = 25


def nodes():
    return np.cos((2.0 * np.arange(4) + 1.0) * np.pi / 8.0)


def cubic():
    t = nodes()
    t2, t3 = 2 * t * t - 1, 4 * t**3 - 3 * t
    return np.stack([0.25 - 0.5 * t2, 0.5 * t - 1.5 * t3, t2, 2 * t3])


def split(x):
    hi = x.astype(ml_dtypes.bfloat16)
    lo = (x - hi.astype(np.float64)).astype(ml_dtypes.bfloat16)
    return hi, lo


def constants():
    t = nodes()
    c = cubic()
    shifted = (t[None, :] + 2.0 * np.arange(2)[:, None] - 1.0) / 2.0
    f = sum(c[k][None, None, :] * shifted[:, :, None] ** k for k in range(4))
    up = np.einsum("xia,yjb,zkc->xyzijkabc", f, f, f).reshape(2, 2, 2, 64, 64)
    uf = up.transpose(2, 4, 0, 1, 3).reshape(128, 256)
    uf = np.concatenate(split(uf), 0)
    u2 = up.transpose(0, 1, 2, 4, 3).reshape(2, 256, 64)
    u2 = np.concatenate(split(u2), 1)
    return [uf, u2]


def pair_split(x):
    hi = x.astype(BF16)
    lo = (x - hi.astype(F32)).astype(BF16)
    return hi, lo


def wide(x):
    return jnp.concatenate(pair_split(x), 1)


def folded(product, rows):
    return product[:rows, :128] + product[:rows, 128:] + product[rows:, :128] + product[rows:, 128:]


def dot(left, right):
    return jnp.dot(left, right, preferred_element_type=F32)


def kernel(
    count_x, count_y,
    off_hbm, charge_hbm, uf_hbm, u2_hbm,
    out_ref,
    off_ref, charge_ref, flat, uf_ref, u2_ref,
    halo, moments, near_rows, rows, seconds, thirds, pieces, source, charge, target, sums, near,
    table, table3, right, right3, product, bq, leaf, bases,
    load_s, send_s, recv_s,
):
    loads = [
        pltpu.make_async_copy(src, dst, load_s.at[i])
        for i, (src, dst) in enumerate(
            [(off_hbm, off_ref), (charge_hbm, charge_ref)]
            + [(uf_hbm, uf_ref), (u2_hbm, u2_ref)]
        )
    ]
    for load in loads:
        load.start()
    at_rxy = 96
    at_z2 = at_rxy + 128
    at_w = at_z2 + 56
    at_l3 = at_w + 24
    ix = lax.axis_index("gx")
    iy = lax.axis_index("gy")
    lane = lax.broadcasted_iota(jnp.int32, (8, 128), 1)
    lane64 = lax.broadcasted_iota(jnp.int32, (64, 128), 1)
    row64 = lax.broadcasted_iota(jnp.int32, (64, 128), 0)
    eye = row64 == lane64 % 64
    sub = lax.broadcasted_iota(jnp.int32, (8, 128), 0)
    c = cubic()
    t = nodes()

    def pick(index, values):
        result = jnp.full(index.shape, float(values[3]), F32)
        for e in (2, 1, 0):
            result = jnp.where(index == e, float(values[e]), result)
        return result

    for i, index in enumerate((sub % 4, sub // 4, 2 + sub // 4)):
        for e in range(4):
            flat[32 * i + 8 * e : 32 * i + 8 * e + 8] = pick(index, c[e])
    flat[at_rxy : at_rxy + 64] = 0.5 * pick(row64 // 16, t)
    flat[at_rxy + 64 : at_rxy + 128] = 0.5 * pick(row64 // 4 % 4, t)
    gap_z = 0.5 * (pick(lane % 4, t) - pick(sub % 4, t))
    for i in range(7):
        gap = gap_z + (i - 3.0)
        flat[at_z2 + 8 * i : at_z2 + 8 * i + 8] = gap * gap
    for level, start, length in ((0, 0, 64), (1, 0, 16), (2, 16, 16)):
        z = lane % 16
        seen = z + (sub - 3) * 2**level
        odd = (z // 2**level) % 2
        ok = (z % 2**level == 0) & (seen >= 0) & (seen < 16) & (sub < 7)
        ok = ok & (lane >= start) & (lane < start + length)
        ok = ok & ((sub < 6) | (odd == 0)) & ((sub > 0) | (odd == 1))
        flat[at_w + 8 * level : at_w + 8 * level + 8] = jnp.where(ok, 0.5**level, 0.0)
    lane_x = 0.5 * pick(lane % 64 // 16, t)
    lane_y = 0.5 * pick(lane // 4 % 4, t)
    flat[at_l3 : at_l3 + 8] = jnp.where(sub == 0, lane_x, lane_y)

    def remote(src, dst, send, recv, dx, dy):
        device = (lax.rem(ix + dx + count_x, count_x), lax.rem(iy + dy + count_y, count_y))
        return pltpu.make_async_remote_copy(
            src_ref=src, dst_ref=dst, send_sem=send, recv_sem=recv,
            device_id=device, device_id_type=MESH,
        )

    barrier = pltpu.get_barrier_semaphore()

    def greet(dx, dy):
        device = (lax.rem(ix + dx + count_x, count_x), lax.rem(iy + dy + count_y, count_y))
        pl.semaphore_signal(barrier, inc=1, device_id=device, device_id_type=MESH)

    for ox, oy in DIRS:
        greet(ox, oy)

    for k in range(1, count_y):
        greet(0, k)
    for k in range(1, count_x):
        greet(k, 0)

    def table_tile(j):
        dx = [(2 * j + e) // 7 - 3 for e in range(2)]
        dy = [(2 * j + e) % 7 - 3 for e in range(2)]
        dx, dy = (jnp.where(lane < 64, v[0], v[1]).astype(F32) for v in (dx, dy))
        gap_x = (dx + lane_x)[:1] - flat[at_rxy : at_rxy + 64]
        gap_y = (dy + lane_y)[:1] - flat[at_rxy + 64 : at_rxy + 128]
        adjacent = jnp.maximum(jnp.abs(dx), jnp.abs(dy))[:1]
        adjacent = jnp.broadcast_to(adjacent, (64, 128)) <= 1.0
        plane = gap_x * gap_x + gap_y * gap_y
        at = pl.ds(pl.multiple_of(j * 128, 128), 128)
        for i in range(7):
            value = lax.rsqrt(plane + jnp.concatenate([flat[at_z2 + 8 * i : at_z2 + 8 * i + 8]] * 8, 0))
            if i in (2, 3, 4):
                value = jnp.where(adjacent, 0.0, value)
            hi, lo = pair_split(value)
            table[64 * i : 64 * i + 64, at] = hi
            table[448 + 64 * i : 512 + 64 * i, at] = lo

    @pl.loop(0, count_x // 4)
    def _(j):
        apart = (j - ix // 4).astype(F32)
        side = (lane64 // 64 - iy // 4).astype(F32)
        gap_x = apart + flat[at_l3 : at_l3 + 1] - flat[at_rxy : at_rxy + 64]
        gap_y = side + flat[at_l3 + 1 : at_l3 + 2] - flat[at_rxy + 64 : at_rxy + 128]
        adjacent = jnp.maximum(jnp.abs(side), jnp.abs(apart)) <= 1.0
        plane = gap_x * gap_x + gap_y * gap_y
        at = pl.ds(pl.multiple_of(j * 128, 128), 128)
        for i in range(3):
            value = lax.rsqrt(plane + jnp.concatenate([flat[at_z2 + 8 * i + 16 : at_z2 + 8 * i + 24]] * 8, 0))
            value = jnp.where(adjacent, 0.0, value)
            hi, lo = pair_split(value)
            table3[64 * i : 64 * i + 64, at] = hi
            table3[192 + 64 * i : 256 + 64 * i, at] = lo

    pl.loop(0, 8)(table_tile)

    def basis(column, k, level=0, col=None):
        places = [halo[column, comp, k : k + 1, :] for comp in range(3)]
        if level:
            size = 2**level
            corner = (
                ((2 * ix + col // 2) % size).astype(F32),
                ((2 * iy + col % 2) % size).astype(F32),
                (2 * k) % size + (lane[:1] // 64).astype(F32),
            )
            places = [(place + at) * (1.0 / size) for place, at in zip(places, corner)]
        x, y, z = (2.0 * place - 1.0 for place in places)

        def poly(i, u):
            p = [flat[32 * i + 8 * e : 32 * i + 8 * e + 8] for e in range(4)]
            return ((p[3] * u + p[2]) * u + p[1]) * u + p[0]

        along_z = poly(0, z)
        low, high = poly(1, y) * along_z, poly(2, y) * along_z
        pieces = []
        for a in range(4):
            s = ((float(c[3, a]) * x + float(c[2, a])) * x + float(c[1, a])) * x + float(c[0, a])
            pieces += [s * low, s * high]
        return jnp.concatenate(pieces, 0)

    def column_of(cx, cy):
        return (1 + cx) * 4 + 1 + cy

    for load in loads[:2]:
        load.wait()
    for cx in range(2):
        for cy in range(2):
            for k in range(8):
                at = slice(128 * k, 128 * k + 128)
                for comp in range(3):
                    halo[column_of(cx, cy), comp, k : k + 1] = off_ref[comp, cx, cy : cy + 1, at]
                halo[column_of(cx, cy), 3, k : k + 1] = charge_ref[cx, cy : cy + 1, at]
    ROW, HALO, LEAF, LINE, SECOND, THIRD = range(6)
    buffers = (near_rows, halo, moments, rows, seconds, thirds)
    counts = (count_y - 1, 12, 8, len(ROWS) + 1, len(WIDER), count_x - 1)

    def send(kind, index, at, dx, dy):
        buffer = buffers[kind]
        sems = (send_s.at[kind], recv_s.at[kind])
        remote(buffer.at[index], buffer.at[at], *sems, dx, dy).start()

    def all_of(kind):
        part = buffers[kind].at[pl.ds(0, counts[kind])]
        return remote(part, part, send_s.at[kind], recv_s.at[kind], 1, 1)

    half_row = lax.broadcasted_iota(jnp.int32, (128, 128), 0) // 64
    half_lane = lax.broadcasted_iota(jnp.int32, (128, 128), 1)
    parity = (half_row == half_lane % 2).astype(F32).astype(BF16)
    halves = (half_row == half_lane // 64).astype(F32).astype(BF16)
    leaf[...] = jnp.zeros((64, 128), F32)

    @pl.loop(0, 4, unroll=True)
    def _(col):
        column = (1 + col // 2) * 4 + 1 + col % 2
        for k in range(8):
            value = basis(column, k)
            bases[0, 8 * col + k] = value
            value = value * halo[column, 3, k : k + 1, :]
            hi, lo = pair_split(value)
            bq[col, 64 * k : 64 * k + 64] = hi
            bq[col, 512 + 64 * k : 576 + 64 * k] = lo
        summed = dot(bq[col], parity)
        total = leaf[...]
        for k in range(8):
            here = (lane64 % 64) // 2 == col * 8 + k
            total = jnp.where(
                here,
                summed[64 * k : 64 * k + 64] + summed[512 + 64 * k : 576 + 64 * k],
                total,
            )
        leaf[...] = total

    for load in loads[2:]:
        load.wait()
    own = leaf[...]
    moments[4] = jnp.where(lane64[:32] < 64, own[:32], own[32:])
    stacked = jnp.concatenate(
        [own] + [pltpu.roll(own, 128 - 16 * col, 1) for col in range(1, 4)], 0
    )
    first = folded(dot(uf_ref[...], wide(stacked)), 128)
    first = first[:64] + pltpu.roll(first[64:], 127, 1)
    first = jnp.where((lane64 < 16) & (lane64 % 2 == 0), first, 0.0)
    packet = first[:8]
    for g in range(1, 8):
        packet = packet + pltpu.roll(first[8 * g : 8 * g + 8], 16 * g, 1)
    near_rows[iy] = packet

    pl.semaphore_wait(barrier, len(DIRS) + count_y - 1 + count_x - 1)
    for k in range(1, count_y):
        send(ROW, iy, iy, 0, k)
    for ox, oy in DIRS:
        take_x = {1: [2], -1: [1], 0: [1, 2]}[ox]
        put_x = {1: [0], -1: [3], 0: [1, 2]}[ox]
        take_y = {1: (2, 1), -1: (1, 1), 0: (1, 2)}[oy]
        put_y = {1: 0, -1: 3, 0: 1}[oy]
        for a, b in zip(take_x, put_x):
            at = (pl.ds(a * 4 + take_y[0], take_y[1]), pl.ds(b * 4 + put_y, take_y[1]))
            send(HALO, *at, ox, oy)
    for ox, oy in DIRS:
        send(LEAF, 4, (1 - ox) * 3 + 1 - oy, ox, oy)

    pl.loop(8, TILES)(table_tile)

    @pl.loop(0, 4, unroll=True)
    def _(col):
        column = (1 + col // 2) * 4 + 1 + col % 2
        for level in range(1, 4):
            for k in range(8):
                bases[level, 8 * col + k] = basis(column, k, level, col)

    first_term = (sub == 0) | (sub == 1) | (sub == 3)
    second_term = (sub == 2) | (sub == 4)
    half = (lane // 64).astype(F32)

    def three(value):
        a = value.astype(BF16).astype(F32)
        rest = value - a
        b = rest.astype(BF16).astype(F32)
        return [a, b, rest - b]

    def features(column, wx, wy, both):
        x = halo[column, 0] + (wx - 1.0)
        y = halo[column, 1] + (wy - 1.0)
        z = halo[column, 2] + (half - 1.0)
        plane = x * x + y * y
        parts = three(x) + three(y) + three(z) + three(plane + z * z)
        if both:
            beside = z + (2.0 - 4.0 * half)
            parts += three(beside) + three(plane + beside * beside)
        for i, part in enumerate(parts):
            pieces[column, i] = part

    def spread(column, i, k):
        return jnp.broadcast_to(pieces[column, i, k : k + 1], (8, 128))

    def chosen(column, i, k, six, seven, terms):
        a, b, c = (spread(column, i + e, k) for e in range(3))
        value = jnp.where(terms[0], a, jnp.where(terms[1], b, c))
        return jnp.where(sub == 6, six, jnp.where(sub == 7, seven, value))

    zero8 = jnp.zeros((8, 128), F32)
    one8 = jnp.ones((8, 128), F32)
    t_terms = ((sub == 0) | (sub == 2) | (sub == 5), (sub == 1) | (sub == 4))
    s_terms = (first_term, second_term)
    scale8 = jnp.where(sub < 6, -2.0, 1.0)

    @pl.loop(0, 4, unroll=True)
    def _(col):
        cx, cy = col // 2, col % 2
        column = (1 + cx) * 4 + 1 + cy
        features(column, cx.astype(F32), cy.astype(F32), False)
        for k in range(0, 8, 2):
            turned = []
            for e in (k, k + 1):
                tiles = [
                    chosen(column, 0, e, one8, one8, t_terms),
                    chosen(column, 3, e, one8, spread(column, 9, e), t_terms),
                    chosen(column, 6, e, spread(column, 10, e), spread(column, 11, e), t_terms),
                ]
                tiles = jnp.concatenate([t * scale8 for t in tiles] + [zero8], 0)
                turned.append((tiles, pltpu.roll(tiles, 64, 1)))
            lane32 = lane64[:32] < 64
            upper = jnp.where(lane32, turned[0][0], turned[1][1])
            lower = jnp.where(lane32, turned[0][1], turned[1][0])
            stack = jnp.concatenate([upper, lower], 0).T.astype(BF16)
            target[col * 8 + k] = stack[:64]
            target[col * 8 + k + 1] = stack[64:]

    outside = jnp.where(lax.broadcasted_iota(jnp.int32, (32, 128), 0) == 6, 16384.0, 0.0)
    lane32 = lane64[:32] < 64
    left_half = lane32
    outside_low = jnp.where(left_half, outside, 0.0).astype(BF16)
    outside_high = jnp.where(left_half, 0.0, outside).astype(BF16)

    def source_column(column):
        wx, wy = column // 4, column % 4
        features(column, wx.astype(F32) - 1.0, wy.astype(F32) - 1.0, True)
        at_x, at_y = 2 * ix + wx - 1, 2 * iy + wy - 1
        inside = (at_x >= 0) & (at_x < 2 * count_x) & (at_y >= 0) & (at_y < 2 * count_y)
        q = halo[column, 3] * inside.astype(F32)
        after = jnp.where(sub == 7, 0.0, pltpu.roll(q, 7, 0))
        before = jnp.where(sub == 0, 0.0, pltpu.roll(q, 1, 0))
        charge[column, 0] = jnp.where(lane < 64, q, before)
        charge[column, 1] = q
        charge[column, 2] = jnp.where(lane < 64, after, q)
        source[column, 9, 2] = outside_low
        source[column, 0, 3] = outside_high
        for k in range(8):
            own_tiles = [
                chosen(column, 0, k, spread(column, 9, k), spread(column, 10, k), s_terms),
                chosen(column, 3, k, spread(column, 11, k), one8, s_terms),
                chosen(column, 6, k, one8, one8, s_terms),
                zero8,
            ]
            beside_tiles = [
                jnp.where(sub == 6, spread(column, 15, k), jnp.where(sub == 7, spread(column, 16, k), own_tiles[0])),
                jnp.where(sub == 6, spread(column, 17, k), own_tiles[1]),
                chosen(column, 12, k, one8, one8, s_terms),
                zero8,
            ]
            for e, tiles in enumerate((own_tiles, beside_tiles)):
                tiles = jnp.concatenate(tiles, 0)
                source[column, k + 1, 2 * e] = jnp.where(left_half, tiles, 0.0).astype(BF16)
                source[column, k + 1, 2 * e + 1] = jnp.where(left_half, 0.0, tiles).astype(BF16)

    def near_sum(mine, k, columns, own):
        straight = jnp.zeros((64, 128), F32)
        crossed = jnp.zeros((64, 128), F32)

        def side(column, a, b):
            return jnp.concatenate([source[column, a[0], a[1]], source[column, b[0], b[1]]], 0)

        def row_of(column, dz):
            return charge[column, dz, pl.ds(k, 1), :]

        for column in columns:
            above = side(column, (k + 1, 1), (k + 2, 2))
            below = side(column, (k, 3), (k + 1, 0))
            inverse = lax.rsqrt(dot(mine, jnp.concatenate([above, below], 1)))
            crossed = crossed + inverse[:, :128] * row_of(column, 2)
            crossed = crossed + inverse[:, 128:] * row_of(column, 0)
        for i in range(0, len(columns), 2):
            group = columns[i : i + 2]
            both = [side(column, (k + 1, 0), (k + 1, 1)) for column in group]
            inverse = lax.rsqrt(dot(mine, jnp.concatenate(both, 1)))
            for e, column in enumerate(group):
                value = inverse[:, 128 * e : 128 * e + 128]
                if own and i + e == 0:
                    value = jnp.where(eye, 0.0, value)
                straight = straight + value * row_of(column, 1)
        return straight + pltpu.roll(crossed, 64, 1)

    @pl.loop(0, 4, unroll=True)
    def _(col):
        source_column((1 + col // 2) * 4 + 1 + col % 2)

    def inner_block(block, carry):
        col, k = block // 8, block % 8
        cx, cy = col // 2, col % 2
        columns = [(1 + a) * 4 + 1 + b for a in (cx, 1 - cx) for b in (cy, 1 - cy)]
        sums[block] = near_sum(target[block], k, columns, True)
        return carry

    lax.fori_loop(0, 32, inner_block, 0, unroll=16)

    all_of(ROW).wait_recv()
    packets = [near_rows[k] for k in range(count_y)]
    full = []
    for g in range(8):
        tile = jnp.zeros((8, 128), F32)
        for k in range(count_y):
            moved = pltpu.roll(packets[k], 16 * (k - g) % 128, 1) if k != g else packets[k]
            tile = jnp.where(lane // 16 == k, moved, tile)
        full.append(tile)
    full = jnp.concatenate(full, 0)
    rows[ix] = full[:32] + pltpu.roll(full[32:], 1, 1)

    def part(source, which, step_z, step_y):
        o = folded(dot(u2_ref[which], wide(source)), 256)
        return (
            o[:64]
            + pltpu.roll(o[64:128], 128 - step_z, 1)
            + pltpu.roll(o[128:192], 128 - step_y, 1)
            + pltpu.roll(o[192:], 128 - step_z - step_y, 1)
        )

    second = part(full, ix % 2, 2, 16)
    second = jnp.where((lane64 // 16 % 2 == 0) & (lane64 % 4 == 0), second, 0.0)
    third = part(second, ix // 2 % 2, 4, 32)
    third = jnp.where((lane64 // 16 % 4 == 0) & (lane64 % 8 == 0), third, 0.0)
    packed = second[:8]
    for g in range(1, 8):
        packed = packed + pltpu.roll(second[8 * g : 8 * g + 8], g % 4 + 16 * (g // 4), 1)
    seconds[ix] = packed
    packed = third[:8]
    for g in range(1, 8):
        packed = packed + pltpu.roll(third[8 * g : 8 * g + 8], g, 1)
    pair = packed[:2]
    for e in range(1, 4):
        pair = pair + pltpu.roll(packed[2 * e : 2 * e + 2], 16 * e, 1)
    thirds[ix] = pair

    for k in range(1, count_x):
        send(THIRD, ix, ix, k, 0)
    for dx in WIDER:
        send(SECOND, ix, ix, dx, 0)
    for dx in ROWS:
        send(LINE, ix, ix, dx, 0)
    send(LINE, ix, ix, 3 - 6 * (ix % 2), 0)

    all_of(HALO).wait_recv()


    @pl.loop(0, 4, unroll=True)
    def _(e):
        for column in (e, 12 + e):
            source_column(column)

    @pl.loop(0, 2, unroll=True)
    def _(e):
        for column in (4, 7):
            source_column(column + 4 * e)

    def outer_block(block, carry):
        col, k = block // 8, block % 8
        cx, cy = col // 2, col % 2
        columns = [12 * cx + cy + b for b in range(3)] + [4 + 3 * cy, 8 + 3 * cy]
        sums[block] = sums[block] + near_sum(target[block], k, columns, False)
        return carry

    lax.fori_loop(0, 32, outer_block, 0, unroll=16)

    @pl.loop(0, 4, unroll=True)
    def _(col):
        value = sums[pl.ds(pl.multiple_of(col * 8, 8), 8)].reshape(512, 128)
        hi, lo = pair_split(value)
        value = dot(hi, halves) + dot(lo, halves)
        for k in range(8):
            mine = jnp.where(eye, value[64 * k : 64 * k + 64], 0.0)
            near[col, k : k + 1] = jnp.sum(mine, 0, keepdims=True)

    all_of(LEAF).wait_recv()
    plain = {}
    for ox in (-1, 0, 1):
        for oy in (-1, 0, 1):
            value = moments[(ox + 1) * 3 + oy + 1]
            turned = pltpu.roll(value, 64, 1)
            lane32 = lane64[:32]
            value = jnp.concatenate(
                [jnp.where(lane32 < 64, value, turned), jnp.where(lane32 < 64, turned, value)], 0
            )
            scale = F32(1.0)
            if ox:
                scale = scale * (ix > 0 if ox < 0 else ix < count_x - 1).astype(F32)
            if oy:
                scale = scale * (iy > 0 if oy < 0 else iy < count_y - 1).astype(F32)
            plain[ox, oy] = value * scale
    by_x = lane64 // 32 % 2
    by_y = lane64 // 16 % 2

    def swap_y(value):
        return jnp.where(by_y == 0, pltpu.roll(value, 112, 1), pltpu.roll(value, 16, 1))

    def leaf_block(dx, dy):
        result = None
        for cx in range(2):
            for cy in range(2):
                ox, oy = (cx + dx) // 2, (cy + dy) // 2
                if abs(ox) > 1 or abs(oy) > 1:
                    continue
                value = plain[ox, oy]
                if dy % 2:
                    value = swap_y(value)
                if dx % 2:
                    value = pltpu.roll(value, 32, 1)
                mine = (by_x == cx) & (by_y == cy)
                value = jnp.where(mine, value, 0.0)
                result = value if result is None else result + value
        return result

    for dx in range(-3, 4):
        for dy in range(-3, 4):
            value = leaf_block(dx, dy)
            high = value.astype(BF16).astype(F32)
            at = ((dx + 3) * 7 + dy + 3) * 64
            right[at : at + 64] = jnp.where(lane64 < 64, high, value - high).astype(BF16)
    right[49 * 64 : 50 * 64] = jnp.zeros((64, 128), BF16)

    product[...] = dot(table[...], right[...])

    def shifted(i, fold, levels):
        o = product[64 * i : 64 * i + 64] + product[448 + 64 * i : 512 + 64 * i]
        o = o + pltpu.roll(o, fold, 1)
        total = jnp.zeros((64, 128), F32)
        for level in levels:
            value = o if i == 3 else pltpu.roll(o, (-(i - 3) * 2**level) % 128, 1)
            total = total + value * flat[at_w + 8 * level + i : at_w + 8 * level + i + 1]
        return total

    far = shifted(0, 64, (0,))
    for i in range(1, 7):
        far = far + shifted(i, 64, (0,))
    leaf[...] = far

    @pl.loop(0, 4, unroll=True)
    def _(col):
        here = pltpu.roll(leaf[...], (128 - 16 * col) % 128, 1)
        for k in range(8):
            spread = jnp.where(
                lane64 < 64,
                jnp.broadcast_to(here[:, 2 * k : 2 * k + 1], (64, 128)),
                jnp.broadcast_to(here[:, 2 * k + 1 : 2 * k + 2], (64, 128)),
            )
            both = jnp.sum(bases[0, 8 * col + k] * spread, 0, keepdims=True)
            near[col, k : k + 1] = near[col, k : k + 1] + both

    for kind in (LINE, SECOND):
        all_of(kind).wait_recv()
    def within(value, count, step, odd):
        ok = (value >= 0) & (value < count)
        if step == 3:
            ok = ok & (odd == 0)
        if step == -3:
            ok = ok & (odd == 1)
        return ok.astype(F32)

    for dx in range(-3, 4):
        step = {3: 3 * (1 - ix % 2), -3: -3 * (ix % 2)}.get(dx, dx)
        line = rows[lax.rem(ix + step + count_x, count_x)]
        line = jnp.concatenate([line, pltpu.roll(line, 127, 1)], 0)
        line = pltpu.roll(line, lax.rem(128 - 16 * iy, 128), 1)
        line = line * within(ix + dx, count_x, dx, ix % 2)
        x2 = ix // 2 + dx
        base = lax.rem(2 * x2 + 2 * count_x, count_x)
        pair = seconds[base] + seconds[base + 1]
        pair = pltpu.roll(pair, lax.rem(144 - 32 * (iy // 2), 128), 1)
        pair = [pltpu.roll(pair, (-(g % 4) - 16 * (g // 4)) % 128, 1) if g else pair for g in range(8)]
        pair = jnp.concatenate(pair, 0)
        pair = pair * within(x2, count_x // 2, dx, ix // 2 % 2)
        for dy in range(-3, 4):
            one = pltpu.roll(line, (-16 * dy) % 128, 1) * within(iy + dy, count_y, dy, iy % 2)
            two = pltpu.roll(pair, (-32 * dy) % 128, 1)
            two = two * within(iy // 2 + dy, count_y // 2, dy, iy // 2 % 2)
            value = jnp.where(lane64 < 16, one, two)
            high = value.astype(BF16).astype(F32)
            low = jnp.where(lane64 < 64, pltpu.roll(value - high, 32, 1), 0.0)
            at = ((dx + 3) * 7 + dy + 3) * 64
            right[at : at + 64] = jnp.where(lane64 < 32, high, low).astype(BF16)

    product[...] = dot(table[...], right[...])

    far12 = shifted(0, 96, (1, 2))
    for i in range(1, 7):
        far12 = far12 + shifted(i, 96, (1, 2))

    all_of(THIRD).wait_recv()
    for j in range(count_x // 4):
        group = thirds[4 * j] + thirds[4 * j + 1] + thirds[4 * j + 2] + thirds[4 * j + 3]
        group = jnp.concatenate([group] + [pltpu.roll(group, 128 - 16 * e, 1) for e in range(1, 4)], 0)
        third = [group] + [pltpu.roll(group, 128 - g, 1) for g in range(1, 8)]
        third = jnp.concatenate(third, 0)
        right3[128 * j : 128 * j + 64] = wide(third)
        right3[128 * j + 64 : 128 * j + 128] = wide(pltpu.roll(third, 64, 1))
    o = folded(dot(table3[...], right3[...]), 192)
    local = o[64:128]
    local = local + jnp.where(lane64 == 0, pltpu.roll(o[128:], 120, 1), 0.0)
    local = local + jnp.where(lane64 == 8, pltpu.roll(o[:64], 8, 1), 0.0)
    local3 = jnp.where((lane64 < 16) & (lane64 % 8 == 0), 0.125 * local, 0.0)

    def column(value, at):
        return jnp.broadcast_to(value[:, at : at + 1], (64, 128))

    for k in range(8):
        if k % 4 == 0:
            high3 = column(local3, 2 * k)
        if k % 2 == 0:
            high2 = column(far12, 16 + 2 * k)
        high1 = column(far12, 2 * k)
        for col in range(4):
            block = 8 * col + k
            both = bases[1, block] * high1 + bases[2, block] * high2 + bases[3, block] * high3
            both = jnp.sum(both, 0, keepdims=True) + near[col, k : k + 1]
            out_ref[col // 2, col % 2 : col % 2 + 1, 128 * k : 128 * k + 128] = both

    for kind in range(6):
        all_of(kind).wait_send()


def solution(mesh):
    count_x, count_y = mesh.shape["gx"], mesh.shape["gy"]
    fixed = constants()
    vmem = pl.BlockSpec(memory_space=pltpu.VMEM)
    hbm = pl.BlockSpec(memory_space=pltpu.HBM)
    dma = pltpu.SemaphoreType.DMA
    call = pl.pallas_call(
        functools.partial(kernel, count_x, count_y),
        out_shape=jax.ShapeDtypeStruct((2, 2, 1024), F32),
        in_specs=[hbm] * (2 + len(fixed)),
        out_specs=vmem,
        scratch_shapes=[
            pltpu.VMEM((3, 2, 2, 1024), F32),
            pltpu.VMEM((2, 2, 1024), F32),
            pltpu.VMEM((96 + 128 + 56 + 24 + 8, 128), F32),
            pltpu.VMEM(fixed[0].shape, BF16),
            pltpu.VMEM(fixed[1].shape, BF16),
            pltpu.VMEM((16, 4, 8, 128), F32),
            pltpu.VMEM((9, 32, 128), F32),
            pltpu.VMEM((count_y, 8, 128), F32),
            pltpu.VMEM((count_x, 32, 128), F32),
            pltpu.VMEM((count_x, 8, 128), F32),
            pltpu.VMEM((count_x, 2, 128), F32),
            pltpu.VMEM((16, 18, 8, 128), F32),
            pltpu.VMEM((16, 10, 4, 32, 128), BF16),
            pltpu.VMEM((16, 3, 8, 128), F32),
            pltpu.VMEM((32, 64, 64), BF16),
            pltpu.VMEM((32, 64, 128), F32),
            pltpu.VMEM((4, 8, 128), F32),
            pltpu.VMEM((896, TILES * 128), BF16),
            pltpu.VMEM((384, count_x // 4 * 128), BF16),
            pltpu.VMEM((TILES * 128, 128), BF16),
            pltpu.VMEM((count_x // 4 * 128, 256), BF16),
            pltpu.VMEM((896, 128), F32),
            pltpu.VMEM((4, 1024, 128), BF16),
            pltpu.VMEM((64, 128), F32),
            pltpu.VMEM((4, 32, 64, 128), F32),
            dma((4,)),
            dma((6,)),
            dma((6,)),
        ],
        compiler_params=pltpu.CompilerParams(
            collective_id=0, has_side_effects=True, vmem_limit_bytes=64 << 20
        ),
    )

    def body(offsets, charges):
        return call(offsets, charges, *fixed)

    in_specs = (P(None, "gx", "gy", None), P("gx", "gy", None))
    out_specs = P("gx", "gy", None)
    return jax.shard_map(body, mesh=mesh, in_specs=in_specs, out_specs=out_specs, check_vma=False)
```

```python
import functools

import jax
import jax.numpy as jnp
import ml_dtypes
import numpy as np
from jax import lax
from jax.experimental import pallas as pl
from jax.experimental.pallas import tpu as pltpu
from jax.sharding import PartitionSpec as P

MESH = pl.DeviceIdType.MESH
F32 = jnp.float32
BF16 = jnp.bfloat16
DIRS = [(ox, oy) for ox in (-1, 0, 1) for oy in (-1, 0, 1) if (ox, oy) != (0, 0)]
ROWS = (2, -2, 1, -1)
WIDER = (4, -4, 3, -3, 5, -5, 2, -2, 6, -6, 1, -1, 7, -7)
TILES = 25


def hops(k):
    return min(k % 8, 8 - k % 8) + min(k // 8, 4 - k // 8)


def nodes():
    return np.cos((2.0 * np.arange(4) + 1.0) * np.pi / 8.0)


def cubic():
    t = nodes()
    t2, t3 = 2 * t * t - 1, 4 * t**3 - 3 * t
    return np.stack([0.25 - 0.5 * t2, 0.5 * t - 1.5 * t3, t2, 2 * t3])


def split(x):
    hi = x.astype(ml_dtypes.bfloat16)
    lo = (x - hi.astype(np.float64)).astype(ml_dtypes.bfloat16)
    return hi, lo


def constants():
    t = nodes()
    c = cubic()
    shifted = (t[None, :] + 2.0 * np.arange(2)[:, None] - 1.0) / 2.0
    f = sum(c[k][None, None, :] * shifted[:, :, None] ** k for k in range(4))
    up = np.einsum("xia,yjb,zkc->xyzijkabc", f, f, f).reshape(2, 2, 2, 64, 64)
    uf = up.transpose(2, 4, 0, 1, 3).reshape(128, 256)
    uf = np.concatenate(split(uf), 0)
    u2 = up.transpose(0, 1, 2, 4, 3).reshape(2, 256, 64)
    u2 = np.concatenate(split(u2), 1)
    return [uf, u2]


def pair_split(x):
    hi = x.astype(BF16)
    lo = (x - hi.astype(F32)).astype(BF16)
    return hi, lo


def wide(x):
    return jnp.concatenate(pair_split(x), 1)


def folded(product, rows):
    return product[:rows, :128] + product[:rows, 128:] + product[rows:, :128] + product[rows:, 128:]


def dot(left, right):
    return jnp.dot(left, right, preferred_element_type=F32)


def kernel(
    count_x, count_y,
    off_hbm, charge_hbm, uf_hbm, u2_hbm,
    out_ref,
    off_ref, charge_ref, flat, uf_ref, u2_ref,
    halo, moments, near_rows, rows, seconds, thirds, pieces, source, charge, target, sums, near,
    table, table3, right, right3, product, bq, leaf, bases,
    load_s, send_s, recv_s,
):
    loads = [
        pltpu.make_async_copy(src, dst, load_s.at[i])
        for i, (src, dst) in enumerate(
            [(off_hbm, off_ref), (charge_hbm, charge_ref)]
            + [(uf_hbm, uf_ref), (u2_hbm, u2_ref)]
        )
    ]
    for load in loads:
        load.start()
    at_rxy = 96
    at_z2 = at_rxy + 128
    at_w = at_z2 + 56
    at_l3 = at_w + 24
    ix = lax.axis_index("gx")
    iy = lax.axis_index("gy")
    lane = lax.broadcasted_iota(jnp.int32, (8, 128), 1)
    lane64 = lax.broadcasted_iota(jnp.int32, (64, 128), 1)
    row64 = lax.broadcasted_iota(jnp.int32, (64, 128), 0)
    eye = row64 == lane64 % 64
    sub = lax.broadcasted_iota(jnp.int32, (8, 128), 0)
    c = cubic()
    t = nodes()

    def pick(index, values):
        result = jnp.full(index.shape, float(values[3]), F32)
        for e in (2, 1, 0):
            result = jnp.where(index == e, float(values[e]), result)
        return result

    for i, index in enumerate((sub % 4, sub // 4, 2 + sub // 4)):
        for e in range(4):
            flat[32 * i + 8 * e : 32 * i + 8 * e + 8] = pick(index, c[e])
    flat[at_rxy : at_rxy + 64] = 0.5 * pick(row64 // 16, t)
    flat[at_rxy + 64 : at_rxy + 128] = 0.5 * pick(row64 // 4 % 4, t)
    gap_z = 0.5 * (pick(lane % 4, t) - pick(sub % 4, t))
    for i in range(7):
        gap = gap_z + (i - 3.0)
        flat[at_z2 + 8 * i : at_z2 + 8 * i + 8] = gap * gap
    for level, start, length in ((0, 0, 64), (1, 0, 16), (2, 16, 16)):
        z = lane % 16
        seen = z + (sub - 3) * 2**level
        odd = (z // 2**level) % 2
        ok = (z % 2**level == 0) & (seen >= 0) & (seen < 16) & (sub < 7)
        ok = ok & (lane >= start) & (lane < start + length)
        ok = ok & ((sub < 6) | (odd == 0)) & ((sub > 0) | (odd == 1))
        flat[at_w + 8 * level : at_w + 8 * level + 8] = jnp.where(ok, 0.5**level, 0.0)
    lane_x = 0.5 * pick(lane % 64 // 16, t)
    lane_y = 0.5 * pick(lane // 4 % 4, t)
    flat[at_l3 : at_l3 + 8] = jnp.where(sub == 0, lane_x, lane_y)

    def remote(src, dst, send, recv, dx, dy):
        device = (lax.rem(ix + dx + count_x, count_x), lax.rem(iy + dy + count_y, count_y))
        return pltpu.make_async_remote_copy(
            src_ref=src, dst_ref=dst, send_sem=send, recv_sem=recv,
            device_id=device, device_id_type=MESH,
        )

    barrier = pltpu.get_barrier_semaphore()

    def greet(dx, dy):
        device = (lax.rem(ix + dx + count_x, count_x), lax.rem(iy + dy + count_y, count_y))
        pl.semaphore_signal(barrier, inc=1, device_id=device, device_id_type=MESH)

    for ox, oy in DIRS:
        greet(ox, oy)

    for k in range(1, count_y):
        greet(0, k)
    for k in range(1, count_x):
        greet(k, 0)

    def table_tile(j):
        dx = [(2 * j + e) // 7 - 3 for e in range(2)]
        dy = [(2 * j + e) % 7 - 3 for e in range(2)]
        dx, dy = (jnp.where(lane < 64, v[0], v[1]).astype(F32) for v in (dx, dy))
        gap_x = (dx + lane_x)[:1] - flat[at_rxy : at_rxy + 64]
        gap_y = (dy + lane_y)[:1] - flat[at_rxy + 64 : at_rxy + 128]
        adjacent = jnp.maximum(jnp.abs(dx), jnp.abs(dy))[:1]
        adjacent = jnp.broadcast_to(adjacent, (64, 128)) <= 1.0
        plane = gap_x * gap_x + gap_y * gap_y
        at = pl.ds(pl.multiple_of(j * 128, 128), 128)
        for i in range(7):
            value = lax.rsqrt(plane + jnp.concatenate([flat[at_z2 + 8 * i : at_z2 + 8 * i + 8]] * 8, 0))
            if i in (2, 3, 4):
                value = jnp.where(adjacent, 0.0, value)
            hi, lo = pair_split(value)
            table[64 * i : 64 * i + 64, at] = hi
            table[448 + 64 * i : 512 + 64 * i, at] = lo

    @pl.loop(0, count_x // 4)
    def _(j):
        apart = (j - ix // 4).astype(F32)
        side = (lane64 // 64 - iy // 4).astype(F32)
        gap_x = apart + flat[at_l3 : at_l3 + 1] - flat[at_rxy : at_rxy + 64]
        gap_y = side + flat[at_l3 + 1 : at_l3 + 2] - flat[at_rxy + 64 : at_rxy + 128]
        adjacent = jnp.maximum(jnp.abs(side), jnp.abs(apart)) <= 1.0
        plane = gap_x * gap_x + gap_y * gap_y
        at = pl.ds(pl.multiple_of(j * 128, 128), 128)
        for i in range(3):
            value = lax.rsqrt(plane + jnp.concatenate([flat[at_z2 + 8 * i + 16 : at_z2 + 8 * i + 24]] * 8, 0))
            value = jnp.where(adjacent, 0.0, value)
            hi, lo = pair_split(value)
            table3[64 * i : 64 * i + 64, at] = hi
            table3[192 + 64 * i : 256 + 64 * i, at] = lo

    pl.loop(0, 9)(table_tile)

    def basis(column, k, level=0, col=None):
        places = [halo[column, comp, k : k + 1, :] for comp in range(3)]
        if level:
            size = 2**level
            corner = (
                ((2 * ix + col // 2) % size).astype(F32),
                ((2 * iy + col % 2) % size).astype(F32),
                (2 * k) % size + (lane[:1] // 64).astype(F32),
            )
            places = [(place + at) * (1.0 / size) for place, at in zip(places, corner)]
        x, y, z = (2.0 * place - 1.0 for place in places)

        def poly(i, u):
            p = [flat[32 * i + 8 * e : 32 * i + 8 * e + 8] for e in range(4)]
            return ((p[3] * u + p[2]) * u + p[1]) * u + p[0]

        along_z = poly(0, z)
        low, high = poly(1, y) * along_z, poly(2, y) * along_z
        pieces = []
        for a in range(4):
            s = ((float(c[3, a]) * x + float(c[2, a])) * x + float(c[1, a])) * x + float(c[0, a])
            pieces += [s * low, s * high]
        return jnp.concatenate(pieces, 0)

    def column_of(cx, cy):
        return (1 + cx) * 4 + 1 + cy

    for load in loads[:2]:
        load.wait()
    for cx in range(2):
        for cy in range(2):
            for k in range(8):
                at = slice(128 * k, 128 * k + 128)
                for comp in range(3):
                    halo[column_of(cx, cy), comp, k : k + 1] = off_ref[comp, cx, cy : cy + 1, at]
                halo[column_of(cx, cy), 3, k : k + 1] = charge_ref[cx, cy : cy + 1, at]
    ROW, HALO, LEAF, LINE, SECOND, THIRD = range(6)
    buffers = (near_rows, halo, moments, rows, seconds, thirds)
    counts = (count_y - 1, 12, 8, len(ROWS) + 1, len(WIDER), count_x - 1)

    def send(kind, index, at, dx, dy):
        buffer = buffers[kind]
        sems = (send_s.at[kind], recv_s.at[kind])
        remote(buffer.at[index], buffer.at[at], *sems, dx, dy).start()

    def all_of(kind):
        part = buffers[kind].at[pl.ds(0, counts[kind])]
        return remote(part, part, send_s.at[kind], recv_s.at[kind], 1, 1)

    half_row = lax.broadcasted_iota(jnp.int32, (128, 128), 0) // 64
    half_lane = lax.broadcasted_iota(jnp.int32, (128, 128), 1)
    parity = (half_row == half_lane % 2).astype(F32).astype(BF16)
    halves = (half_row == half_lane // 64).astype(F32).astype(BF16)
    leaf[...] = jnp.zeros((64, 128), F32)

    @pl.loop(0, 4, unroll=True)
    def _(col):
        column = (1 + col // 2) * 4 + 1 + col % 2
        for k in range(8):
            value = basis(column, k)
            bases[0, 8 * col + k] = value
            value = value * halo[column, 3, k : k + 1, :]
            hi, lo = pair_split(value)
            bq[col, 64 * k : 64 * k + 64] = hi
            bq[col, 512 + 64 * k : 576 + 64 * k] = lo
        summed = dot(bq[col], parity)
        total = leaf[...]
        for k in range(8):
            here = (lane64 % 64) // 2 == col * 8 + k
            total = jnp.where(
                here,
                summed[64 * k : 64 * k + 64] + summed[512 + 64 * k : 576 + 64 * k],
                total,
            )
        leaf[...] = total

    for load in loads[2:]:
        load.wait()
    own = leaf[...]
    moments[4] = jnp.where(lane64[:32] < 64, own[:32], own[32:])
    stacked = jnp.concatenate(
        [own] + [pltpu.roll(own, 128 - 16 * col, 1) for col in range(1, 4)], 0
    )
    first = folded(dot(uf_ref[...], wide(stacked)), 128)
    first = first[:64] + pltpu.roll(first[64:], 127, 1)
    first = jnp.where((lane64 < 16) & (lane64 % 2 == 0), first, 0.0)
    packet = first[:8]
    for g in range(1, 8):
        packet = packet + pltpu.roll(first[8 * g : 8 * g + 8], 16 * g, 1)
    near_rows[iy] = packet

    pl.semaphore_wait(barrier, len(DIRS) + count_y - 1 + count_x - 1)
    for k in range(1, count_y):
        send(ROW, iy, iy, 0, k)
    for ox, oy in DIRS:
        take_x = {1: [2], -1: [1], 0: [1, 2]}[ox]
        put_x = {1: [0], -1: [3], 0: [1, 2]}[ox]
        take_y = {1: (2, 1), -1: (1, 1), 0: (1, 2)}[oy]
        put_y = {1: 0, -1: 3, 0: 1}[oy]
        for a, b in zip(take_x, put_x):
            at = (pl.ds(a * 4 + take_y[0], take_y[1]), pl.ds(b * 4 + put_y, take_y[1]))
            send(HALO, *at, ox, oy)
    for ox, oy in DIRS:
        send(LEAF, 4, (1 - ox) * 3 + 1 - oy, ox, oy)

    pl.loop(9, TILES)(table_tile)

    @pl.loop(0, 4, unroll=True)
    def _(col):
        column = (1 + col // 2) * 4 + 1 + col % 2
        for level in range(1, 4):
            for k in range(8):
                bases[level, 8 * col + k] = basis(column, k, level, col)

    first_term = (sub == 0) | (sub == 1) | (sub == 3)
    second_term = (sub == 2) | (sub == 4)
    half = (lane // 64).astype(F32)

    def three(value):
        a = value.astype(BF16).astype(F32)
        rest = value - a
        b = rest.astype(BF16).astype(F32)
        return [a, b, rest - b]

    def features(column, wx, wy, both):
        x = halo[column, 0] + (wx - 1.0)
        y = halo[column, 1] + (wy - 1.0)
        z = halo[column, 2] + (half - 1.0)
        plane = x * x + y * y
        parts = three(x) + three(y) + three(z) + three(plane + z * z)
        if both:
            beside = z + (2.0 - 4.0 * half)
            parts += three(beside) + three(plane + beside * beside)
        for i, part in enumerate(parts):
            pieces[column, i] = part

    def spread(column, i, k):
        return jnp.broadcast_to(pieces[column, i, k : k + 1], (8, 128))

    def chosen(column, i, k, six, seven, terms):
        a, b, c = (spread(column, i + e, k) for e in range(3))
        value = jnp.where(terms[0], a, jnp.where(terms[1], b, c))
        return jnp.where(sub == 6, six, jnp.where(sub == 7, seven, value))

    zero8 = jnp.zeros((8, 128), F32)
    one8 = jnp.ones((8, 128), F32)
    t_terms = ((sub == 0) | (sub == 2) | (sub == 5), (sub == 1) | (sub == 4))
    s_terms = (first_term, second_term)
    scale8 = jnp.where(sub < 6, -2.0, 1.0)

    @pl.loop(0, 4, unroll=True)
    def _(col):
        cx, cy = col // 2, col % 2
        column = (1 + cx) * 4 + 1 + cy
        features(column, cx.astype(F32), cy.astype(F32), False)
        for k in range(0, 8, 2):
            turned = []
            for e in (k, k + 1):
                tiles = [
                    chosen(column, 0, e, one8, one8, t_terms),
                    chosen(column, 3, e, one8, spread(column, 9, e), t_terms),
                    chosen(column, 6, e, spread(column, 10, e), spread(column, 11, e), t_terms),
                ]
                tiles = jnp.concatenate([t * scale8 for t in tiles] + [zero8], 0)
                turned.append((tiles, pltpu.roll(tiles, 64, 1)))
            lane32 = lane64[:32] < 64
            upper = jnp.where(lane32, turned[0][0], turned[1][1])
            lower = jnp.where(lane32, turned[0][1], turned[1][0])
            stack = jnp.concatenate([upper, lower], 0).T.astype(BF16)
            target[col * 8 + k] = stack[:64]
            target[col * 8 + k + 1] = stack[64:]

    outside = jnp.where(lax.broadcasted_iota(jnp.int32, (32, 128), 0) == 6, 16384.0, 0.0)
    lane32 = lane64[:32] < 64
    left_half = lane32
    outside_low = jnp.where(left_half, outside, 0.0).astype(BF16)
    outside_high = jnp.where(left_half, 0.0, outside).astype(BF16)

    def source_column(column):
        wx, wy = column // 4, column % 4
        features(column, wx.astype(F32) - 1.0, wy.astype(F32) - 1.0, True)
        at_x, at_y = 2 * ix + wx - 1, 2 * iy + wy - 1
        inside = (at_x >= 0) & (at_x < 2 * count_x) & (at_y >= 0) & (at_y < 2 * count_y)
        q = halo[column, 3] * inside.astype(F32)
        after = jnp.where(sub == 7, 0.0, pltpu.roll(q, 7, 0))
        before = jnp.where(sub == 0, 0.0, pltpu.roll(q, 1, 0))
        charge[column, 0] = jnp.where(lane < 64, q, before)
        charge[column, 1] = q
        charge[column, 2] = jnp.where(lane < 64, after, q)
        source[column, 9, 2] = outside_low
        source[column, 0, 3] = outside_high
        for k in range(8):
            own_tiles = [
                chosen(column, 0, k, spread(column, 9, k), spread(column, 10, k), s_terms),
                chosen(column, 3, k, spread(column, 11, k), one8, s_terms),
                chosen(column, 6, k, one8, one8, s_terms),
                zero8,
            ]
            beside_tiles = [
                jnp.where(sub == 6, spread(column, 15, k), jnp.where(sub == 7, spread(column, 16, k), own_tiles[0])),
                jnp.where(sub == 6, spread(column, 17, k), own_tiles[1]),
                chosen(column, 12, k, one8, one8, s_terms),
                zero8,
            ]
            for e, tiles in enumerate((own_tiles, beside_tiles)):
                tiles = jnp.concatenate(tiles, 0)
                source[column, k + 1, 2 * e] = jnp.where(left_half, tiles, 0.0).astype(BF16)
                source[column, k + 1, 2 * e + 1] = jnp.where(left_half, 0.0, tiles).astype(BF16)

    def near_sum(mine, k, columns, own):
        straight = jnp.zeros((64, 128), F32)
        crossed = jnp.zeros((64, 128), F32)

        def side(column, a, b):
            return jnp.concatenate([source[column, a[0], a[1]], source[column, b[0], b[1]]], 0)

        def row_of(column, dz):
            return charge[column, dz, pl.ds(k, 1), :]

        for column in columns:
            above = side(column, (k + 1, 1), (k + 2, 2))
            below = side(column, (k, 3), (k + 1, 0))
            inverse = lax.rsqrt(dot(mine, jnp.concatenate([above, below], 1)))
            crossed = crossed + inverse[:, :128] * row_of(column, 2)
            crossed = crossed + inverse[:, 128:] * row_of(column, 0)
        for i in range(0, len(columns), 2):
            group = columns[i : i + 2]
            both = [side(column, (k + 1, 0), (k + 1, 1)) for column in group]
            inverse = lax.rsqrt(dot(mine, jnp.concatenate(both, 1)))
            for e, column in enumerate(group):
                value = inverse[:, 128 * e : 128 * e + 128]
                if own and i + e == 0:
                    value = jnp.where(eye, 0.0, value)
                straight = straight + value * row_of(column, 1)
        return straight + pltpu.roll(crossed, 64, 1)

    @pl.loop(0, 4, unroll=True)
    def _(col):
        source_column((1 + col // 2) * 4 + 1 + col % 2)

    def inner_block(block, carry):
        col, k = block // 8, block % 8
        cx, cy = col // 2, col % 2
        columns = [(1 + a) * 4 + 1 + b for a in (cx, 1 - cx) for b in (cy, 1 - cy)]
        sums[block] = near_sum(target[block], k, columns, True)
        return carry

    lax.fori_loop(0, 32, inner_block, 0, unroll=16)

    all_of(ROW).wait_recv()
    packets = [near_rows[k] for k in range(count_y)]
    full = []
    for g in range(8):
        tile = jnp.zeros((8, 128), F32)
        for k in range(count_y):
            moved = pltpu.roll(packets[k], 16 * (k - g) % 128, 1) if k != g else packets[k]
            tile = jnp.where(lane // 16 == k, moved, tile)
        full.append(tile)
    full = jnp.concatenate(full, 0)
    rows[ix] = full[:32] + pltpu.roll(full[32:], 1, 1)

    def part(source, which, step_z, step_y):
        o = folded(dot(u2_ref[which], wide(source)), 256)
        return (
            o[:64]
            + pltpu.roll(o[64:128], 128 - step_z, 1)
            + pltpu.roll(o[128:192], 128 - step_y, 1)
            + pltpu.roll(o[192:], 128 - step_z - step_y, 1)
        )

    second = part(full, ix % 2, 2, 16)
    second = jnp.where((lane64 // 16 % 2 == 0) & (lane64 % 4 == 0), second, 0.0)
    third = part(second, ix // 2 % 2, 4, 32)
    third = jnp.where((lane64 // 16 % 4 == 0) & (lane64 % 8 == 0), third, 0.0)
    packed = second[:8]
    for g in range(1, 8):
        packed = packed + pltpu.roll(second[8 * g : 8 * g + 8], g % 4 + 16 * (g // 4), 1)
    seconds[ix] = packed
    packed = third[:8]
    for g in range(1, 8):
        packed = packed + pltpu.roll(third[8 * g : 8 * g + 8], g, 1)
    pair = packed[:2]
    for e in range(1, 4):
        pair = pair + pltpu.roll(packed[2 * e : 2 * e + 2], 16 * e, 1)
    thirds[ix] = pair

    for dx in WIDER:
        send(SECOND, ix, ix, dx, 0)
    send(LINE, ix, ix, 3 - 6 * (ix % 2), 0)
    for dx in ROWS:
        send(LINE, ix, ix, dx, 0)
    for k in sorted(range(1, count_x), key=hops, reverse=True):
        send(THIRD, ix, ix, k, 0)

    all_of(HALO).wait_recv()


    @pl.loop(0, 4, unroll=True)
    def _(e):
        for column in (e, 12 + e):
            source_column(column)

    @pl.loop(0, 2, unroll=True)
    def _(e):
        for column in (4, 7):
            source_column(column + 4 * e)

    def outer_block(block, carry):
        col, k = block // 8, block % 8
        cx, cy = col // 2, col % 2
        columns = [12 * cx + cy + b for b in range(3)] + [4 + 3 * cy, 8 + 3 * cy]
        sums[block] = sums[block] + near_sum(target[block], k, columns, False)
        return carry

    lax.fori_loop(0, 32, outer_block, 0, unroll=16)

    @pl.loop(0, 4, unroll=True)
    def _(col):
        value = sums[pl.ds(pl.multiple_of(col * 8, 8), 8)].reshape(512, 128)
        hi, lo = pair_split(value)
        value = dot(hi, halves) + dot(lo, halves)
        for k in range(8):
            mine = jnp.where(eye, value[64 * k : 64 * k + 64], 0.0)
            near[col, k : k + 1] = jnp.sum(mine, 0, keepdims=True)

    all_of(LEAF).wait_recv()
    plain = {}
    for ox in (-1, 0, 1):
        for oy in (-1, 0, 1):
            value = moments[(ox + 1) * 3 + oy + 1]
            turned = pltpu.roll(value, 64, 1)
            lane32 = lane64[:32]
            value = jnp.concatenate(
                [jnp.where(lane32 < 64, value, turned), jnp.where(lane32 < 64, turned, value)], 0
            )
            scale = F32(1.0)
            if ox:
                scale = scale * (ix > 0 if ox < 0 else ix < count_x - 1).astype(F32)
            if oy:
                scale = scale * (iy > 0 if oy < 0 else iy < count_y - 1).astype(F32)
            plain[ox, oy] = value * scale
    by_x = lane64 // 32 % 2
    by_y = lane64 // 16 % 2

    def swap_y(value):
        return jnp.where(by_y == 0, pltpu.roll(value, 112, 1), pltpu.roll(value, 16, 1))

    def leaf_block(dx, dy):
        result = None
        for cx in range(2):
            for cy in range(2):
                ox, oy = (cx + dx) // 2, (cy + dy) // 2
                if abs(ox) > 1 or abs(oy) > 1:
                    continue
                value = plain[ox, oy]
                if dy % 2:
                    value = swap_y(value)
                if dx % 2:
                    value = pltpu.roll(value, 32, 1)
                mine = (by_x == cx) & (by_y == cy)
                value = jnp.where(mine, value, 0.0)
                result = value if result is None else result + value
        return result

    for dx in range(-3, 4):
        for dy in range(-3, 4):
            value = leaf_block(dx, dy)
            high = value.astype(BF16).astype(F32)
            at = ((dx + 3) * 7 + dy + 3) * 64
            right[at : at + 64] = jnp.where(lane64 < 64, high, value - high).astype(BF16)
    right[49 * 64 : 50 * 64] = jnp.zeros((64, 128), BF16)

    product[...] = dot(table[...], right[...])

    def shifted(i, fold, levels):
        o = product[64 * i : 64 * i + 64] + product[448 + 64 * i : 512 + 64 * i]
        o = o + pltpu.roll(o, fold, 1)
        total = jnp.zeros((64, 128), F32)
        for level in levels:
            value = o if i == 3 else pltpu.roll(o, (-(i - 3) * 2**level) % 128, 1)
            total = total + value * flat[at_w + 8 * level + i : at_w + 8 * level + i + 1]
        return total

    far = shifted(0, 64, (0,))
    for i in range(1, 7):
        far = far + shifted(i, 64, (0,))
    leaf[...] = far

    @pl.loop(0, 4, unroll=True)
    def _(col):
        here = pltpu.roll(leaf[...], (128 - 16 * col) % 128, 1)
        for k in range(8):
            spread = jnp.where(
                lane64 < 64,
                jnp.broadcast_to(here[:, 2 * k : 2 * k + 1], (64, 128)),
                jnp.broadcast_to(here[:, 2 * k + 1 : 2 * k + 2], (64, 128)),
            )
            both = jnp.sum(bases[0, 8 * col + k] * spread, 0, keepdims=True)
            near[col, k : k + 1] = near[col, k : k + 1] + both

    for kind in (LINE, SECOND):
        all_of(kind).wait_recv()
    def within(value, count, step, odd):
        ok = (value >= 0) & (value < count)
        if step == 3:
            ok = ok & (odd == 0)
        if step == -3:
            ok = ok & (odd == 1)
        return ok.astype(F32)

    def beside(value, every):
        high = value.astype(BF16).astype(F32)
        return jnp.where(lane64 % every == 0, high, pltpu.roll(value - high, 1, 1))

    valid = []
    for dy in range(-3, 4):
        one = within(iy + dy, count_y, dy, iy % 2)
        two = within(iy // 2 + dy, count_y // 2, dy, iy // 2 % 2)
        valid.append(jnp.where(lane64 < 16, one, jnp.where(lane64 < 32, two, 0.0)))
    for dx in range(-3, 4):
        step = {3: 3 * (1 - ix % 2), -3: -3 * (ix % 2)}.get(dx, dx)
        line = rows[lax.rem(ix + step + count_x, count_x)]
        line = jnp.concatenate([line, pltpu.roll(line, 127, 1)], 0)
        line = beside(line * within(ix + dx, count_x, dx, ix % 2), 2)
        line = pltpu.roll(line, lax.rem(128 - 16 * iy, 128), 1)
        x2 = ix // 2 + dx
        base = lax.rem(2 * x2 + 2 * count_x, count_x)
        pair = (seconds[base] + seconds[base + 1]) * within(x2, count_x // 2, dx, ix // 2 % 2)
        pair = [pltpu.roll(pair, (-(g % 4) - 16 * (g // 4)) % 128, 1) if g else pair for g in range(8)]
        pair = beside(jnp.concatenate(pair, 0), 4)
        pair = pltpu.roll(pair, lax.rem(144 - 32 * (iy // 2), 128), 1)
        for dy in range(-3, 4):
            one = pltpu.roll(line, (-16 * dy) % 128, 1)
            two = pltpu.roll(pair, (-32 * dy) % 128, 1)
            value = jnp.where(lane64 < 16, one, two) * valid[dy + 3]
            at = ((dx + 3) * 7 + dy + 3) * 64
            right[at : at + 64] = value.astype(BF16)

    product[...] = dot(table[...], right[...])

    far12 = shifted(0, 127, (1, 2))
    for i in range(1, 7):
        far12 = far12 + shifted(i, 127, (1, 2))

    all_of(THIRD).wait_recv()
    for j in range(count_x // 4):
        group = thirds[4 * j] + thirds[4 * j + 1] + thirds[4 * j + 2] + thirds[4 * j + 3]
        group = jnp.concatenate([group] + [pltpu.roll(group, 128 - 16 * e, 1) for e in range(1, 4)], 0)
        third = [group] + [pltpu.roll(group, 128 - g, 1) for g in range(1, 8)]
        third = jnp.concatenate(third, 0)
        third = beside(third, 8)
        right3[128 * j : 128 * j + 64] = third.astype(BF16)
        right3[128 * j + 64 : 128 * j + 128] = pltpu.roll(third, 64, 1).astype(BF16)
    o = dot(table3[...], right3[...])
    o = o[:192] + o[192:]
    o = o + pltpu.roll(o, 127, 1)
    local = o[64:128]
    local = local + jnp.where(lane64 == 0, pltpu.roll(o[128:], 120, 1), 0.0)
    local = local + jnp.where(lane64 == 8, pltpu.roll(o[:64], 8, 1), 0.0)
    local3 = jnp.where((lane64 < 16) & (lane64 % 8 == 0), 0.125 * local, 0.0)

    def column(value, at):
        return jnp.broadcast_to(value[:, at : at + 1], (64, 128))

    for k in range(8):
        if k % 4 == 0:
            high3 = column(local3, 2 * k)
        if k % 2 == 0:
            high2 = column(far12, 16 + 2 * k)
        high1 = column(far12, 2 * k)
        for col in range(4):
            block = 8 * col + k
            both = bases[1, block] * high1 + bases[2, block] * high2 + bases[3, block] * high3
            both = jnp.sum(both, 0, keepdims=True) + near[col, k : k + 1]
            out_ref[col // 2, col % 2 : col % 2 + 1, 128 * k : 128 * k + 128] = both

    for kind in range(6):
        all_of(kind).wait_send()


def solution(mesh):
    count_x, count_y = mesh.shape["gx"], mesh.shape["gy"]
    fixed = constants()
    vmem = pl.BlockSpec(memory_space=pltpu.VMEM)
    hbm = pl.BlockSpec(memory_space=pltpu.HBM)
    dma = pltpu.SemaphoreType.DMA
    call = pl.pallas_call(
        functools.partial(kernel, count_x, count_y),
        out_shape=jax.ShapeDtypeStruct((2, 2, 1024), F32),
        in_specs=[hbm] * (2 + len(fixed)),
        out_specs=vmem,
        scratch_shapes=[
            pltpu.VMEM((3, 2, 2, 1024), F32),
            pltpu.VMEM((2, 2, 1024), F32),
            pltpu.VMEM((96 + 128 + 56 + 24 + 8, 128), F32),
            pltpu.VMEM(fixed[0].shape, BF16),
            pltpu.VMEM(fixed[1].shape, BF16),
            pltpu.VMEM((16, 4, 8, 128), F32),
            pltpu.VMEM((9, 32, 128), F32),
            pltpu.VMEM((count_y, 8, 128), F32),
            pltpu.VMEM((count_x, 32, 128), F32),
            pltpu.VMEM((count_x, 8, 128), F32),
            pltpu.VMEM((count_x, 2, 128), F32),
            pltpu.VMEM((16, 18, 8, 128), F32),
            pltpu.VMEM((16, 10, 4, 32, 128), BF16),
            pltpu.VMEM((16, 3, 8, 128), F32),
            pltpu.VMEM((32, 64, 64), BF16),
            pltpu.VMEM((32, 64, 128), F32),
            pltpu.VMEM((4, 8, 128), F32),
            pltpu.VMEM((896, TILES * 128), BF16),
            pltpu.VMEM((384, count_x // 4 * 128), BF16),
            pltpu.VMEM((TILES * 128, 128), BF16),
            pltpu.VMEM((count_x // 4 * 128, 128), BF16),
            pltpu.VMEM((896, 128), F32),
            pltpu.VMEM((4, 1024, 128), BF16),
            pltpu.VMEM((64, 128), F32),
            pltpu.VMEM((4, 32, 64, 128), F32),
            dma((4,)),
            dma((6,)),
            dma((6,)),
        ],
        compiler_params=pltpu.CompilerParams(
            collective_id=0, has_side_effects=True, vmem_limit_bytes=64 << 20
        ),
    )

    def body(offsets, charges):
        return call(offsets, charges, *fixed)

    in_specs = (P(None, "gx", "gy", None), P("gx", "gy", None))
    out_specs = P("gx", "gy", None)
    return jax.shard_map(body, mesh=mesh, in_specs=in_specs, out_specs=out_specs, check_vma=False)
```

```python
import functools

import jax
import jax.numpy as jnp
import ml_dtypes
import numpy as np
from jax import lax
from jax.experimental import pallas as pl
from jax.experimental.pallas import tpu as pltpu
from jax.sharding import PartitionSpec as P

MESH = pl.DeviceIdType.MESH
F32 = jnp.float32
BF16 = jnp.bfloat16
DIRS = [(ox, oy) for ox in (-1, 0, 1) for oy in (-1, 0, 1) if (ox, oy) != (0, 0)]
ROWS = (2, -2, 1, -1)
WIDER = (4, -4, 3, -3, 5, -5, 2, -2, 6, -6, 1, -1, 7, -7)
TILES = 25


def hops(k):
    return min(k % 8, 8 - k % 8) + min(k // 8, 4 - k // 8)


def nodes():
    return np.cos((2.0 * np.arange(4) + 1.0) * np.pi / 8.0)


def cubic():
    t = nodes()
    t2, t3 = 2 * t * t - 1, 4 * t**3 - 3 * t
    return np.stack([0.25 - 0.5 * t2, 0.5 * t - 1.5 * t3, t2, 2 * t3])


def split(x):
    hi = x.astype(ml_dtypes.bfloat16)
    lo = (x - hi.astype(np.float64)).astype(ml_dtypes.bfloat16)
    return hi, lo


def constants():
    t = nodes()
    c = cubic()
    shifted = (t[None, :] + 2.0 * np.arange(2)[:, None] - 1.0) / 2.0
    f = sum(c[k][None, None, :] * shifted[:, :, None] ** k for k in range(4))
    up = np.einsum("xia,yjb,zkc->xyzijkabc", f, f, f).reshape(2, 2, 2, 64, 64)
    uf = up.transpose(2, 4, 0, 1, 3).reshape(128, 256)
    uf = np.concatenate(split(uf), 0)
    u2 = up.transpose(0, 1, 2, 4, 3).reshape(2, 256, 64)
    u2 = np.concatenate(split(u2), 1)
    dn = up.reshape(4, 128, 64)
    dn = np.concatenate(split(dn), 1)
    return [uf, u2, dn]


def pair_split(x):
    hi = x.astype(BF16)
    lo = (x - hi.astype(F32)).astype(BF16)
    return hi, lo


def wide(x):
    return jnp.concatenate(pair_split(x), 1)


def folded(product, rows):
    return product[:rows, :128] + product[:rows, 128:] + product[rows:, :128] + product[rows:, 128:]


def dot(left, right):
    return jnp.dot(left, right, preferred_element_type=F32)


def kernel(
    count_x, count_y,
    off_hbm, charge_hbm, uf_hbm, u2_hbm, dn_hbm,
    out_ref,
    off_ref, charge_ref, flat, uf_ref, u2_ref, dn_ref,
    halo, moments, near_rows, rows, seconds, thirds, pieces, source, charge, target, sums, near,
    table, table3, right, right3, product, bq, leaf, bases,
    load_s, send_s, recv_s,
):
    loads = [
        pltpu.make_async_copy(src, dst, load_s.at[i])
        for i, (src, dst) in enumerate(
            [(off_hbm, off_ref), (charge_hbm, charge_ref)]
            + [(uf_hbm, uf_ref), (u2_hbm, u2_ref), (dn_hbm, dn_ref)]
        )
    ]
    for load in loads:
        load.start()
    at_rxy = 96
    at_z2 = at_rxy + 128
    at_w = at_z2 + 56
    at_l3 = at_w + 24
    ix = lax.axis_index("gx")
    iy = lax.axis_index("gy")
    lane = lax.broadcasted_iota(jnp.int32, (8, 128), 1)
    lane64 = lax.broadcasted_iota(jnp.int32, (64, 128), 1)
    row64 = lax.broadcasted_iota(jnp.int32, (64, 128), 0)
    eye = row64 == lane64 % 64
    sub = lax.broadcasted_iota(jnp.int32, (8, 128), 0)
    c = cubic()
    t = nodes()

    def pick(index, values):
        result = jnp.full(index.shape, float(values[3]), F32)
        for e in (2, 1, 0):
            result = jnp.where(index == e, float(values[e]), result)
        return result

    for i, index in enumerate((sub % 4, sub // 4, 2 + sub // 4)):
        for e in range(4):
            flat[32 * i + 8 * e : 32 * i + 8 * e + 8] = pick(index, c[e])
    flat[at_rxy : at_rxy + 64] = 0.5 * pick(row64 // 16, t)
    flat[at_rxy + 64 : at_rxy + 128] = 0.5 * pick(row64 // 4 % 4, t)
    gap_z = 0.5 * (pick(lane % 4, t) - pick(sub % 4, t))
    for i in range(7):
        gap = gap_z + (i - 3.0)
        flat[at_z2 + 8 * i : at_z2 + 8 * i + 8] = gap * gap
    for level, start, length in ((0, 0, 64), (1, 64, 16), (2, 80, 16)):
        z = lane % 16
        seen = z + (sub - 3) * 2**level
        odd = (z // 2**level) % 2
        ok = (z % 2**level == 0) & (seen >= 0) & (seen < 16) & (sub < 7)
        ok = ok & (lane >= start) & (lane < start + length)
        ok = ok & ((sub < 6) | (odd == 0)) & ((sub > 0) | (odd == 1))
        flat[at_w + 8 * level : at_w + 8 * level + 8] = jnp.where(ok, 0.5**level, 0.0)
    lane_x = 0.5 * pick(lane % 64 // 16, t)
    lane_y = 0.5 * pick(lane // 4 % 4, t)
    flat[at_l3 : at_l3 + 8] = jnp.where(sub == 0, lane_x, lane_y)

    def remote(src, dst, send, recv, dx, dy):
        device = (lax.rem(ix + dx + count_x, count_x), lax.rem(iy + dy + count_y, count_y))
        return pltpu.make_async_remote_copy(
            src_ref=src, dst_ref=dst, send_sem=send, recv_sem=recv,
            device_id=device, device_id_type=MESH,
        )

    barrier = pltpu.get_barrier_semaphore()

    def greet(dx, dy):
        device = (lax.rem(ix + dx + count_x, count_x), lax.rem(iy + dy + count_y, count_y))
        pl.semaphore_signal(barrier, inc=1, device_id=device, device_id_type=MESH)

    for ox, oy in DIRS:
        greet(ox, oy)

    for k in range(1, count_y):
        greet(0, k)
    for k in range(1, count_x):
        greet(k, 0)

    def table_tile(j):
        dx = [(2 * j + e) // 7 - 3 for e in range(2)]
        dy = [(2 * j + e) % 7 - 3 for e in range(2)]
        dx, dy = (jnp.where(lane < 64, v[0], v[1]).astype(F32) for v in (dx, dy))
        gap_x = (dx + lane_x)[:1] - flat[at_rxy : at_rxy + 64]
        gap_y = (dy + lane_y)[:1] - flat[at_rxy + 64 : at_rxy + 128]
        adjacent = jnp.maximum(jnp.abs(dx), jnp.abs(dy))[:1]
        adjacent = jnp.broadcast_to(adjacent, (64, 128)) <= 1.0
        plane = gap_x * gap_x + gap_y * gap_y
        at = pl.ds(pl.multiple_of(j * 128, 128), 128)
        for i in range(7):
            value = lax.rsqrt(plane + jnp.concatenate([flat[at_z2 + 8 * i : at_z2 + 8 * i + 8]] * 8, 0))
            if i in (2, 3, 4):
                value = jnp.where(adjacent, 0.0, value)
            hi, lo = pair_split(value)
            table[64 * i : 64 * i + 64, at] = hi
            table[448 + 64 * i : 512 + 64 * i, at] = lo

    @pl.loop(0, count_x // 4)
    def _(j):
        apart = (j - ix // 4).astype(F32)
        side = (lane64 // 64 - iy // 4).astype(F32)
        gap_x = apart + flat[at_l3 : at_l3 + 1] - flat[at_rxy : at_rxy + 64]
        gap_y = side + flat[at_l3 + 1 : at_l3 + 2] - flat[at_rxy + 64 : at_rxy + 128]
        adjacent = jnp.maximum(jnp.abs(side), jnp.abs(apart)) <= 1.0
        plane = gap_x * gap_x + gap_y * gap_y
        at = pl.ds(pl.multiple_of(j * 128, 128), 128)
        for i in range(3):
            value = lax.rsqrt(plane + jnp.concatenate([flat[at_z2 + 8 * i + 16 : at_z2 + 8 * i + 24]] * 8, 0))
            value = jnp.where(adjacent, 0.0, value)
            hi, lo = pair_split(value)
            table3[64 * i : 64 * i + 64, at] = hi
            table3[192 + 64 * i : 256 + 64 * i, at] = lo

    pl.loop(0, 8)(table_tile)

    def basis(column, k):
        x = 2.0 * halo[column, 0, k : k + 1, :] - 1.0
        y = 2.0 * halo[column, 1, k : k + 1, :] - 1.0
        z = 2.0 * halo[column, 2, k : k + 1, :] - 1.0

        def poly(i, u):
            p = [flat[32 * i + 8 * e : 32 * i + 8 * e + 8] for e in range(4)]
            return ((p[3] * u + p[2]) * u + p[1]) * u + p[0]

        along_z = poly(0, z)
        low, high = poly(1, y) * along_z, poly(2, y) * along_z
        pieces = []
        for a in range(4):
            s = ((float(c[3, a]) * x + float(c[2, a])) * x + float(c[1, a])) * x + float(c[0, a])
            pieces += [s * low, s * high]
        return jnp.concatenate(pieces, 0)

    def column_of(cx, cy):
        return (1 + cx) * 4 + 1 + cy

    for load in loads[:2]:
        load.wait()
    for cx in range(2):
        for cy in range(2):
            for k in range(8):
                at = slice(128 * k, 128 * k + 128)
                for comp in range(3):
                    halo[column_of(cx, cy), comp, k : k + 1] = off_ref[comp, cx, cy : cy + 1, at]
                halo[column_of(cx, cy), 3, k : k + 1] = charge_ref[cx, cy : cy + 1, at]
    ROW, HALO, LEAF, LINE, SECOND, THIRD = range(6)
    buffers = (near_rows, halo, moments, rows, seconds, thirds)
    counts = (count_y - 1, 12, 8, len(ROWS) + 1, len(WIDER), count_x - 1)

    def send(kind, index, at, dx, dy):
        buffer = buffers[kind]
        sems = (send_s.at[kind], recv_s.at[kind])
        remote(buffer.at[index], buffer.at[at], *sems, dx, dy).start()

    def all_of(kind):
        part = buffers[kind].at[pl.ds(0, counts[kind])]
        return remote(part, part, send_s.at[kind], recv_s.at[kind], 1, 1)

    half_row = lax.broadcasted_iota(jnp.int32, (128, 128), 0) // 64
    half_lane = lax.broadcasted_iota(jnp.int32, (128, 128), 1)
    parity = (half_row == half_lane % 2).astype(F32).astype(BF16)
    halves = (half_row == half_lane // 64).astype(F32).astype(BF16)
    leaf[...] = jnp.zeros((64, 128), F32)

    @pl.loop(0, 4, unroll=True)
    def _(col):
        column = (1 + col // 2) * 4 + 1 + col % 2
        for k in range(8):
            value = basis(column, k)
            bases[8 * col + k] = value
            value = value * halo[column, 3, k : k + 1, :]
            hi, lo = pair_split(value)
            bq[col, 64 * k : 64 * k + 64] = hi
            bq[col, 512 + 64 * k : 576 + 64 * k] = lo
        summed = dot(bq[col], parity)
        total = leaf[...]
        for k in range(8):
            here = (lane64 % 64) // 2 == col * 8 + k
            total = jnp.where(
                here,
                summed[64 * k : 64 * k + 64] + summed[512 + 64 * k : 576 + 64 * k],
                total,
            )
        leaf[...] = total

    for load in loads[2:]:
        load.wait()
    own = leaf[...]
    moments[4] = jnp.where(lane64[:32] < 64, own[:32], own[32:])
    stacked = jnp.concatenate(
        [own] + [pltpu.roll(own, 128 - 16 * col, 1) for col in range(1, 4)], 0
    )
    first = folded(dot(uf_ref[...], wide(stacked)), 128)
    first = first[:64] + pltpu.roll(first[64:], 127, 1)
    first = jnp.where((lane64 < 16) & (lane64 % 2 == 0), first, 0.0)
    packet = first[:8]
    for g in range(1, 8):
        packet = packet + pltpu.roll(first[8 * g : 8 * g + 8], 16 * g, 1)
    near_rows[iy] = packet

    pl.semaphore_wait(barrier, len(DIRS) + count_y - 1 + count_x - 1)
    for k in range(1, count_y):
        send(ROW, iy, iy, 0, k)
    for ox, oy in DIRS:
        take_x = {1: [2], -1: [1], 0: [1, 2]}[ox]
        put_x = {1: [0], -1: [3], 0: [1, 2]}[ox]
        take_y = {1: (2, 1), -1: (1, 1), 0: (1, 2)}[oy]
        put_y = {1: 0, -1: 3, 0: 1}[oy]
        for a, b in zip(take_x, put_x):
            at = (pl.ds(a * 4 + take_y[0], take_y[1]), pl.ds(b * 4 + put_y, take_y[1]))
            send(HALO, *at, ox, oy)
    for ox, oy in DIRS:
        send(LEAF, 4, (1 - ox) * 3 + 1 - oy, ox, oy)

    pl.loop(8, TILES)(table_tile)

    first_term = (sub == 0) | (sub == 1) | (sub == 3)
    second_term = (sub == 2) | (sub == 4)
    half = (lane // 64).astype(F32)

    def three(value):
        a = value.astype(BF16).astype(F32)
        rest = value - a
        b = rest.astype(BF16).astype(F32)
        return [a, b, rest - b]

    def features(column, wx, wy, both):
        x = halo[column, 0] + (wx - 1.0)
        y = halo[column, 1] + (wy - 1.0)
        z = halo[column, 2] + (half - 1.0)
        plane = x * x + y * y
        parts = three(x) + three(y) + three(z) + three(plane + z * z)
        if both:
            beside = z + (2.0 - 4.0 * half)
            parts += three(beside) + three(plane + beside * beside)
        for i, part in enumerate(parts):
            pieces[column, i] = part

    def spread(column, i, k):
        return jnp.broadcast_to(pieces[column, i, k : k + 1], (8, 128))

    def chosen(column, i, k, six, seven, terms):
        a, b, c = (spread(column, i + e, k) for e in range(3))
        value = jnp.where(terms[0], a, jnp.where(terms[1], b, c))
        return jnp.where(sub == 6, six, jnp.where(sub == 7, seven, value))

    zero8 = jnp.zeros((8, 128), F32)
    one8 = jnp.ones((8, 128), F32)
    t_terms = ((sub == 0) | (sub == 2) | (sub == 5), (sub == 1) | (sub == 4))
    s_terms = (first_term, second_term)
    scale8 = jnp.where(sub < 6, -2.0, 1.0)

    @pl.loop(0, 4, unroll=True)
    def _(col):
        cx, cy = col // 2, col % 2
        column = (1 + cx) * 4 + 1 + cy
        features(column, cx.astype(F32), cy.astype(F32), False)
        for k in range(0, 8, 2):
            turned = []
            for e in (k, k + 1):
                tiles = [
                    chosen(column, 0, e, one8, one8, t_terms),
                    chosen(column, 3, e, one8, spread(column, 9, e), t_terms),
                    chosen(column, 6, e, spread(column, 10, e), spread(column, 11, e), t_terms),
                ]
                tiles = jnp.concatenate([t * scale8 for t in tiles] + [zero8], 0)
                turned.append((tiles, pltpu.roll(tiles, 64, 1)))
            lane32 = lane64[:32] < 64
            upper = jnp.where(lane32, turned[0][0], turned[1][1])
            lower = jnp.where(lane32, turned[0][1], turned[1][0])
            stack = jnp.concatenate([upper, lower], 0).T.astype(BF16)
            target[col * 8 + k] = stack[:64]
            target[col * 8 + k + 1] = stack[64:]

    all_of(ROW).wait_recv()
    packets = [near_rows[k] for k in range(count_y)]
    full = []
    for g in range(8):
        tile = jnp.zeros((8, 128), F32)
        for k in range(count_y):
            moved = pltpu.roll(packets[k], 16 * (k - g) % 128, 1) if k != g else packets[k]
            tile = jnp.where(lane // 16 == k, moved, tile)
        full.append(tile)
    full = jnp.concatenate(full, 0)
    rows[ix] = full[:32] + pltpu.roll(full[32:], 1, 1)

    def part(source, which, step_z, step_y):
        o = folded(dot(u2_ref[which], wide(source)), 256)
        return (
            o[:64]
            + pltpu.roll(o[64:128], 128 - step_z, 1)
            + pltpu.roll(o[128:192], 128 - step_y, 1)
            + pltpu.roll(o[192:], 128 - step_z - step_y, 1)
        )

    second = part(full, ix % 2, 2, 16)
    second = jnp.where((lane64 // 16 % 2 == 0) & (lane64 % 4 == 0), second, 0.0)
    third = part(second, ix // 2 % 2, 4, 32)
    third = jnp.where((lane64 // 16 % 4 == 0) & (lane64 % 8 == 0), third, 0.0)
    packed = second[:8]
    for g in range(1, 8):
        packed = packed + pltpu.roll(second[8 * g : 8 * g + 8], g % 4 + 16 * (g // 4), 1)
    seconds[ix] = packed
    packed = third[:8]
    for g in range(1, 8):
        packed = packed + pltpu.roll(third[8 * g : 8 * g + 8], g, 1)
    pair = packed[:2]
    for e in range(1, 4):
        pair = pair + pltpu.roll(packed[2 * e : 2 * e + 2], 16 * e, 1)
    thirds[ix] = pair

    for dx in WIDER:
        send(SECOND, ix, ix, dx, 0)
    send(LINE, ix, ix, 3 - 6 * (ix % 2), 0)
    for dx in ROWS:
        send(LINE, ix, ix, dx, 0)
    for k in sorted(range(1, count_x), key=hops, reverse=True):
        send(THIRD, ix, ix, k, 0)

    all_of(HALO).wait_recv()

    outside = jnp.where(lax.broadcasted_iota(jnp.int32, (32, 128), 0) == 6, 16384.0, 0.0)
    lane32 = lane64[:32] < 64
    left_half = lane32
    outside_low = jnp.where(left_half, outside, 0.0).astype(BF16)
    outside_high = jnp.where(left_half, 0.0, outside).astype(BF16)

    @pl.loop(0, 16, unroll=4)
    def _(column):
        wx, wy = column // 4, column % 4
        features(column, wx.astype(F32) - 1.0, wy.astype(F32) - 1.0, True)
        at_x, at_y = 2 * ix + wx - 1, 2 * iy + wy - 1
        inside = (at_x >= 0) & (at_x < 2 * count_x) & (at_y >= 0) & (at_y < 2 * count_y)
        q = halo[column, 3] * inside.astype(F32)
        after = jnp.where(sub == 7, 0.0, pltpu.roll(q, 7, 0))
        before = jnp.where(sub == 0, 0.0, pltpu.roll(q, 1, 0))
        charge[column, 0] = jnp.where(lane < 64, q, before)
        charge[column, 1] = q
        charge[column, 2] = jnp.where(lane < 64, after, q)
        source[column, 9, 2] = outside_low
        source[column, 0, 3] = outside_high
        for k in range(8):
            own_tiles = [
                chosen(column, 0, k, spread(column, 9, k), spread(column, 10, k), s_terms),
                chosen(column, 3, k, spread(column, 11, k), one8, s_terms),
                chosen(column, 6, k, one8, one8, s_terms),
                zero8,
            ]
            beside_tiles = [
                jnp.where(sub == 6, spread(column, 15, k), jnp.where(sub == 7, spread(column, 16, k), own_tiles[0])),
                jnp.where(sub == 6, spread(column, 17, k), own_tiles[1]),
                chosen(column, 12, k, one8, one8, s_terms),
                zero8,
            ]
            for e, tiles in enumerate((own_tiles, beside_tiles)):
                tiles = jnp.concatenate(tiles, 0)
                source[column, k + 1, 2 * e] = jnp.where(left_half, tiles, 0.0).astype(BF16)
                source[column, k + 1, 2 * e + 1] = jnp.where(left_half, 0.0, tiles).astype(BF16)

    def near_block(block, carry):
        col, k = block // 8, block % 8
        cx, cy = col // 2, col % 2
        mine = target[block]
        straight = jnp.zeros((64, 128), F32)
        crossed = jnp.zeros((64, 128), F32)
        columns = [(cx + dx) * 4 + cy + dy for dx in range(3) for dy in range(3)]

        def side(column, a, b):
            return jnp.concatenate([source[column, a[0], a[1]], source[column, b[0], b[1]]], 0)

        def row_of(column, dz):
            return charge[column, dz, pl.ds(k, 1), :]

        for column in columns:
            above = side(column, (k + 1, 1), (k + 2, 2))
            below = side(column, (k, 3), (k + 1, 0))
            inverse = lax.rsqrt(dot(mine, jnp.concatenate([above, below], 1)))
            crossed = crossed + inverse[:, :128] * row_of(column, 2)
            crossed = crossed + inverse[:, 128:] * row_of(column, 0)
        for i in range(0, 9, 2):
            group = columns[i : i + 2]
            both = [side(column, (k + 1, 0), (k + 1, 1)) for column in group]
            inverse = lax.rsqrt(dot(mine, jnp.concatenate(both, 1)))
            for e, column in enumerate(group):
                value = inverse[:, 128 * e : 128 * e + 128]
                if i + e == 4:
                    value = jnp.where(eye, 0.0, value)
                straight = straight + value * row_of(column, 1)
        sums[block] = straight + pltpu.roll(crossed, 64, 1)
        return carry

    lax.fori_loop(0, 32, near_block, 0, unroll=16)

    @pl.loop(0, 4, unroll=True)
    def _(col):
        value = sums[pl.ds(pl.multiple_of(col * 8, 8), 8)].reshape(512, 128)
        hi, lo = pair_split(value)
        value = dot(hi, halves) + dot(lo, halves)
        for k in range(8):
            mine = jnp.where(eye, value[64 * k : 64 * k + 64], 0.0)
            near[col, k : k + 1] = jnp.sum(mine, 0, keepdims=True)

    for kind in (LEAF, LINE, SECOND):
        all_of(kind).wait_recv()

    plain, crossed = {}, {}
    for ox in (-1, 0, 1):
        for oy in (-1, 0, 1):
            value = moments[(ox + 1) * 3 + oy + 1]
            turned = pltpu.roll(value, 64, 1)
            lane32 = lane64[:32]
            value = jnp.concatenate(
                [jnp.where(lane32 < 64, value, turned), jnp.where(lane32 < 64, turned, value)], 0
            )
            scale = F32(1.0)
            if ox:
                scale = scale * (ix > 0 if ox < 0 else ix < count_x - 1).astype(F32)
            if oy:
                scale = scale * (iy > 0 if oy < 0 else iy < count_y - 1).astype(F32)
            plain[ox, oy] = value * scale
    by_x = lane64 // 32 % 2
    by_y = lane64 // 16 % 2

    def swap_y(value):
        return jnp.where(by_y == 0, pltpu.roll(value, 112, 1), pltpu.roll(value, 16, 1))

    def leaf_block(dx, dy):
        result = None
        for cx in range(2):
            for cy in range(2):
                ox, oy = (cx + dx) // 2, (cy + dy) // 2
                if abs(ox) > 1 or abs(oy) > 1:
                    continue
                value = plain[ox, oy]
                if dy % 2:
                    value = swap_y(value)
                if dx % 2:
                    value = pltpu.roll(value, 32, 1)
                mine = (by_x == cx) & (by_y == cy)
                value = jnp.where(mine, value, 0.0)
                result = value if result is None else result + value
        return result

    def within(value, count, step, odd):
        ok = (value >= 0) & (value < count)
        if step == 3:
            ok = ok & (odd == 0)
        if step == -3:
            ok = ok & (odd == 1)
        return ok.astype(F32)

    for dx in range(-3, 4):
        step = {3: 3 * (1 - ix % 2), -3: -3 * (ix % 2)}.get(dx, dx)
        line = rows[lax.rem(ix + step + count_x, count_x)]
        line = jnp.concatenate([line, pltpu.roll(line, 127, 1)], 0)
        line = pltpu.roll(line, lax.rem(64 - 16 * iy + 128, 128), 1)
        line = line * within(ix + dx, count_x, dx, ix % 2)
        x2 = ix // 2 + dx
        base = lax.rem(2 * x2 + 2 * count_x, count_x)
        pair = seconds[base] + seconds[base + 1]
        pair = pltpu.roll(pair, lax.rem(80 - 32 * (iy // 2) + 128, 128), 1)
        pair = [pltpu.roll(pair, (-(g % 4) - 16 * (g // 4)) % 128, 1) if g else pair for g in range(8)]
        pair = jnp.concatenate(pair, 0)
        pair = pair * within(x2, count_x // 2, dx, ix // 2 % 2)
        for dy in range(-3, 4):
            one = pltpu.roll(line, (-16 * dy) % 128, 1) * within(iy + dy, count_y, dy, iy % 2)
            two = pltpu.roll(pair, (-32 * dy) % 128, 1)
            two = two * within(iy // 2 + dy, count_y // 2, dy, iy // 2 % 2)
            value = jnp.where(lane64 < 64, leaf_block(dx, dy), jnp.where(lane64 < 80, one, two))
            value = jnp.where(lane64 < 96, value, 0.0)
            at = ((dx + 3) * 7 + dy + 3) * 64
            right[at : at + 64] = wide(value)
    right[49 * 64 : 50 * 64] = jnp.zeros((64, 256), BF16)

    product[...] = dot(table[...], right[...])

    far = jnp.zeros((64, 128), F32)
    for i in range(7):
        dz = i - 3
        o = product[64 * i : 64 * i + 64]
        o2 = product[448 + 64 * i : 512 + 64 * i]
        o = o[:, :128] + o[:, 128:] + o2[:, :128] + o2[:, 128:]
        for level in range(3):
            value = o if dz == 0 else pltpu.roll(o, (-dz * 2**level) % 128, 1)
            far = far + value * flat[at_w + 8 * level + i : at_w + 8 * level + i + 1]

    all_of(THIRD).wait_recv()
    for j in range(count_x // 4):
        group = thirds[4 * j] + thirds[4 * j + 1] + thirds[4 * j + 2] + thirds[4 * j + 3]
        group = jnp.concatenate([group] + [pltpu.roll(group, 128 - 16 * e, 1) for e in range(1, 4)], 0)
        third = [group] + [pltpu.roll(group, 128 - g, 1) for g in range(1, 8)]
        third = jnp.concatenate(third, 0)
        right3[128 * j : 128 * j + 64] = wide(third)
        right3[128 * j + 64 : 128 * j + 128] = wide(pltpu.roll(third, 64, 1))
    o = folded(dot(table3[...], right3[...]), 192)
    local = o[64:128]
    local = local + jnp.where(lane64 == 0, pltpu.roll(o[128:], 120, 1), 0.0)
    local = local + jnp.where(lane64 == 8, pltpu.roll(o[:64], 8, 1), 0.0)
    local3 = jnp.where((lane64 < 16) & (lane64 % 8 == 0), 0.125 * local, 0.0)

    def down(source, which, step):
        o = folded(dot(dn_ref[which], wide(source)), 128)
        return jnp.where(lane64 % (2 * step) == 0, o[:64], pltpu.roll(o[64:], step, 1))

    low = lane64 < 16
    local2 = down(local3, ix // 2 % 2 * 2 + iy // 2 % 2, 4) + pltpu.roll(far, 48, 1)
    local2 = jnp.where(low & (lane64 % 4 == 0), local2, 0.0)
    local1 = down(local2, ix % 2 * 2 + iy % 2, 2) + pltpu.roll(far, 64, 1)
    local1 = jnp.where(low & (lane64 % 2 == 0), local1, 0.0)
    local0 = far
    for col in range(4):
        value = down(local1, col, 1)
        if col:
            value = pltpu.roll(value, 16 * col, 1)
        local0 = local0 + jnp.where(lane64 // 16 == col, value, 0.0)
    leaf[...] = local0

    @pl.loop(0, 4, unroll=True)
    def _(col):
        column = (1 + col // 2) * 4 + 1 + col % 2
        here = pltpu.roll(leaf[...], lax.rem(128 - 16 * col, 128), 1)
        for k in range(8):
            spread = jnp.where(
                lane64 < 64,
                jnp.broadcast_to(here[:, 2 * k : 2 * k + 1], (64, 128)),
                jnp.broadcast_to(here[:, 2 * k + 1 : 2 * k + 2], (64, 128)),
            )
            both = bases[8 * col + k] * spread
            near[col, k : k + 1] = jnp.sum(both, 0, keepdims=True) + near[col, k : k + 1]

    for col in range(4):
        for k in range(8):
            at = slice(128 * k, 128 * k + 128)
            out_ref[col // 2, col % 2 : col % 2 + 1, at] = near[col, k : k + 1]

    for kind in range(6):
        all_of(kind).wait_send()


def solution(mesh):
    count_x, count_y = mesh.shape["gx"], mesh.shape["gy"]
    fixed = constants()
    vmem = pl.BlockSpec(memory_space=pltpu.VMEM)
    hbm = pl.BlockSpec(memory_space=pltpu.HBM)
    dma = pltpu.SemaphoreType.DMA
    call = pl.pallas_call(
        functools.partial(kernel, count_x, count_y),
        out_shape=jax.ShapeDtypeStruct((2, 2, 1024), F32),
        in_specs=[hbm] * (2 + len(fixed)),
        out_specs=vmem,
        scratch_shapes=[
            pltpu.VMEM((3, 2, 2, 1024), F32),
            pltpu.VMEM((2, 2, 1024), F32),
            pltpu.VMEM((96 + 128 + 56 + 24 + 8, 128), F32),
            pltpu.VMEM(fixed[0].shape, BF16),
            pltpu.VMEM(fixed[1].shape, BF16),
            pltpu.VMEM(fixed[2].shape, BF16),
            pltpu.VMEM((16, 4, 8, 128), F32),
            pltpu.VMEM((9, 32, 128), F32),
            pltpu.VMEM((count_y, 8, 128), F32),
            pltpu.VMEM((count_x, 32, 128), F32),
            pltpu.VMEM((count_x, 8, 128), F32),
            pltpu.VMEM((count_x, 2, 128), F32),
            pltpu.VMEM((16, 18, 8, 128), F32),
            pltpu.VMEM((16, 10, 4, 32, 128), BF16),
            pltpu.VMEM((16, 3, 8, 128), F32),
            pltpu.VMEM((32, 64, 64), BF16),
            pltpu.VMEM((32, 64, 128), F32),
            pltpu.VMEM((4, 8, 128), F32),
            pltpu.VMEM((896, TILES * 128), BF16),
            pltpu.VMEM((384, count_x // 4 * 128), BF16),
            pltpu.VMEM((TILES * 128, 256), BF16),
            pltpu.VMEM((count_x // 4 * 128, 256), BF16),
            pltpu.VMEM((896, 256), F32),
            pltpu.VMEM((4, 1024, 128), BF16),
            pltpu.VMEM((64, 128), F32),
            pltpu.VMEM((32, 64, 128), F32),
            dma((5,)),
            dma((6,)),
            dma((6,)),
        ],
        compiler_params=pltpu.CompilerParams(
            collective_id=0, has_side_effects=True, vmem_limit_bytes=64 << 20
        ),
    )

    def body(offsets, charges):
        return call(offsets, charges, *fixed)

    in_specs = (P(None, "gx", "gy", None), P("gx", "gy", None))
    out_specs = P("gx", "gy", None)
    return jax.shard_map(body, mesh=mesh, in_specs=in_specs, out_specs=out_specs, check_vma=False)
```

```python
import functools

import jax
import jax.numpy as jnp
import ml_dtypes
import numpy as np
from jax import lax
from jax.experimental import pallas as pl
from jax.experimental.pallas import tpu as pltpu
from jax.sharding import PartitionSpec as P

MESH = pl.DeviceIdType.MESH
F32 = jnp.float32
BF16 = jnp.bfloat16
DIRS = [(ox, oy) for ox in (-1, 0, 1) for oy in (-1, 0, 1) if (ox, oy) != (0, 0)]
ROWS = (2, -2, 1, -1)
WIDER = (4, -4, 3, -3, 5, -5, 2, -2, 6, -6, 1, -1, 7, -7)
TILES = 25


def hops(k):
    return min(k % 8, 8 - k % 8) + min(k // 8, 4 - k // 8)


def nodes():
    return np.cos((2.0 * np.arange(4) + 1.0) * np.pi / 8.0)


def cubic():
    t = nodes()
    t2, t3 = 2 * t * t - 1, 4 * t**3 - 3 * t
    return np.stack([0.25 - 0.5 * t2, 0.5 * t - 1.5 * t3, t2, 2 * t3])


def split(x):
    hi = x.astype(ml_dtypes.bfloat16)
    lo = (x - hi.astype(np.float64)).astype(ml_dtypes.bfloat16)
    return hi, lo


def constants():
    t = nodes()
    c = cubic()
    shifted = (t[None, :] + 2.0 * np.arange(2)[:, None] - 1.0) / 2.0
    f = sum(c[k][None, None, :] * shifted[:, :, None] ** k for k in range(4))
    up = np.einsum("xia,yjb,zkc->xyzijkabc", f, f, f).reshape(2, 2, 2, 64, 64)
    uf = up.transpose(2, 4, 0, 1, 3).reshape(128, 256)
    uf = np.concatenate(split(uf), 0)
    u2 = up.transpose(0, 1, 2, 4, 3).reshape(2, 256, 64)
    u2 = np.concatenate(split(u2), 1)
    return [uf, u2]


def pair_split(x):
    hi = x.astype(BF16)
    lo = (x - hi.astype(F32)).astype(BF16)
    return hi, lo


def wide(x):
    return jnp.concatenate(pair_split(x), 1)


def folded(product, rows):
    return product[:rows, :128] + product[:rows, 128:] + product[rows:, :128] + product[rows:, 128:]


def dot(left, right):
    return jnp.dot(left, right, preferred_element_type=F32)


def kernel(
    count_x, count_y,
    off_hbm, charge_hbm, uf_hbm, u2_hbm,
    out_ref,
    off_ref, charge_ref, flat, uf_ref, u2_ref,
    halo, moments, near_rows, rows, seconds, thirds, pieces, source, charge, target, sums, near,
    table, table3, right, right3, product, bq, leaf, bases,
    load_s, send_s, recv_s,
):
    loads = [
        pltpu.make_async_copy(src, dst, load_s.at[i])
        for i, (src, dst) in enumerate(
            [(off_hbm, off_ref), (charge_hbm, charge_ref)]
            + [(uf_hbm, uf_ref), (u2_hbm, u2_ref)]
        )
    ]
    for load in loads:
        load.start()
    at_rxy = 96
    at_z2 = at_rxy + 128
    at_w = at_z2 + 56
    at_l3 = at_w + 24
    ix = lax.axis_index("gx")
    iy = lax.axis_index("gy")
    lane = lax.broadcasted_iota(jnp.int32, (8, 128), 1)
    lane64 = lax.broadcasted_iota(jnp.int32, (64, 128), 1)
    row64 = lax.broadcasted_iota(jnp.int32, (64, 128), 0)
    eye = row64 == lane64 % 64
    sub = lax.broadcasted_iota(jnp.int32, (8, 128), 0)
    c = cubic()
    t = nodes()

    def pick(index, values):
        result = jnp.full(index.shape, float(values[3]), F32)
        for e in (2, 1, 0):
            result = jnp.where(index == e, float(values[e]), result)
        return result

    for i, index in enumerate((sub % 4, sub // 4, 2 + sub // 4)):
        for e in range(4):
            flat[32 * i + 8 * e : 32 * i + 8 * e + 8] = pick(index, c[e])
    flat[at_rxy : at_rxy + 64] = 0.5 * pick(row64 // 16, t)
    flat[at_rxy + 64 : at_rxy + 128] = 0.5 * pick(row64 // 4 % 4, t)
    gap_z = 0.5 * (pick(lane % 4, t) - pick(sub % 4, t))
    for i in range(7):
        gap = gap_z + (i - 3.0)
        flat[at_z2 + 8 * i : at_z2 + 8 * i + 8] = gap * gap
    for level, start, length in ((0, 0, 64), (1, 64, 16), (2, 80, 16)):
        z = lane % 16
        seen = z + (sub - 3) * 2**level
        odd = (z // 2**level) % 2
        ok = (z % 2**level == 0) & (seen >= 0) & (seen < 16) & (sub < 7)
        ok = ok & (lane >= start) & (lane < start + length)
        ok = ok & ((sub < 6) | (odd == 0)) & ((sub > 0) | (odd == 1))
        flat[at_w + 8 * level : at_w + 8 * level + 8] = jnp.where(ok, 0.5**level, 0.0)
    lane_x = 0.5 * pick(lane % 64 // 16, t)
    lane_y = 0.5 * pick(lane // 4 % 4, t)
    flat[at_l3 : at_l3 + 8] = jnp.where(sub == 0, lane_x, lane_y)

    def remote(src, dst, send, recv, dx, dy):
        device = (lax.rem(ix + dx + count_x, count_x), lax.rem(iy + dy + count_y, count_y))
        return pltpu.make_async_remote_copy(
            src_ref=src, dst_ref=dst, send_sem=send, recv_sem=recv,
            device_id=device, device_id_type=MESH,
        )

    barrier = pltpu.get_barrier_semaphore()

    def greet(dx, dy):
        device = (lax.rem(ix + dx + count_x, count_x), lax.rem(iy + dy + count_y, count_y))
        pl.semaphore_signal(barrier, inc=1, device_id=device, device_id_type=MESH)

    for ox, oy in DIRS:
        greet(ox, oy)

    for k in range(1, count_y):
        greet(0, k)
    for k in range(1, count_x):
        greet(k, 0)

    def table_tile(j):
        dx = [(2 * j + e) // 7 - 3 for e in range(2)]
        dy = [(2 * j + e) % 7 - 3 for e in range(2)]
        dx, dy = (jnp.where(lane < 64, v[0], v[1]).astype(F32) for v in (dx, dy))
        gap_x = (dx + lane_x)[:1] - flat[at_rxy : at_rxy + 64]
        gap_y = (dy + lane_y)[:1] - flat[at_rxy + 64 : at_rxy + 128]
        adjacent = jnp.maximum(jnp.abs(dx), jnp.abs(dy))[:1]
        adjacent = jnp.broadcast_to(adjacent, (64, 128)) <= 1.0
        plane = gap_x * gap_x + gap_y * gap_y
        at = pl.ds(pl.multiple_of(j * 128, 128), 128)
        for i in range(7):
            value = lax.rsqrt(plane + jnp.concatenate([flat[at_z2 + 8 * i : at_z2 + 8 * i + 8]] * 8, 0))
            if i in (2, 3, 4):
                value = jnp.where(adjacent, 0.0, value)
            hi, lo = pair_split(value)
            table[64 * i : 64 * i + 64, at] = hi
            table[448 + 64 * i : 512 + 64 * i, at] = lo

    @pl.loop(0, count_x // 4)
    def _(j):
        apart = (j - ix // 4).astype(F32)
        side = (lane64 // 64 - iy // 4).astype(F32)
        gap_x = apart + flat[at_l3 : at_l3 + 1] - flat[at_rxy : at_rxy + 64]
        gap_y = side + flat[at_l3 + 1 : at_l3 + 2] - flat[at_rxy + 64 : at_rxy + 128]
        adjacent = jnp.maximum(jnp.abs(side), jnp.abs(apart)) <= 1.0
        plane = gap_x * gap_x + gap_y * gap_y
        at = pl.ds(pl.multiple_of(j * 128, 128), 128)
        for i in range(3):
            value = lax.rsqrt(plane + jnp.concatenate([flat[at_z2 + 8 * i + 16 : at_z2 + 8 * i + 24]] * 8, 0))
            value = jnp.where(adjacent, 0.0, value)
            hi, lo = pair_split(value)
            table3[64 * i : 64 * i + 64, at] = hi
            table3[192 + 64 * i : 256 + 64 * i, at] = lo

    pl.loop(0, 8)(table_tile)

    def basis(column, k, level=0, col=None):
        places = [halo[column, comp, k : k + 1, :] for comp in range(3)]
        if level:
            size = 2**level
            corner = (
                ((2 * ix + col // 2) % size).astype(F32),
                ((2 * iy + col % 2) % size).astype(F32),
                (2 * k) % size + (lane[:1] // 64).astype(F32),
            )
            places = [(place + at) * (1.0 / size) for place, at in zip(places, corner)]
        x, y, z = (2.0 * place - 1.0 for place in places)

        def poly(i, u):
            p = [flat[32 * i + 8 * e : 32 * i + 8 * e + 8] for e in range(4)]
            return ((p[3] * u + p[2]) * u + p[1]) * u + p[0]

        along_z = poly(0, z)
        low, high = poly(1, y) * along_z, poly(2, y) * along_z
        pieces = []
        for a in range(4):
            s = ((float(c[3, a]) * x + float(c[2, a])) * x + float(c[1, a])) * x + float(c[0, a])
            pieces += [s * low, s * high]
        return jnp.concatenate(pieces, 0)

    def column_of(cx, cy):
        return (1 + cx) * 4 + 1 + cy

    for load in loads[:2]:
        load.wait()
    for cx in range(2):
        for cy in range(2):
            for k in range(8):
                at = slice(128 * k, 128 * k + 128)
                for comp in range(3):
                    halo[column_of(cx, cy), comp, k : k + 1] = off_ref[comp, cx, cy : cy + 1, at]
                halo[column_of(cx, cy), 3, k : k + 1] = charge_ref[cx, cy : cy + 1, at]
    ROW, HALO, LEAF, LINE, SECOND, THIRD = range(6)
    buffers = (near_rows, halo, moments, rows, seconds, thirds)
    counts = (count_y - 1, 12, 8, len(ROWS) + 1, len(WIDER), count_x - 1)

    def send(kind, index, at, dx, dy):
        buffer = buffers[kind]
        sems = (send_s.at[kind], recv_s.at[kind])
        remote(buffer.at[index], buffer.at[at], *sems, dx, dy).start()

    def all_of(kind):
        part = buffers[kind].at[pl.ds(0, counts[kind])]
        return remote(part, part, send_s.at[kind], recv_s.at[kind], 1, 1)

    half_row = lax.broadcasted_iota(jnp.int32, (128, 128), 0) // 64
    half_lane = lax.broadcasted_iota(jnp.int32, (128, 128), 1)
    parity = (half_row == half_lane % 2).astype(F32).astype(BF16)
    halves = (half_row == half_lane // 64).astype(F32).astype(BF16)
    leaf[...] = jnp.zeros((64, 128), F32)

    @pl.loop(0, 4, unroll=True)
    def _(col):
        column = (1 + col // 2) * 4 + 1 + col % 2
        for k in range(8):
            value = basis(column, k)
            bases[0, 8 * col + k] = value
            value = value * halo[column, 3, k : k + 1, :]
            hi, lo = pair_split(value)
            bq[col, 64 * k : 64 * k + 64] = hi
            bq[col, 512 + 64 * k : 576 + 64 * k] = lo
        summed = dot(bq[col], parity)
        total = leaf[...]
        for k in range(8):
            here = (lane64 % 64) // 2 == col * 8 + k
            total = jnp.where(
                here,
                summed[64 * k : 64 * k + 64] + summed[512 + 64 * k : 576 + 64 * k],
                total,
            )
        leaf[...] = total

    for load in loads[2:]:
        load.wait()
    own = leaf[...]
    moments[4] = jnp.where(lane64[:32] < 64, own[:32], own[32:])
    stacked = jnp.concatenate(
        [own] + [pltpu.roll(own, 128 - 16 * col, 1) for col in range(1, 4)], 0
    )
    first = folded(dot(uf_ref[...], wide(stacked)), 128)
    first = first[:64] + pltpu.roll(first[64:], 127, 1)
    first = jnp.where((lane64 < 16) & (lane64 % 2 == 0), first, 0.0)
    packet = first[:8]
    for g in range(1, 8):
        packet = packet + pltpu.roll(first[8 * g : 8 * g + 8], 16 * g, 1)
    near_rows[iy] = packet

    pl.semaphore_wait(barrier, len(DIRS) + count_y - 1 + count_x - 1)
    for k in range(1, count_y):
        send(ROW, iy, iy, 0, k)
    for ox, oy in DIRS:
        take_x = {1: [2], -1: [1], 0: [1, 2]}[ox]
        put_x = {1: [0], -1: [3], 0: [1, 2]}[ox]
        take_y = {1: (2, 1), -1: (1, 1), 0: (1, 2)}[oy]
        put_y = {1: 0, -1: 3, 0: 1}[oy]
        for a, b in zip(take_x, put_x):
            at = (pl.ds(a * 4 + take_y[0], take_y[1]), pl.ds(b * 4 + put_y, take_y[1]))
            send(HALO, *at, ox, oy)
    for ox, oy in DIRS:
        send(LEAF, 4, (1 - ox) * 3 + 1 - oy, ox, oy)

    pl.loop(8, TILES)(table_tile)

    @pl.loop(0, 4, unroll=True)
    def _(col):
        column = (1 + col // 2) * 4 + 1 + col % 2
        for level in range(1, 4):
            for k in range(8):
                bases[level, 8 * col + k] = basis(column, k, level, col)

    first_term = (sub == 0) | (sub == 1) | (sub == 3)
    second_term = (sub == 2) | (sub == 4)
    half = (lane // 64).astype(F32)

    def three(value):
        a = value.astype(BF16).astype(F32)
        rest = value - a
        b = rest.astype(BF16).astype(F32)
        return [a, b, rest - b]

    def features(column, wx, wy, both):
        x = halo[column, 0] + (wx - 1.0)
        y = halo[column, 1] + (wy - 1.0)
        z = halo[column, 2] + (half - 1.0)
        plane = x * x + y * y
        parts = three(x) + three(y) + three(z) + three(plane + z * z)
        if both:
            beside = z + (2.0 - 4.0 * half)
            parts += three(beside) + three(plane + beside * beside)
        for i, part in enumerate(parts):
            pieces[column, i] = part

    def spread(column, i, k):
        return jnp.broadcast_to(pieces[column, i, k : k + 1], (8, 128))

    def chosen(column, i, k, six, seven, terms):
        a, b, c = (spread(column, i + e, k) for e in range(3))
        value = jnp.where(terms[0], a, jnp.where(terms[1], b, c))
        return jnp.where(sub == 6, six, jnp.where(sub == 7, seven, value))

    zero8 = jnp.zeros((8, 128), F32)
    one8 = jnp.ones((8, 128), F32)
    t_terms = ((sub == 0) | (sub == 2) | (sub == 5), (sub == 1) | (sub == 4))
    s_terms = (first_term, second_term)
    scale8 = jnp.where(sub < 6, -2.0, 1.0)

    @pl.loop(0, 4, unroll=True)
    def _(col):
        cx, cy = col // 2, col % 2
        column = (1 + cx) * 4 + 1 + cy
        features(column, cx.astype(F32), cy.astype(F32), False)
        for k in range(0, 8, 2):
            turned = []
            for e in (k, k + 1):
                tiles = [
                    chosen(column, 0, e, one8, one8, t_terms),
                    chosen(column, 3, e, one8, spread(column, 9, e), t_terms),
                    chosen(column, 6, e, spread(column, 10, e), spread(column, 11, e), t_terms),
                ]
                tiles = jnp.concatenate([t * scale8 for t in tiles] + [zero8], 0)
                turned.append((tiles, pltpu.roll(tiles, 64, 1)))
            lane32 = lane64[:32] < 64
            upper = jnp.where(lane32, turned[0][0], turned[1][1])
            lower = jnp.where(lane32, turned[0][1], turned[1][0])
            stack = jnp.concatenate([upper, lower], 0).T.astype(BF16)
            target[col * 8 + k] = stack[:64]
            target[col * 8 + k + 1] = stack[64:]

    all_of(ROW).wait_recv()
    packets = [near_rows[k] for k in range(count_y)]
    full = []
    for g in range(8):
        tile = jnp.zeros((8, 128), F32)
        for k in range(count_y):
            moved = pltpu.roll(packets[k], 16 * (k - g) % 128, 1) if k != g else packets[k]
            tile = jnp.where(lane // 16 == k, moved, tile)
        full.append(tile)
    full = jnp.concatenate(full, 0)
    rows[ix] = full[:32] + pltpu.roll(full[32:], 1, 1)

    def part(source, which, step_z, step_y):
        o = folded(dot(u2_ref[which], wide(source)), 256)
        return (
            o[:64]
            + pltpu.roll(o[64:128], 128 - step_z, 1)
            + pltpu.roll(o[128:192], 128 - step_y, 1)
            + pltpu.roll(o[192:], 128 - step_z - step_y, 1)
        )

    second = part(full, ix % 2, 2, 16)
    second = jnp.where((lane64 // 16 % 2 == 0) & (lane64 % 4 == 0), second, 0.0)
    third = part(second, ix // 2 % 2, 4, 32)
    third = jnp.where((lane64 // 16 % 4 == 0) & (lane64 % 8 == 0), third, 0.0)
    packed = second[:8]
    for g in range(1, 8):
        packed = packed + pltpu.roll(second[8 * g : 8 * g + 8], g % 4 + 16 * (g // 4), 1)
    seconds[ix] = packed
    packed = third[:8]
    for g in range(1, 8):
        packed = packed + pltpu.roll(third[8 * g : 8 * g + 8], g, 1)
    pair = packed[:2]
    for e in range(1, 4):
        pair = pair + pltpu.roll(packed[2 * e : 2 * e + 2], 16 * e, 1)
    thirds[ix] = pair

    for dx in WIDER:
        send(SECOND, ix, ix, dx, 0)
    send(LINE, ix, ix, 3 - 6 * (ix % 2), 0)
    for dx in ROWS:
        send(LINE, ix, ix, dx, 0)
    for k in sorted(range(1, count_x), key=hops, reverse=True):
        send(THIRD, ix, ix, k, 0)

    all_of(HALO).wait_recv()

    outside = jnp.where(lax.broadcasted_iota(jnp.int32, (32, 128), 0) == 6, 16384.0, 0.0)
    lane32 = lane64[:32] < 64
    left_half = lane32
    outside_low = jnp.where(left_half, outside, 0.0).astype(BF16)
    outside_high = jnp.where(left_half, 0.0, outside).astype(BF16)

    @pl.loop(0, 16, unroll=4)
    def _(column):
        wx, wy = column // 4, column % 4
        features(column, wx.astype(F32) - 1.0, wy.astype(F32) - 1.0, True)
        at_x, at_y = 2 * ix + wx - 1, 2 * iy + wy - 1
        inside = (at_x >= 0) & (at_x < 2 * count_x) & (at_y >= 0) & (at_y < 2 * count_y)
        q = halo[column, 3] * inside.astype(F32)
        after = jnp.where(sub == 7, 0.0, pltpu.roll(q, 7, 0))
        before = jnp.where(sub == 0, 0.0, pltpu.roll(q, 1, 0))
        charge[column, 0] = jnp.where(lane < 64, q, before)
        charge[column, 1] = q
        charge[column, 2] = jnp.where(lane < 64, after, q)
        source[column, 9, 2] = outside_low
        source[column, 0, 3] = outside_high
        for k in range(8):
            own_tiles = [
                chosen(column, 0, k, spread(column, 9, k), spread(column, 10, k), s_terms),
                chosen(column, 3, k, spread(column, 11, k), one8, s_terms),
                chosen(column, 6, k, one8, one8, s_terms),
                zero8,
            ]
            beside_tiles = [
                jnp.where(sub == 6, spread(column, 15, k), jnp.where(sub == 7, spread(column, 16, k), own_tiles[0])),
                jnp.where(sub == 6, spread(column, 17, k), own_tiles[1]),
                chosen(column, 12, k, one8, one8, s_terms),
                zero8,
            ]
            for e, tiles in enumerate((own_tiles, beside_tiles)):
                tiles = jnp.concatenate(tiles, 0)
                source[column, k + 1, 2 * e] = jnp.where(left_half, tiles, 0.0).astype(BF16)
                source[column, k + 1, 2 * e + 1] = jnp.where(left_half, 0.0, tiles).astype(BF16)

    def near_block(block, carry):
        col, k = block // 8, block % 8
        cx, cy = col // 2, col % 2
        mine = target[block]
        straight = jnp.zeros((64, 128), F32)
        crossed = jnp.zeros((64, 128), F32)
        columns = [(cx + dx) * 4 + cy + dy for dx in range(3) for dy in range(3)]

        def side(column, a, b):
            return jnp.concatenate([source[column, a[0], a[1]], source[column, b[0], b[1]]], 0)

        def row_of(column, dz):
            return charge[column, dz, pl.ds(k, 1), :]

        for column in columns:
            above = side(column, (k + 1, 1), (k + 2, 2))
            below = side(column, (k, 3), (k + 1, 0))
            inverse = lax.rsqrt(dot(mine, jnp.concatenate([above, below], 1)))
            crossed = crossed + inverse[:, :128] * row_of(column, 2)
            crossed = crossed + inverse[:, 128:] * row_of(column, 0)
        for i in range(0, 9, 2):
            group = columns[i : i + 2]
            both = [side(column, (k + 1, 0), (k + 1, 1)) for column in group]
            inverse = lax.rsqrt(dot(mine, jnp.concatenate(both, 1)))
            for e, column in enumerate(group):
                value = inverse[:, 128 * e : 128 * e + 128]
                if i + e == 4:
                    value = jnp.where(eye, 0.0, value)
                straight = straight + value * row_of(column, 1)
        sums[block] = straight + pltpu.roll(crossed, 64, 1)
        return carry

    lax.fori_loop(0, 32, near_block, 0, unroll=16)

    @pl.loop(0, 4, unroll=True)
    def _(col):
        value = sums[pl.ds(pl.multiple_of(col * 8, 8), 8)].reshape(512, 128)
        hi, lo = pair_split(value)
        value = dot(hi, halves) + dot(lo, halves)
        for k in range(8):
            mine = jnp.where(eye, value[64 * k : 64 * k + 64], 0.0)
            near[col, k : k + 1] = jnp.sum(mine, 0, keepdims=True)

    for kind in (LEAF, LINE, SECOND):
        all_of(kind).wait_recv()

    plain, crossed = {}, {}
    for ox in (-1, 0, 1):
        for oy in (-1, 0, 1):
            value = moments[(ox + 1) * 3 + oy + 1]
            turned = pltpu.roll(value, 64, 1)
            lane32 = lane64[:32]
            value = jnp.concatenate(
                [jnp.where(lane32 < 64, value, turned), jnp.where(lane32 < 64, turned, value)], 0
            )
            scale = F32(1.0)
            if ox:
                scale = scale * (ix > 0 if ox < 0 else ix < count_x - 1).astype(F32)
            if oy:
                scale = scale * (iy > 0 if oy < 0 else iy < count_y - 1).astype(F32)
            plain[ox, oy] = value * scale
    by_x = lane64 // 32 % 2
    by_y = lane64 // 16 % 2

    def swap_y(value):
        return jnp.where(by_y == 0, pltpu.roll(value, 112, 1), pltpu.roll(value, 16, 1))

    def leaf_block(dx, dy):
        result = None
        for cx in range(2):
            for cy in range(2):
                ox, oy = (cx + dx) // 2, (cy + dy) // 2
                if abs(ox) > 1 or abs(oy) > 1:
                    continue
                value = plain[ox, oy]
                if dy % 2:
                    value = swap_y(value)
                if dx % 2:
                    value = pltpu.roll(value, 32, 1)
                mine = (by_x == cx) & (by_y == cy)
                value = jnp.where(mine, value, 0.0)
                result = value if result is None else result + value
        return result

    def within(value, count, step, odd):
        ok = (value >= 0) & (value < count)
        if step == 3:
            ok = ok & (odd == 0)
        if step == -3:
            ok = ok & (odd == 1)
        return ok.astype(F32)

    for dx in range(-3, 4):
        step = {3: 3 * (1 - ix % 2), -3: -3 * (ix % 2)}.get(dx, dx)
        line = rows[lax.rem(ix + step + count_x, count_x)]
        line = jnp.concatenate([line, pltpu.roll(line, 127, 1)], 0)
        line = pltpu.roll(line, lax.rem(64 - 16 * iy + 128, 128), 1)
        line = line * within(ix + dx, count_x, dx, ix % 2)
        x2 = ix // 2 + dx
        base = lax.rem(2 * x2 + 2 * count_x, count_x)
        pair = seconds[base] + seconds[base + 1]
        pair = pltpu.roll(pair, lax.rem(80 - 32 * (iy // 2) + 128, 128), 1)
        pair = [pltpu.roll(pair, (-(g % 4) - 16 * (g // 4)) % 128, 1) if g else pair for g in range(8)]
        pair = jnp.concatenate(pair, 0)
        pair = pair * within(x2, count_x // 2, dx, ix // 2 % 2)
        for dy in range(-3, 4):
            one = pltpu.roll(line, (-16 * dy) % 128, 1) * within(iy + dy, count_y, dy, iy % 2)
            two = pltpu.roll(pair, (-32 * dy) % 128, 1)
            two = two * within(iy // 2 + dy, count_y // 2, dy, iy // 2 % 2)
            value = jnp.where(lane64 < 64, leaf_block(dx, dy), jnp.where(lane64 < 80, one, two))
            value = jnp.where(lane64 < 96, value, 0.0)
            at = ((dx + 3) * 7 + dy + 3) * 64
            right[at : at + 64] = wide(value)
    right[49 * 64 : 50 * 64] = jnp.zeros((64, 256), BF16)

    product[...] = dot(table[...], right[...])

    far = jnp.zeros((64, 128), F32)
    for i in range(7):
        dz = i - 3
        o = product[64 * i : 64 * i + 64]
        o2 = product[448 + 64 * i : 512 + 64 * i]
        o = o[:, :128] + o[:, 128:] + o2[:, :128] + o2[:, 128:]
        for level in range(3):
            value = o if dz == 0 else pltpu.roll(o, (-dz * 2**level) % 128, 1)
            far = far + value * flat[at_w + 8 * level + i : at_w + 8 * level + i + 1]

    all_of(THIRD).wait_recv()
    for j in range(count_x // 4):
        group = thirds[4 * j] + thirds[4 * j + 1] + thirds[4 * j + 2] + thirds[4 * j + 3]
        group = jnp.concatenate([group] + [pltpu.roll(group, 128 - 16 * e, 1) for e in range(1, 4)], 0)
        third = [group] + [pltpu.roll(group, 128 - g, 1) for g in range(1, 8)]
        third = jnp.concatenate(third, 0)
        right3[128 * j : 128 * j + 64] = wide(third)
        right3[128 * j + 64 : 128 * j + 128] = wide(pltpu.roll(third, 64, 1))
    o = folded(dot(table3[...], right3[...]), 192)
    local = o[64:128]
    local = local + jnp.where(lane64 == 0, pltpu.roll(o[128:], 120, 1), 0.0)
    local = local + jnp.where(lane64 == 8, pltpu.roll(o[:64], 8, 1), 0.0)
    local3 = jnp.where((lane64 < 16) & (lane64 % 8 == 0), 0.125 * local, 0.0)

    def column(value, at):
        return jnp.broadcast_to(value[:, at : at + 1], (64, 128))

    for k in range(8):
        if k % 4 == 0:
            high3 = column(local3, 2 * k)
        if k % 2 == 0:
            high2 = column(far, 80 + 2 * k)
        high1 = column(far, 64 + 2 * k)
        for col in range(4):
            block = 8 * col + k
            here = 16 * col + 2 * k
            high0 = jnp.where(lane64 < 64, column(far, here), column(far, here + 1))
            both = bases[0, block] * high0 + bases[1, block] * high1
            both = both + bases[2, block] * high2 + bases[3, block] * high3
            both = jnp.sum(both, 0, keepdims=True) + near[col, k : k + 1]
            out_ref[col // 2, col % 2 : col % 2 + 1, 128 * k : 128 * k + 128] = both

    for kind in range(6):
        all_of(kind).wait_send()


def solution(mesh):
    count_x, count_y = mesh.shape["gx"], mesh.shape["gy"]
    fixed = constants()
    vmem = pl.BlockSpec(memory_space=pltpu.VMEM)
    hbm = pl.BlockSpec(memory_space=pltpu.HBM)
    dma = pltpu.SemaphoreType.DMA
    call = pl.pallas_call(
        functools.partial(kernel, count_x, count_y),
        out_shape=jax.ShapeDtypeStruct((2, 2, 1024), F32),
        in_specs=[hbm] * (2 + len(fixed)),
        out_specs=vmem,
        scratch_shapes=[
            pltpu.VMEM((3, 2, 2, 1024), F32),
            pltpu.VMEM((2, 2, 1024), F32),
            pltpu.VMEM((96 + 128 + 56 + 24 + 8, 128), F32),
            pltpu.VMEM(fixed[0].shape, BF16),
            pltpu.VMEM(fixed[1].shape, BF16),
            pltpu.VMEM((16, 4, 8, 128), F32),
            pltpu.VMEM((9, 32, 128), F32),
            pltpu.VMEM((count_y, 8, 128), F32),
            pltpu.VMEM((count_x, 32, 128), F32),
            pltpu.VMEM((count_x, 8, 128), F32),
            pltpu.VMEM((count_x, 2, 128), F32),
            pltpu.VMEM((16, 18, 8, 128), F32),
            pltpu.VMEM((16, 10, 4, 32, 128), BF16),
            pltpu.VMEM((16, 3, 8, 128), F32),
            pltpu.VMEM((32, 64, 64), BF16),
            pltpu.VMEM((32, 64, 128), F32),
            pltpu.VMEM((4, 8, 128), F32),
            pltpu.VMEM((896, TILES * 128), BF16),
            pltpu.VMEM((384, count_x // 4 * 128), BF16),
            pltpu.VMEM((TILES * 128, 256), BF16),
            pltpu.VMEM((count_x // 4 * 128, 256), BF16),
            pltpu.VMEM((896, 256), F32),
            pltpu.VMEM((4, 1024, 128), BF16),
            pltpu.VMEM((64, 128), F32),
            pltpu.VMEM((4, 32, 64, 128), F32),
            dma((4,)),
            dma((6,)),
            dma((6,)),
        ],
        compiler_params=pltpu.CompilerParams(
            collective_id=0, has_side_effects=True, vmem_limit_bytes=64 << 20
        ),
    )

    def body(offsets, charges):
        return call(offsets, charges, *fixed)

    in_specs = (P(None, "gx", "gy", None), P("gx", "gy", None))
    out_specs = P("gx", "gy", None)
    return jax.shard_map(body, mesh=mesh, in_specs=in_specs, out_specs=out_specs, check_vma=False)
```
